512 devices in a mesh: seq: 64 (over z, x), head: 8 (over y, core).
Axes of the slice: x: 4, y: 4, z: 16, core: 2. Of those that a mesh axis runs over, the one named last changes fastest.
Arguments:
- x_in: bfloat16 [16384, 2048], P('seq', 'head'), may hold values from -45 to 45
- gate_in: bfloat16 [16384, 2048], P('seq', 'head'), may hold values from -6 to 6
- b_in: bfloat16 [16384, 128], P('seq'), may hold values from -0.375 to 0.375
- c_in: bfloat16 [16384, 128], P('seq'), may hold values from -0.375 to 0.375
- decay_fwd: float32 [32, 16384], P('head', 'seq'), may hold values from -1 to 0
- decay_bwd: float32 [32, 16384], P('head', 'seq'), may hold values from -1 to 0
- skip_gain: float32 [32], P('head'), may hold values from 0.5 to 1.5
- norm_gain: float32 [2048], P('head'), may hold values from 0.1 to 1.9
- w_out: bfloat16 [2048, 1024], P('head'), may hold values from -0.125 to 0.125
- d_out: bfloat16 [16384, 1024], P('seq'), may hold values from -6 to 6
Outputs:
- grad_x: bfloat16 [16384, 2048], P('seq', 'head')
- grad_z: bfloat16 [16384, 2048], P('seq', 'head')
- grad_b: float32 [16384, 128], P('seq')
- grad_c: float32 [16384, 128], P('seq')
- grad_w: float32 [2048, 1024], P('head')
The draws below stay inside these ranges and needn't reach their ends.
All inputs are finite; a program needn't handle non-finite values.
Results may differ from the reference program's by a relative error of at most 0.0029.
Values sent between devices are 32-bit elements; how exact they have to be, the bound alone decides.
No kernel may reach another device: no remote copies, remote signals or barrier semaphores. Data moves between devices by JAX's collectives and lax.ppermute only.
A program may use at most 64 MiB of HBM per device.

```python
import math
import jax
import jax.numpy as jnp
from jax import lax

DM = 1024
STATE_HEADS = 32
HEAD_DIM = 64
STATE = 128
FR_DEV = 256
INNER = 2048
WINDOW_FRAMES = 16384


def draw_x_in(key, part):
    random_keys = jax.random.split(key, 3)
    column = 0.3 * jnp.exp(jax.random.uniform(random_keys[0], (INNER,), jnp.float32, 0.0, math.log(10.0)))
    head_place = (jnp.arange(INNER) // HEAD_DIM).astype(jnp.float32) / max(STATE_HEADS - 1, 1)
    rising = jnp.exp(0.5 * math.log(3.0) * head_place)
    row_scale = jnp.exp(jax.random.uniform(random_keys[1], (WINDOW_FRAMES, 1), jnp.float32, -math.log(2.0), math.log(2.0)))
    base = jnp.clip(jax.random.normal(random_keys[2], (WINDOW_FRAMES, INNER), jnp.float32), -4.0, 4.0)
    return (base * column[None, :] * rising[None, :] * row_scale).astype(jnp.bfloat16)


def log_decays(key):
    random_keys = jax.random.split(key, 7)
    fast_cut = 4
    fast_heads = jax.random.randint(random_keys[0], (STATE_HEADS, 1), 0, 8) < fast_cut
    fast_rate = jnp.exp(jax.random.uniform(random_keys[1], (STATE_HEADS, 1), jnp.float32, math.log(1.0 / 50.0), math.log(1.0 / 30.0)))
    slow_rate = jnp.exp(jax.random.uniform(random_keys[2], (STATE_HEADS, 1), jnp.float32, math.log(0.2), math.log(1.0))) / WINDOW_FRAMES
    decay_rate = jnp.where(fast_heads, fast_rate, slow_rate)
    random_offset = jnp.exp(jax.random.uniform(random_keys[3], (STATE_HEADS, WINDOW_FRAMES), jnp.float32, -math.log(2.0), math.log(2.0)))
    tile_multiplier = jnp.exp(jax.random.uniform(random_keys[4], (STATE_HEADS, WINDOW_FRAMES // FR_DEV, 1), jnp.float32, -math.log(2.0), math.log(2.0)))
    tile_multiplier = jnp.broadcast_to(tile_multiplier, (STATE_HEADS, WINDOW_FRAMES // FR_DEV, FR_DEV)).reshape(STATE_HEADS, WINDOW_FRAMES)
    spike_mask = jax.random.randint(random_keys[5], (STATE_HEADS, WINDOW_FRAMES), 0, WINDOW_FRAMES) < 2
    spike_length = jnp.log(jax.random.uniform(random_keys[6], (STATE_HEADS, WINDOW_FRAMES), jnp.float32, 0.6, 0.8))
    return -(decay_rate * random_offset * tile_multiplier) + jnp.where(spike_mask, spike_length, 0.0)


def draw_decay_fwd(key, part):
    return log_decays(jax.random.fold_in(key, 11))


def draw_decay_bwd(key, part):
    return log_decays(jax.random.fold_in(key, 12))


def shard_levels(stream_key, shape, cuts, smallest, top_value):
    gain, own = 1.0, jax.random.fold_in(stream_key, 6)
    for axis_at, parts in cuts:
        steps = jnp.exp(jax.random.uniform(jax.random.fold_in(own, axis_at), (parts,), jnp.float32, smallest / len(cuts), top_value / len(cuts)))
        gain = gain * jnp.repeat(steps, shape[axis_at] // parts).reshape([-1 if axis == axis_at else 1 for axis in range(len(shape))])
    return gain


def scatter_about(rng, dims, scale, bound, cuts=(), held_as=jnp.bfloat16):
    drawn = jax.random.normal(rng, dims, jnp.float32) * scale
    if len(cuts) > 0:
        drawn = shard_levels(rng, dims, cuts, -0.22, 0.18) * drawn
    return jnp.clip(drawn, min=-bound, max=bound).astype(held_as)


def setup_inputs(seed: int = 0) -> dict:
    splits = jax.random.split(jax.random.key(seed), 11)
    return {
        "x_in": draw_x_in(jax.random.fold_in(splits[10], 71), 0),
        "gate_in": scatter_about(splits[1], (WINDOW_FRAMES, INNER), 1.0, 6.0, ((0, 64), (1, 8))),
        "b_in": scatter_about(splits[2], (WINDOW_FRAMES, STATE), 256 ** -0.5, 0.375, ((0, 64),)),
        "c_in": scatter_about(splits[3], (WINDOW_FRAMES, STATE), 256 ** -0.5, 0.375, ((0, 64),)),
        "decay_fwd": draw_decay_fwd(jax.random.fold_in(splits[10], 71), 0),
        "decay_bwd": draw_decay_bwd(jax.random.fold_in(splits[10], 71), 0),
        "skip_gain": jnp.clip(0.5 + 1.0 * jax.random.uniform(splits[6], (STATE_HEADS,), jnp.float32) ** shard_levels(splits[6], (STATE_HEADS,), ((0, 8),), -0.2, 0.2), 0.5, 1.5),
        "norm_gain": jnp.clip(1.0 + 0.18 * jax.random.normal(splits[7], (INNER,), jnp.float32), 0.1, 1.9),
        "w_out": scatter_about(splits[8], (INNER, DM), INNER ** -0.5, 0.125, ((0, 8),)),
        "d_out": scatter_about(splits[9], (WINDOW_FRAMES, DM), 1.0, 6.0, ((0, 64),)),
    }


exact_mode = lax.Precision.HIGHEST
eps_norm = 1e-05
weight_scale = 0.0078125

def group_step(carry_state, pieces):
    signal, b_rows, c_rows, log_rates = pieces
    cumul = jnp.cumsum(log_rates, axis=1)
    spread = cumul[:, :, None] - cumul[:, None, :]
    positions = jnp.arange(log_rates.shape[1])
    causal_mask = positions[:, None] >= positions[None, :]
    weights = jnp.exp(jnp.where(causal_mask[None], spread, -jnp.inf))
    scores = jnp.dot(c_rows, b_rows.T, precision=exact_mode)
    within = jnp.einsum('hts,shp->thp', weights * scores[None], signal, precision=exact_mode)
    across = jnp.einsum('tn,hpn->thp', c_rows, carry_state, precision=exact_mode) * jnp.exp(cumul).T[:, :, None]
    end_total = cumul[:, -1]
    tail_rate = jnp.exp(end_total[:, None] - cumul)
    fresh_state = jnp.einsum('hs,shp,sn->hpn', tail_rate, signal, b_rows, precision=exact_mode)
    next_state = jnp.exp(end_total)[:, None, None] * carry_state + fresh_state
    return (next_state, within + across)

def causal(signal, b_rows, c_rows, log_rates):
    blocks = signal.shape[0] // FR_DEV
    signal_blocks = signal.reshape(blocks, FR_DEV, STATE_HEADS, HEAD_DIM)
    b_blocks = b_rows.reshape(blocks, FR_DEV, STATE)
    c_blocks = c_rows.reshape(blocks, FR_DEV, STATE)
    rate_blocks = log_rates.reshape(STATE_HEADS, blocks, FR_DEV).transpose(1, 0, 2)
    initial = jnp.zeros((STATE_HEADS, HEAD_DIM, STATE), jnp.float32)
    _, outputs = lax.scan(jax.checkpoint(group_step), initial, (signal_blocks, b_blocks, c_blocks, rate_blocks))
    return outputs.reshape(signal.shape)

def anticausal(signal, b_rows, c_rows, log_rates):
    flipped = causal(jnp.flip(signal, 0), jnp.flip(b_rows, 0), jnp.flip(c_rows, 0), jnp.flip(log_rates, 1))
    return jnp.flip(flipped, 0)

def reference(x_in, gate_in, b_in, c_in, decay_fwd, decay_bwd, skip_gain, norm_gain, w_out, d_out):
    signal = x_in.astype(jnp.float32).reshape(WINDOW_FRAMES, STATE_HEADS, HEAD_DIM)
    b_rows = b_in.astype(jnp.float32)
    c_rows = c_in.astype(jnp.float32)

    def branches(sig_vals, b_vals, c_vals):
        return causal(sig_vals, b_vals, c_vals, decay_fwd) + anticausal(sig_vals, b_vals, c_vals, decay_bwd)
    ssd_out, pullback = jax.vjp(branches, signal, b_rows, c_rows)
    merged = (ssd_out + skip_gain[None, :, None] * signal).reshape(WINDOW_FRAMES, INNER)
    gate_rows = gate_in.astype(jnp.float32)
    sigmoid_z = jax.nn.sigmoid(gate_rows)
    gated_y = merged * gate_rows * sigmoid_z
    inv_rms = lax.rsqrt(lax.optimization_barrier(jnp.mean(gated_y * gated_y, axis=1, keepdims=True)) + eps_norm)
    normed = gated_y * inv_rms * norm_gain
    grad_w = jnp.dot(normed.astype(jnp.bfloat16).T, d_out, preferred_element_type=jnp.float32) * weight_scale
    grad_n = jnp.dot(d_out, w_out.T, preferred_element_type=jnp.float32)
    scaled = grad_n * norm_gain
    cross_mean = lax.optimization_barrier(jnp.mean(gated_y * scaled, axis=1, keepdims=True))
    grad_g = inv_rms * scaled - gated_y * inv_rms * inv_rms * inv_rms * cross_mean
    grad_y = grad_g * gate_rows * sigmoid_z
    grad_z = grad_g * merged * sigmoid_z * (1.0 + gate_rows * (1.0 - sigmoid_z))
    grad_rows = grad_y.reshape(WINDOW_FRAMES, STATE_HEADS, HEAD_DIM)
    grad_sig, grad_b, grad_c = pullback(grad_rows)
    grad_x = (grad_sig + skip_gain[None, :, None] * grad_rows).reshape(WINDOW_FRAMES, INNER)
    return (grad_x.astype(jnp.bfloat16), grad_z.astype(jnp.bfloat16), grad_b, grad_c, grad_w)
```

```python
import jax
import jax.numpy as jnp
from jax import lax
from jax.experimental import pallas as pl
from jax.experimental.pallas import tpu as pltpu
from jax.sharding import Mesh, PartitionSpec as P

HEADS = 4
HEAD_DIM = 64
STATE = 128
FRAMES = 256
WIDTH = HEADS * HEAD_DIM
LANES = 128
EPS_NORM = 1e-05
WEIGHT_SCALE = 0.0078125
F32, BF16 = jnp.float32, jnp.bfloat16


def dot(a, b, ca, cb):
    return lax.dot_general(a, b, (((ca,), (cb,)), ((), ())), preferred_element_type=F32)


def halves(a):
    high = a.astype(BF16)
    return high, (a - high.astype(F32)).astype(BF16)


def dot_left(a, b, ca, cb):
    ah, al = halves(a)
    return dot(ah, b, ca, cb) + dot(al, b, ca, cb)


def dot_right(a, b, ca, cb):
    bh, bl = halves(b)
    return dot(a, bh, ca, cb) + dot(a, bl, ca, cb)


def dot_both(a, b, ca, cb):
    ah, al = halves(a)
    bh, bl = halves(b)
    return dot(ah, bh, ca, cb) + (dot(ah, bl, ca, cb) + dot(al, bh, ca, cb))


def dot_exact(a, b, ca, cb):
    return lax.dot_general(
        a, b, (((ca,), (cb,)), ((), ())), precision=lax.Precision.HIGHEST, preferred_element_type=F32
    )


def places():
    row = lax.broadcasted_iota(jnp.int32, (FRAMES, FRAMES), 0)
    col = lax.broadcasted_iota(jnp.int32, (FRAMES, FRAMES), 1)
    return row, col


def columns(df, db):
    row, col = places()
    upto = (col <= row).astype(F32)
    before = (col < row).astype(F32)
    cf = dot_exact(upto, df, 1, 1)
    be = dot_exact(before, db, 1, 1)
    end_f = cf[FRAMES - 1 :, :]
    end_b = dot_exact(jnp.ones((8, FRAMES), F32), db, 1, 1)[:1, :]
    return cf, be, end_f, end_b


def rows(df, db):
    row, col = places()
    upto = (row <= col).astype(F32)
    before = (row < col).astype(F32)
    return dot_exact(df, upto, 1, 0), dot_exact(db, before, 1, 0)


def spread(cols):
    lane = lax.broadcasted_iota(jnp.int32, (cols.shape[0], LANES), 1)
    pairs = [
        jnp.where(lane < HEAD_DIM, cols[:, 2 * g : 2 * g + 1], cols[:, 2 * g + 1 : 2 * g + 2])
        for g in range(HEADS // 2)
    ]
    return jnp.concatenate(pairs, axis=1)


def pair_decay(h, cf, be, cf_row, be_row, row, col):
    gap = jnp.where(
        row > col,
        cf[:, h : h + 1] - cf_row[h : h + 1, :],
        be_row[h : h + 1, :] - be[:, h : h + 1],
    )
    return jnp.where(row == col, 2.0, jnp.exp(jnp.minimum(gap, 0.0)))


def own_lanes(pair, hh):
    lane = lax.broadcasted_iota(jnp.int32, pair.shape, 1)
    mine = lane < HEAD_DIM if hh == 0 else lane >= HEAD_DIM
    return jnp.where(mine, pair, jnp.zeros_like(pair))


def stack(ref, start):
    return jnp.concatenate([ref[j, start : start + HEAD_DIM, :] for j in range(HEADS)], axis=0)


def local_states(x_ref, b_ref, df_ref, db_ref, out_ref):
    cf, be, end_f, end_b = columns(df_ref[...], db_ref[...])
    x = x_ref[...].astype(F32)
    b = b_ref[...]
    state_f = dot_left(x * spread(jnp.exp(end_f - cf)), b, 0, 0)
    state_b = dot_left(x * spread(jnp.exp(be)), b, 0, 0)
    total_f = jnp.exp(end_f)
    total_b = jnp.exp(end_b)
    for j in range(HEADS):
        at = slice(j * HEAD_DIM, (j + 1) * HEAD_DIM)
        out_ref[j, 0:64, :] = state_f[at, :]
        out_ref[j, 64:128, :] = state_b[at, :]
        out_ref[j, 128:136, :] = jnp.broadcast_to(total_f[:, j : j + 1], (8, LANES))
        out_ref[j, 136:144, :] = jnp.broadcast_to(total_b[:, j : j + 1], (8, LANES))


def tiles(a):
    return a.reshape(a.shape[0] // 8, 8, LANES)


def chain(order, states, totals):
    acc = states[order[0]]
    for i in order[1:]:
        acc = totals[i][None] * acc + states[i]
    return acc


def row_parts(dec_ref, rec_ref, n_x):
    state_f = [tiles(rec_ref[i, 0:64, :]) for i in range(n_x)]
    state_b = [tiles(rec_ref[i, 64:128, :]) for i in range(n_x)]
    total_f = [dec_ref[i, 128:136, :] for i in range(n_x)]
    total_b = [dec_ref[i, 136:144, :] for i in range(n_x)]
    return state_f, state_b, total_f, total_b


def product(parts):
    out = parts[0]
    for part in parts[1:]:
        out = out * part
    return out


def row_totals_first(rec_ref, out_ref):
    n_x, n_z = rec_ref.shape[0], out_ref.shape[0]
    state_f, state_b, total_f, total_b = row_parts(rec_ref, rec_ref, n_x)
    up = list(range(n_x))
    sum_f = chain(up, state_f, total_f)
    sum_b = chain(up[::-1], state_b, total_b)
    both = jnp.concatenate([sum_f, sum_b], axis=0).reshape(2 * HEAD_DIM, LANES)
    span = 2 * HEAD_DIM // n_z
    for k in range(n_z):
        out_ref[k, 0:span, :] = both[k * span : (k + 1) * span, :]
        out_ref[k, span : span + 8, :] = product(total_f if 2 * k < n_z else total_b)


def row_totals_second(rec1_ref, rec_ref, out_ref):
    n_x, n_z = rec_ref.shape[0], out_ref.shape[0]
    state_f, state_b, total_f, total_b = row_parts(rec1_ref, rec_ref, n_x)
    up = list(range(n_x))
    sum_f = chain(up[::-1], state_f, total_f)
    sum_b = chain(up, state_b, total_b)
    both = jnp.concatenate([sum_f, sum_b], axis=0).reshape(2 * HEAD_DIM, LANES)
    span = 2 * HEAD_DIM // n_z
    size = 512 // n_z
    for k in range(n_z):
        out_ref[k, 0:span, :] = both[k * span : (k + 1) * span, :]
        at = slice(128 + k * size, 128 + (k + 1) * size)
        out_ref[k, span:, :] = sum(rec_ref[i, at, :] for i in range(1, n_x)) + rec_ref[0, at, :]


def scan_up(states, totals, n):
    out, acc = [], jnp.zeros_like(states[0])
    for i in range(n):
        out.append(acc)
        acc = totals[i][None] * acc + states[i]
    return out


def scan_both(up_ref, data_ref, dec_ref, span, n_z):
    states = [tiles(data_ref[i, 0:span, :]) for i in range(n_z)]
    totals = [dec_ref[i, span : span + 8, :] for i in range(n_z)]
    up = scan_up(states, totals, n_z)
    down = scan_up(states[::-1], totals[::-1], n_z)[::-1]
    upward = up_ref[0] == 1
    return [jnp.where(upward, u, d).reshape(span, LANES) for u, d in zip(up, down)]


def scan_first(up_ref, rec_ref, out_ref):
    n_z, span = out_ref.shape[0], out_ref.shape[1]
    for i, entry in enumerate(scan_both(up_ref, rec_ref, rec_ref, span, n_z)):
        out_ref[i, :, :] = entry


def scan_second(up_ref, dec_ref, rec_ref, out_ref):
    n_z = out_ref.shape[0]
    span = 2 * HEAD_DIM // n_z
    entries = scan_both(up_ref, rec_ref, dec_ref, span, n_z)
    weight = rec_ref[0, span:, :]
    for i in range(1, n_z):
        weight = weight + rec_ref[i, span:, :]
    for i in range(n_z):
        out_ref[i, 0:span, :] = entries[i]
        out_ref[i, span:, :] = weight


def entries_of(back_ref, span, n_z):
    half = n_z // 2
    entry_f = jnp.concatenate([tiles(back_ref[k, 0:span, :]) for k in range(half)], axis=0)
    entry_b = jnp.concatenate([tiles(back_ref[k, 0:span, :]) for k in range(half, n_z)], axis=0)
    return entry_f, entry_b


def put_entries(out_ref, order, entry, states, totals, at):
    for i in order:
        out_ref[i, at : at + HEAD_DIM, :] = entry.reshape(HEAD_DIM, LANES)
        entry = totals[i][None] * entry + states[i]


def row_entries_first(back_ref, rec_ref, out_ref):
    n_z, span = back_ref.shape[0], back_ref.shape[1]
    n_x = rec_ref.shape[0]
    state_f, state_b, total_f, total_b = row_parts(rec_ref, rec_ref, n_x)
    entry_f, entry_b = entries_of(back_ref, span, n_z)
    up = list(range(n_x))
    put_entries(out_ref, up, entry_f, state_f, total_f, 0)
    put_entries(out_ref, up[::-1], entry_b, state_b, total_b, HEAD_DIM)


def row_entries_second(back_ref, rec1_ref, rec_ref, out_ref):
    n_z = back_ref.shape[0]
    n_x = rec_ref.shape[0]
    span, size = 2 * HEAD_DIM // n_z, 512 // n_z
    state_f, state_b, total_f, total_b = row_parts(rec1_ref, rec_ref, n_x)
    entry_f, entry_b = entries_of(back_ref, span, n_z)
    up = list(range(n_x))
    put_entries(out_ref, up[::-1], entry_f, state_f, total_f, 0)
    put_entries(out_ref, up, entry_b, state_b, total_b, HEAD_DIM)
    for k in range(n_z):
        weight = back_ref[k, span:, :]
        for i in range(n_x):
            out_ref[i, 128 + k * size : 128 + (k + 1) * size, :] = weight


def across_rows(cols):
    lane = lax.broadcasted_iota(jnp.int32, (LANES, LANES), 1)
    grid = jnp.zeros((LANES, LANES), F32)
    for i, col in enumerate(cols):
        for part in range(FRAMES // LANES):
            at = i * (FRAMES // LANES) + part
            grid = jnp.where(lane == at, col[part * LANES : (part + 1) * LANES, :], grid)
    return jnp.transpose(grid)[0:8, :]


def outputs(
    skip_ref, x_ref, z_ref, b_ref, c_ref, df_ref, db_ref, gain_ref, w_ref, do_ref, ent_ref,
    y_ref, m_ref, sums_ref,
):
    df, db = df_ref[...], db_ref[...]
    cf, be, end_f, end_b = columns(df, db)
    cf_row, be_row = rows(df, db)
    row, col = places()
    c = c_ref[...]
    scores = dot(c, b_ref[...], 1, 1)
    far = spread(jnp.exp(cf)) * dot_right(c, stack(ent_ref, 0), 1, 1)
    far = far + spread(jnp.exp(end_b - be)) * dot_right(c, stack(ent_ref, HEAD_DIM), 1, 1)
    near = []
    lane = lax.broadcasted_iota(jnp.int32, (1, LANES), 1)
    for g in range(HEADS // 2):
        pair = x_ref[:, g * LANES : (g + 1) * LANES]
        acc = jnp.where(lane < HEAD_DIM, skip_ref[2 * g], skip_ref[2 * g + 1]) * pair.astype(F32)
        for hh in range(2):
            weights = scores * pair_decay(2 * g + hh, cf, be, cf_row, be_row, row, col)
            acc = acc + dot_left(weights, own_lanes(pair, hh), 1, 0)
        near.append(acc)
    y = far + jnp.concatenate(near, axis=1)
    z = z_ref[...].astype(F32)
    u = y * z * jax.nn.sigmoid(z)
    m = dot(do_ref[...], w_ref[...], 1, 1) * gain_ref[...]
    y_ref[...] = y
    m_ref[...] = m
    sums = across_rows([jnp.sum(u * u, axis=1, keepdims=True), jnp.sum(u * m, axis=1, keepdims=True)])
    for i in range(sums_ref.shape[0]):
        sums_ref[i, :, :] = sums


def gradients(
    sums_ref, y_ref, m_ref, z_ref, c_ref, df_ref, db_ref, gain_ref, do_ref,
    dy_ref, gz_ref, out_ref, *, inner,
):
    total = sums_ref[0, :, :]
    for i in range(1, sums_ref.shape[0]):
        total = total + sums_ref[i, :, :]
    grid = jnp.transpose(jnp.concatenate([total, jnp.zeros((LANES - 8, LANES), F32)], axis=0))
    square = jnp.concatenate([grid[:, 0:1], grid[:, 1:2]], axis=0) / inner
    cross = jnp.concatenate([grid[:, 2:3], grid[:, 3:4]], axis=0) / inner
    q = lax.rsqrt(square + EPS_NORM)
    y, m, z = y_ref[...], m_ref[...], z_ref[...].astype(F32)
    sig = jax.nn.sigmoid(z)
    silu = z * sig
    u = y * z * sig
    normed = (u * q * gain_ref[...]).astype(BF16)
    du = q * m - u * (q * q * q * cross)
    dy = du * silu
    gz_ref[...] = (du * y * sig * (1.0 + z * (1.0 - sig))).astype(BF16)
    dy_ref[...] = dy
    cf, be, end_f, end_b = columns(df_ref[...], db_ref[...])
    c = c_ref[...]
    back_f = dot_left(dy * spread(jnp.exp(cf)), c, 0, 0)
    back_b = dot_left(dy * spread(jnp.exp(end_b - be)), c, 0, 0)
    weight = dot(normed, do_ref[...], 0, 0)
    for j in range(HEADS):
        at = slice(j * HEAD_DIM, (j + 1) * HEAD_DIM)
        out_ref[j, 0:64, :] = back_f[at, :]
        out_ref[j, 64:128, :] = back_b[at, :]
        for block in range(weight.shape[1] // LANES):
            out_ref[j, 128 + block * 64 : 192 + block * 64, :] = weight[
                at, block * LANES : (block + 1) * LANES
            ]


def finish(
    skip_ref, x_ref, b_ref, c_ref, df_ref, db_ref, dy_ref, ent_ref, exit_ref,
    gx_ref, gw_ref, out_ref,
):
    df, db = df_ref[...], db_ref[...]
    cf, be, end_f, end_b = columns(df, db)
    cf_row, be_row = rows(df, db)
    row, col = places()
    b, c, dy = b_ref[...], c_ref[...], dy_ref[...]
    x = x_ref[...].astype(F32)
    scores = dot(c, b, 1, 1)
    pair_sum = jnp.zeros((FRAMES, FRAMES), F32)
    near = []
    lane = lax.broadcasted_iota(jnp.int32, (1, LANES), 1)
    for g in range(HEADS // 2):
        at = slice(g * LANES, (g + 1) * LANES)
        acc = jnp.where(lane < HEAD_DIM, skip_ref[2 * g], skip_ref[2 * g + 1]) * dy[:, at]
        for hh in range(2):
            decay = pair_decay(2 * g + hh, cf, be, cf_row, be_row, row, col)
            dy_own = own_lanes(dy[:, at], hh)
            pair_sum = pair_sum + decay * dot_left(dy_own, x_ref[:, at], 1, 1)
            acc = acc + dot_both(scores * decay, dy_own, 0, 0)
        near.append(acc)
    rise_f, rise_b = spread(jnp.exp(cf)), spread(jnp.exp(end_b - be))
    tail_f, lead_b = spread(jnp.exp(end_f - cf)), spread(jnp.exp(be))
    entry_f, entry_b = stack(ent_ref, 0), stack(ent_ref, HEAD_DIM)
    exit_f, exit_b = stack(exit_ref, 0), stack(exit_ref, HEAD_DIM)
    gx = jnp.concatenate(near, axis=1)
    gx = gx + tail_f * dot_right(b, exit_f, 1, 1) + lead_b * dot_right(b, exit_b, 1, 1)
    gx_ref[...] = gx.astype(BF16)
    grad_c = dot_left(pair_sum, b, 1, 0)
    grad_c = grad_c + dot_both(dy * rise_f, entry_f, 1, 0) + dot_both(dy * rise_b, entry_b, 1, 0)
    grad_b = dot_left(pair_sum, c, 0, 0)
    grad_b = grad_b + dot_both(x * tail_f, exit_f, 1, 0) + dot_both(x * lead_b, exit_b, 1, 0)
    n = out_ref.shape[0]
    size = FRAMES // n
    for i in range(n):
        out_ref[i, 0:size, :] = grad_b[i * size : (i + 1) * size, :]
        out_ref[i, size : 2 * size, :] = grad_c[i * size : (i + 1) * size, :]
    for j in range(HEADS):
        for block in range(gw_ref.shape[1] // LANES):
            gw_ref[j * 64 : (j + 1) * 64, block * LANES : (block + 1) * LANES] = (
                exit_ref[j, 128 + block * 64 : 192 + block * 64, :] * WEIGHT_SCALE
            )


def add_up(rec_ref, out_ref):
    n = rec_ref.shape[0]
    total = rec_ref[0, :, :]
    for i in range(1, n):
        total = total + rec_ref[i, :, :]
    for i in range(n):
        out_ref[i, :, :] = total


def deal_out(rec_ref, gb_ref, gc_ref):
    n = rec_ref.shape[0]
    size = FRAMES // n
    for i in range(n):
        gb_ref[i * size : (i + 1) * size, :] = rec_ref[i, 0:size, :]
        gc_ref[i * size : (i + 1) * size, :] = rec_ref[i, size : 2 * size, :]


VMEM = pl.BlockSpec(memory_space=pltpu.VMEM)
SMEM = pl.BlockSpec(memory_space=pltpu.SMEM)


def call(kernel, name, out, *args, scalars=0):
    shapes = [jax.ShapeDtypeStruct(shape, dtype) for shape, dtype in out]
    single = len(shapes) == 1
    return pl.pallas_call(
        kernel,
        name=name,
        out_shape=shapes[0] if single else tuple(shapes),
        in_specs=[SMEM] * scalars + [VMEM] * (len(args) - scalars),
        out_specs=VMEM if single else tuple(VMEM for _ in shapes),
        compiler_params=pltpu.CompilerParams(vmem_limit_bytes=48 * 1024 * 1024),
    )(*args)


def exchange(a, axis):
    return lax.all_to_all(a, axis, 0, 0, tiled=True)


def body(x_in, gate_in, b_in, c_in, decay_fwd, decay_bwd, skip_gain, norm_gain, w_out, d_out):
    n_z, n_x, n_h = lax.axis_size("z"), lax.axis_size("x"), lax.axis_size("head")
    gain = norm_gain.reshape(1, WIDTH)
    span = 2 * HEAD_DIM // n_z
    size = 512 // n_z
    first_half = (2 * lax.axis_index("z") < n_z).astype(jnp.int32).reshape(1)

    sent = call(local_states, "local_states", [((n_x, 144, LANES), F32)], x_in, b_in, decay_fwd, decay_bwd)
    rec1 = exchange(sent, "x")
    sent = call(row_totals_first, "row_totals_first", [((n_z, span + 8, LANES), F32)], rec1)
    recz1 = exchange(sent, "z")
    sent = call(scan_first, "scan_first", [((n_z, span, LANES), F32)], first_half, recz1, scalars=1)
    back = exchange(sent, "z")
    sent = call(row_entries_first, "row_entries_first", [((n_x, 128, LANES), F32)], back, rec1)
    entries = exchange(sent, "x")

    y, m, sums = call(
        outputs, "outputs",
        [((FRAMES, WIDTH), F32), ((FRAMES, WIDTH), F32), ((n_h, 8, LANES), F32)],
        skip_gain, x_in, gate_in, b_in, c_in, decay_fwd, decay_bwd, gain, w_out, d_out, entries,
        scalars=1,
    )
    sums = exchange(sums, "head")

    def gradients_here(*refs):
        gradients(*refs, inner=WIDTH * n_h)

    dy, grad_z, sent = call(
        gradients_here, "gradients",
        [((FRAMES, WIDTH), F32), ((FRAMES, WIDTH), BF16), ((n_x, 640, LANES), F32)],
        sums, y, m, gate_in, c_in, decay_fwd, decay_bwd, gain, d_out,
    )
    rec2 = exchange(sent, "x")
    sent = call(row_totals_second, "row_totals_second", [((n_z, span + size, LANES), F32)], rec1, rec2)
    recz2 = exchange(sent, "z")
    sent = call(
        scan_second, "scan_second", [((n_z, span + size, LANES), F32)],
        1 - first_half, recz1, recz2, scalars=1,
    )
    back = exchange(sent, "z")
    sent = call(row_entries_second, "row_entries_second", [((n_x, 640, LANES), F32)], back, rec1, rec2)
    exits = exchange(sent, "x")

    chunk = 2 * FRAMES // n_h
    grad_x, grad_w, sent = call(
        finish, "finish",
        [((FRAMES, WIDTH), BF16), ((WIDTH, d_out.shape[1]), F32), ((n_h, chunk, LANES), F32)],
        skip_gain, x_in, b_in, c_in, decay_fwd, decay_bwd, dy, entries, exits,
        scalars=1,
    )
    rec = exchange(sent, "head")
    sent = call(add_up, "add_up", [((n_h, chunk, LANES), F32)], rec)
    rec = exchange(sent, "head")
    grad_b, grad_c = call(deal_out, "deal_out", [((FRAMES, STATE), F32)] * 2, rec)
    return grad_x, grad_z, grad_b, grad_c, grad_w


def solution(mesh):
    n_seq, n_head = mesh.devices.shape
    split = Mesh(mesh.devices.reshape(n_seq // HEADS, HEADS, n_head), ("z", "x", "head"))
    seq = ("z", "x")
    in_specs = (
        P(seq, "head"),
        P(seq, "head"),
        P(seq, None),
        P(seq, None),
        P("head", seq),
        P("head", seq),
        P("head"),
        P("head"),
        P("head", None),
        P(seq, None),
    )
    out_specs = (
        P(seq, "head"),
        P(seq, "head"),
        P(seq, None),
        P(seq, None),
        P("head", None),
    )
    return jax.shard_map(body, mesh=split, in_specs=in_specs, out_specs=out_specs, check_vma=False)
```

```python
import functools

import jax
import jax.numpy as jnp
from jax import lax
from jax.experimental import pallas as pl
from jax.experimental.pallas import tpu as pltpu
from jax.sharding import Mesh, PartitionSpec as P

HEADS = 4
HEAD_DIM = 64
STATE = 128
FRAMES = 256
WIDTH = HEADS * HEAD_DIM
LANES = 128
EPS_NORM = 1e-05
WEIGHT_SCALE = 0.0078125
F32, BF16 = jnp.float32, jnp.bfloat16


def dot(a, b, ca, cb):
    return lax.dot_general(a, b, (((ca,), (cb,)), ((), ())), preferred_element_type=F32)


def halves(a):
    high = a.astype(BF16)
    return high, (a - high.astype(F32)).astype(BF16)


def dot_left(a, b, ca, cb):
    ah, al = halves(a)
    return dot(ah, b, ca, cb) + dot(al, b, ca, cb)


def dot_right(a, b, ca, cb):
    bh, bl = halves(b)
    return dot(a, bh, ca, cb) + dot(a, bl, ca, cb)


def dot_both(a, b, ca, cb):
    ah, al = halves(a)
    bh, bl = halves(b)
    return dot(ah, bh, ca, cb) + (dot(ah, bl, ca, cb) + dot(al, bh, ca, cb))


def dot_exact(a, b, ca, cb):
    return lax.dot_general(
        a, b, (((ca,), (cb,)), ((), ())), precision=lax.Precision.HIGHEST, preferred_element_type=F32
    )


def places():
    row = lax.broadcasted_iota(jnp.int32, (FRAMES, FRAMES), 0)
    col = lax.broadcasted_iota(jnp.int32, (FRAMES, FRAMES), 1)
    return row, col


def columns(df, db):
    row, col = places()
    upto = (col <= row).astype(F32)
    before = (col < row).astype(F32)
    cf = dot_exact(upto, df, 1, 1)
    be = dot_exact(before, db, 1, 1)
    end_f = cf[FRAMES - 1 :, :]
    end_b = dot_exact(jnp.ones((8, FRAMES), F32), db, 1, 1)[:1, :]
    return cf, be, end_f, end_b


def rows(df, db):
    row, col = places()
    upto = (row <= col).astype(F32)
    before = (row < col).astype(F32)
    return dot_exact(df, upto, 1, 0), dot_exact(db, before, 1, 0)


def spread(cols):
    lane = lax.broadcasted_iota(jnp.int32, (cols.shape[0], LANES), 1)
    pairs = [
        jnp.where(lane < HEAD_DIM, cols[:, 2 * g : 2 * g + 1], cols[:, 2 * g + 1 : 2 * g + 2])
        for g in range(HEADS // 2)
    ]
    return jnp.concatenate(pairs, axis=1)


def pair_decay(h, cf, be, cf_row, be_row, row, col):
    gap = jnp.where(
        row > col,
        cf[:, h : h + 1] - cf_row[h : h + 1, :],
        be_row[h : h + 1, :] - be[:, h : h + 1],
    )
    return jnp.where(row == col, 2.0, jnp.exp(jnp.minimum(gap, 0.0)))


def own_lanes(pair, hh):
    lane = lax.broadcasted_iota(jnp.int32, pair.shape, 1)
    mine = lane < HEAD_DIM if hh == 0 else lane >= HEAD_DIM
    return jnp.where(mine, pair, jnp.zeros_like(pair))


def put_slices(out_ref, forward, backward):
    n = out_ref.shape[0]
    size = WIDTH // n
    for i in range(n):
        at = slice(i * size, (i + 1) * size)
        out_ref[i, 0:size, :] = forward[at, :]
        out_ref[i, size : 2 * size, :] = backward[at, :]


def take_slices(ref):
    n = ref.shape[0]
    size = WIDTH // n
    forward = jnp.concatenate([ref[i, 0:size, :] for i in range(n)], axis=0)
    backward = jnp.concatenate([ref[i, size : 2 * size, :] for i in range(n)], axis=0)
    return forward, backward


def local_states(x_ref, b_ref, df_ref, db_ref, out_ref):
    cf, be, end_f, end_b = columns(df_ref[...], db_ref[...])
    x = x_ref[...].astype(F32)
    b = b_ref[...]
    state_f = dot_left(x * spread(jnp.exp(end_f - cf)), b, 0, 0)
    state_b = dot_left(x * spread(jnp.exp(be)), b, 0, 0)
    put_slices(out_ref, state_f, state_b)
    n = out_ref.shape[0]
    size = WIDTH // n
    total_f, total_b = jnp.exp(end_f), jnp.exp(end_b)
    half = lax.broadcasted_iota(jnp.int32, (8, LANES), 0) < 4
    for j in range(HEADS):
        both = jnp.where(half, total_f[:, j : j + 1], total_b[:, j : j + 1])
        for i in range(j * n // HEADS, (j + 1) * n // HEADS):
            out_ref[i, 2 * size :, :] = both


def totals_at(ref, i, start):
    return ref[i, start : start + 1, :], ref[i, start + 4 : start + 5, :]


def sliced(ref, i, size):
    return ref[i, 0:size, :], ref[i, size : 2 * size, :]


def group_totals(dec_ref, rec_ref, out_ref, *, forward_up):
    n = rec_ref.shape[0]
    size = WIDTH // n
    decays = [totals_at(dec_ref, i, 2 * size) for i in range(n)]
    parts = [sliced(rec_ref, i, size) for i in range(n)]
    ups = list(range(n))
    for branch, up in enumerate((forward_up, not forward_up)):
        order = ups if up else ups[::-1]
        acc = parts[order[0]][branch]
        for i in order[1:]:
            acc = decays[i][branch] * acc + parts[i][branch]
        for k in range(out_ref.shape[0]):
            out_ref[k, branch * size : (branch + 1) * size, :] = acc
    if out_ref.shape[1] > 2 * size:
        all_f, all_b = decays[0]
        for i in range(1, n):
            all_f, all_b = all_f * decays[i][0], all_b * decays[i][1]
        half = lax.broadcasted_iota(jnp.int32, (8, LANES), 0) < 4
        for k in range(out_ref.shape[0]):
            out_ref[k, 2 * size :, :] = jnp.where(half, all_f, all_b)


def group_entries(place_ref, zdec_ref, zrec_ref, dec_ref, rec_ref, out_ref, *, forward_up):
    n_g, n = zrec_ref.shape[0], rec_ref.shape[0]
    size = WIDTH // n
    place = place_ref[0]
    for branch, up in enumerate((forward_up, not forward_up)):
        groups = list(range(n_g)) if up else list(range(n_g))[::-1]
        entry = jnp.zeros((size, LANES), F32)
        for k in groups:
            state = sliced(zrec_ref, k, size)[branch]
            passed = place > k if up else place < k
            entry = jnp.where(passed, totals_at(zdec_ref, k, 2 * size)[branch] * entry + state, entry)
        members = list(range(n)) if up else list(range(n))[::-1]
        for i in members:
            out_ref[i, branch * size : (branch + 1) * size, :] = entry
            entry = totals_at(dec_ref, i, 2 * size)[branch] * entry + sliced(rec_ref, i, size)[branch]


def add_rows(rec_ref, out_ref):
    total = rec_ref[0, :, :]
    for i in range(1, rec_ref.shape[0]):
        total = total + rec_ref[i, :, :]
    size = out_ref.shape[1]
    for k in range(out_ref.shape[0]):
        out_ref[k, :, :] = total[k * size : (k + 1) * size, :]


def copy_rows(rec_ref, out_ref):
    n = rec_ref.shape[0]
    size = rec_ref.shape[1]
    for k in range(n):
        part = rec_ref[k, :, :]
        for i in range(out_ref.shape[0]):
            out_ref[i, k * size : (k + 1) * size, :] = part


def weight_rows(rec_ref, gw_ref):
    for j in range(HEADS):
        for block in range(gw_ref.shape[1] // LANES):
            gw_ref[j * 64 : (j + 1) * 64, block * LANES : (block + 1) * LANES] = (
                rec_ref[j, block * 64 : (block + 1) * 64, :] * WEIGHT_SCALE
            )


def across_rows(cols):
    lane = lax.broadcasted_iota(jnp.int32, (LANES, LANES), 1)
    grid = jnp.zeros((LANES, LANES), F32)
    for i, col in enumerate(cols):
        for part in range(FRAMES // LANES):
            at = i * (FRAMES // LANES) + part
            grid = jnp.where(lane == at, col[part * LANES : (part + 1) * LANES, :], grid)
    return jnp.transpose(grid)[0:8, :]


def outputs(
    skip_ref, x_ref, z_ref, b_ref, c_ref, df_ref, db_ref, gain_ref, w_ref, do_ref, ent_ref,
    y_ref, m_ref, sums_ref,
):
    df, db = df_ref[...], db_ref[...]
    cf, be, end_f, end_b = columns(df, db)
    cf_row, be_row = rows(df, db)
    row, col = places()
    c = c_ref[...]
    scores = dot(c, b_ref[...], 1, 1)
    entry_f, entry_b = take_slices(ent_ref)
    far = spread(jnp.exp(cf)) * dot_right(c, entry_f, 1, 1)
    far = far + spread(jnp.exp(end_b - be)) * dot_right(c, entry_b, 1, 1)
    near = []
    lane = lax.broadcasted_iota(jnp.int32, (1, LANES), 1)
    for g in range(HEADS // 2):
        pair = x_ref[:, g * LANES : (g + 1) * LANES]
        acc = jnp.where(lane < HEAD_DIM, skip_ref[2 * g], skip_ref[2 * g + 1]) * pair.astype(F32)
        for hh in range(2):
            weights = scores * pair_decay(2 * g + hh, cf, be, cf_row, be_row, row, col)
            acc = acc + dot_left(weights, own_lanes(pair, hh), 1, 0)
        near.append(acc)
    y = far + jnp.concatenate(near, axis=1)
    z = z_ref[...].astype(F32)
    u = y * z * jax.nn.sigmoid(z)
    m = dot(do_ref[...], w_ref[...], 1, 1) * gain_ref[...]
    y_ref[...] = y
    m_ref[...] = m
    sums = across_rows([jnp.sum(u * u, axis=1, keepdims=True), jnp.sum(u * m, axis=1, keepdims=True)])
    for i in range(sums_ref.shape[0]):
        sums_ref[i, :, :] = sums


def gradients(
    sums_ref, y_ref, m_ref, z_ref, c_ref, df_ref, db_ref, gain_ref, do_ref,
    dy_ref, gz_ref, out_ref, w_ref, *, inner,
):
    total = sums_ref[0, :, :]
    for i in range(1, sums_ref.shape[0]):
        total = total + sums_ref[i, :, :]
    grid = jnp.transpose(jnp.concatenate([total, jnp.zeros((LANES - 8, LANES), F32)], axis=0))
    square = jnp.concatenate([grid[:, 0:1], grid[:, 1:2]], axis=0) / inner
    cross = jnp.concatenate([grid[:, 2:3], grid[:, 3:4]], axis=0) / inner
    q = lax.rsqrt(square + EPS_NORM)
    y, m, z = y_ref[...], m_ref[...], z_ref[...].astype(F32)
    sig = jax.nn.sigmoid(z)
    silu = z * sig
    u = y * z * sig
    normed = (u * q * gain_ref[...]).astype(BF16)
    du = q * m - u * (q * q * q * cross)
    dy = du * silu
    gz_ref[...] = (du * y * sig * (1.0 + z * (1.0 - sig))).astype(BF16)
    dy_ref[...] = dy
    cf, be, end_f, end_b = columns(df_ref[...], db_ref[...])
    c = c_ref[...]
    back_f = dot_left(dy * spread(jnp.exp(cf)), c, 0, 0)
    back_b = dot_left(dy * spread(jnp.exp(end_b - be)), c, 0, 0)
    put_slices(out_ref, back_f, back_b)
    weight = dot(normed, do_ref[...], 0, 0)
    for j in range(HEADS):
        for block in range(weight.shape[1] // LANES):
            w_ref[j, block * 64 : (block + 1) * 64, :] = weight[
                j * 64 : (j + 1) * 64, block * LANES : (block + 1) * LANES
            ]


def finish(
    skip_ref, x_ref, b_ref, c_ref, df_ref, db_ref, dy_ref, ent_ref, exit_ref,
    gx_ref, out_ref,
):
    df, db = df_ref[...], db_ref[...]
    cf, be, end_f, end_b = columns(df, db)
    cf_row, be_row = rows(df, db)
    row, col = places()
    b, c, dy = b_ref[...], c_ref[...], dy_ref[...]
    x = x_ref[...].astype(F32)
    scores = dot(c, b, 1, 1)
    pair_sum = jnp.zeros((FRAMES, FRAMES), F32)
    near = []
    lane = lax.broadcasted_iota(jnp.int32, (1, LANES), 1)
    for g in range(HEADS // 2):
        at = slice(g * LANES, (g + 1) * LANES)
        acc = jnp.where(lane < HEAD_DIM, skip_ref[2 * g], skip_ref[2 * g + 1]) * dy[:, at]
        for hh in range(2):
            decay = pair_decay(2 * g + hh, cf, be, cf_row, be_row, row, col)
            dy_own = own_lanes(dy[:, at], hh)
            pair_sum = pair_sum + decay * dot_left(dy_own, x_ref[:, at], 1, 1)
            acc = acc + dot_both(scores * decay, dy_own, 0, 0)
        near.append(acc)
    rise_f, rise_b = spread(jnp.exp(cf)), spread(jnp.exp(end_b - be))
    tail_f, lead_b = spread(jnp.exp(end_f - cf)), spread(jnp.exp(be))
    entry_f, entry_b = take_slices(ent_ref)
    exit_f, exit_b = take_slices(exit_ref)
    gx = jnp.concatenate(near, axis=1)
    gx = gx + tail_f * dot_right(b, exit_f, 1, 1) + lead_b * dot_right(b, exit_b, 1, 1)
    gx_ref[...] = gx.astype(BF16)
    grad_c = dot_left(pair_sum, b, 1, 0)
    grad_c = grad_c + dot_both(dy * rise_f, entry_f, 1, 0) + dot_both(dy * rise_b, entry_b, 1, 0)
    grad_b = dot_left(pair_sum, c, 0, 0)
    grad_b = grad_b + dot_both(x * tail_f, exit_f, 1, 0) + dot_both(x * lead_b, exit_b, 1, 0)
    n = out_ref.shape[0]
    size = FRAMES // n
    for i in range(n):
        out_ref[i, 0:size, :] = grad_b[i * size : (i + 1) * size, :]
        out_ref[i, size : 2 * size, :] = grad_c[i * size : (i + 1) * size, :]


def add_up(rec_ref, out_ref):
    n = rec_ref.shape[0]
    total = rec_ref[0, :, :]
    for i in range(1, n):
        total = total + rec_ref[i, :, :]
    for i in range(n):
        out_ref[i, :, :] = total


def deal_out(rec_ref, gb_ref, gc_ref):
    n = rec_ref.shape[0]
    size = FRAMES // n
    for i in range(n):
        gb_ref[i * size : (i + 1) * size, :] = rec_ref[i, 0:size, :]
        gc_ref[i * size : (i + 1) * size, :] = rec_ref[i, size : 2 * size, :]


VMEM = pl.BlockSpec(memory_space=pltpu.VMEM)
SMEM = pl.BlockSpec(memory_space=pltpu.SMEM)


def call(kernel, name, out, *args, scalars=0):
    shapes = [jax.ShapeDtypeStruct(shape, dtype) for shape, dtype in out]
    single = len(shapes) == 1
    return pl.pallas_call(
        kernel,
        name=name,
        out_shape=shapes[0] if single else tuple(shapes),
        in_specs=[SMEM] * scalars + [VMEM] * (len(args) - scalars),
        out_specs=VMEM if single else tuple(VMEM for _ in shapes),
        compiler_params=pltpu.CompilerParams(vmem_limit_bytes=48 * 1024 * 1024),
    )(*args)


def exchange(a, axis):
    return lax.all_to_all(a, axis, 0, 0, tiled=True)


def body(x_in, gate_in, b_in, c_in, decay_fwd, decay_bwd, skip_gain, norm_gain, w_out, d_out):
    n_hi, n_lo, n_x, n_h = (lax.axis_size(axis) for axis in ("z_hi", "z_lo", "x", "head"))
    group, along = ("z_lo", "x"), ("z_hi", "z_lo")
    n, n_z = n_lo * n_x, n_hi * n_lo
    gain = norm_gain.reshape(1, WIDTH)
    state = 2 * WIDTH // n
    place = lax.axis_index("z_hi").astype(jnp.int32).reshape(1)

    sent = call(local_states, "local_states", [((n, state + 8, LANES), F32)], x_in, b_in, decay_fwd, decay_bwd)
    rec1 = exchange(sent, group)
    up = functools.partial(group_totals, forward_up=True)
    sent = call(up, "totals_up", [((n_hi, state + 8, LANES), F32)], rec1, rec1)
    recz1 = exchange(sent, "z_hi")
    up = functools.partial(group_entries, forward_up=True)
    sent = call(up, "entries_up", [((n, state, LANES), F32)], place, recz1, recz1, rec1, rec1, scalars=1)
    entries = exchange(sent, group)

    y, m, sums = call(
        outputs, "outputs",
        [((FRAMES, WIDTH), F32), ((FRAMES, WIDTH), F32), ((n_h, 8, LANES), F32)],
        skip_gain, x_in, gate_in, b_in, c_in, decay_fwd, decay_bwd, gain, w_out, d_out, entries,
        scalars=1,
    )
    sums = exchange(sums, "head")
    dy, grad_z, sent, weight = call(
        functools.partial(gradients, inner=WIDTH * n_h), "gradients",
        [((FRAMES, WIDTH), F32), ((FRAMES, WIDTH), BF16), ((n, state, LANES), F32), ((n_x, 512, LANES), F32)],
        sums, y, m, gate_in, c_in, decay_fwd, decay_bwd, gain, d_out,
    )

    rec2 = exchange(sent, group)
    down = functools.partial(group_totals, forward_up=False)
    sent = call(down, "totals_down", [((n_hi, state, LANES), F32)], rec1, rec2)
    recz2 = exchange(sent, "z_hi")
    down = functools.partial(group_entries, forward_up=False)
    sent = call(down, "entries_down", [((n, state, LANES), F32)], place, recz1, recz2, rec1, rec2, scalars=1)
    exits = exchange(sent, group)

    weight = exchange(weight, "x")
    weight = call(add_rows, "weight_x", [((n_z, 512 // n_z, LANES), F32)], weight)
    weight = exchange(weight, along)
    weight = call(add_up, "weight_z", [((n_z, 512 // n_z, LANES), F32)], weight)
    weight = exchange(weight, along)
    weight = call(copy_rows, "weight_copy", [((n_x, 512, LANES), F32)], weight)
    weight = exchange(weight, "x")
    grad_w = call(weight_rows, "weight_rows", [((WIDTH, d_out.shape[1]), F32)], weight)

    chunk = 2 * FRAMES // n_h
    grad_x, sent = call(
        finish, "finish",
        [((FRAMES, WIDTH), BF16), ((n_h, chunk, LANES), F32)],
        skip_gain, x_in, b_in, c_in, decay_fwd, decay_bwd, dy, entries, exits,
        scalars=1,
    )
    rec = exchange(sent, "head")
    sent = call(add_up, "add_up", [((n_h, chunk, LANES), F32)], rec)
    rec = exchange(sent, "head")
    grad_b, grad_c = call(deal_out, "deal_out", [((FRAMES, STATE), F32)] * 2, rec)
    return grad_x, grad_z, grad_b, grad_c, grad_w


def solution(mesh):
    n_seq, n_head = mesh.devices.shape
    n_z = n_seq // HEADS
    n_lo = min(4, n_z // 2)
    split = Mesh(mesh.devices.reshape(n_z // n_lo, n_lo, HEADS, n_head), ("z_hi", "z_lo", "x", "head"))
    seq = ("z_hi", "z_lo", "x")
    in_specs = (
        P(seq, "head"),
        P(seq, "head"),
        P(seq, None),
        P(seq, None),
        P("head", seq),
        P("head", seq),
        P("head"),
        P("head"),
        P("head", None),
        P(seq, None),
    )
    out_specs = (
        P(seq, "head"),
        P(seq, "head"),
        P(seq, None),
        P(seq, None),
        P("head", None),
    )
    return jax.shard_map(body, mesh=split, in_specs=in_specs, out_specs=out_specs, check_vma=False)
```

```python
import functools

import jax
import jax.numpy as jnp
from jax import lax
from jax.experimental import pallas as pl
from jax.experimental.pallas import tpu as pltpu
from jax.sharding import Mesh, PartitionSpec as P

HEADS = 4
HEAD_DIM = 64
STATE = 128
FRAMES = 256
WIDTH = HEADS * HEAD_DIM
LANES = 128
EPS_NORM = 1e-05
WEIGHT_SCALE = 0.0078125
F32, BF16 = jnp.float32, jnp.bfloat16


def dot(a, b, ca, cb):
    return lax.dot_general(a, b, (((ca,), (cb,)), ((), ())), preferred_element_type=F32)


def halves(a):
    high = a.astype(BF16)
    return high, (a - high.astype(F32)).astype(BF16)


def dot_left(a, b, ca, cb):
    ah, al = halves(a)
    return dot(ah, b, ca, cb) + dot(al, b, ca, cb)


def dot_right(a, b, ca, cb):
    bh, bl = halves(b)
    return dot(a, bh, ca, cb) + dot(a, bl, ca, cb)


def dot_both(a, b, ca, cb):
    ah, al = halves(a)
    bh, bl = halves(b)
    return dot(ah, bh, ca, cb) + (dot(ah, bl, ca, cb) + dot(al, bh, ca, cb))


def dot_exact(a, b, ca, cb):
    return lax.dot_general(
        a, b, (((ca,), (cb,)), ((), ())), precision=lax.Precision.HIGHEST, preferred_element_type=F32
    )


def places():
    row = lax.broadcasted_iota(jnp.int32, (FRAMES, FRAMES), 0)
    col = lax.broadcasted_iota(jnp.int32, (FRAMES, FRAMES), 1)
    return row, col


def columns(df, db):
    row, col = places()
    upto = (col <= row).astype(F32)
    before = (col < row).astype(F32)
    cf = dot_exact(upto, df, 1, 1)
    be = dot_exact(before, db, 1, 1)
    end_f = cf[FRAMES - 1 :, :]
    end_b = dot_exact(jnp.ones((8, FRAMES), F32), db, 1, 1)[:1, :]
    return cf, be, end_f, end_b


def rows(df, db):
    row, col = places()
    upto = (row <= col).astype(F32)
    before = (row < col).astype(F32)
    return dot_exact(df, upto, 1, 0), dot_exact(db, before, 1, 0)


def spread(cols):
    lane = lax.broadcasted_iota(jnp.int32, (cols.shape[0], LANES), 1)
    pairs = [
        jnp.where(lane < HEAD_DIM, cols[:, 2 * g : 2 * g + 1], cols[:, 2 * g + 1 : 2 * g + 2])
        for g in range(HEADS // 2)
    ]
    return jnp.concatenate(pairs, axis=1)


def pair_decay(h, cf, be, cf_row, be_row, row, col):
    gap = jnp.where(
        row > col,
        cf[:, h : h + 1] - cf_row[h : h + 1, :],
        be_row[h : h + 1, :] - be[:, h : h + 1],
    )
    return jnp.where(row == col, 2.0, jnp.exp(jnp.minimum(gap, 0.0)))


def own_lanes(pair, hh):
    lane = lax.broadcasted_iota(jnp.int32, pair.shape, 1)
    mine = lane < HEAD_DIM if hh == 0 else lane >= HEAD_DIM
    return jnp.where(mine, pair, jnp.zeros_like(pair))


def put_slices(out_ref, forward, backward):
    n = out_ref.shape[0]
    size = WIDTH // n
    for i in range(n):
        at = slice(i * size, (i + 1) * size)
        out_ref[i, 0:size, :] = forward[at, :]
        out_ref[i, size : 2 * size, :] = backward[at, :]


def take_slices(ref):
    n = ref.shape[0]
    size = WIDTH // n
    forward = jnp.concatenate([ref[i, 0:size, :] for i in range(n)], axis=0)
    backward = jnp.concatenate([ref[i, size : 2 * size, :] for i in range(n)], axis=0)
    return forward, backward


def local_states(x_hbm, b_hbm, df_hbm, db_hbm, out_ref, x_ref, b_ref, df_ref, db_ref, sems):
    sources, targets = (x_hbm, b_hbm, df_hbm, db_hbm), (x_ref, b_ref, df_ref, db_ref)
    copies = [pltpu.make_async_copy(s, t, sems.at[i]) for i, (s, t) in enumerate(zip(sources, targets))]
    for copy in copies:
        copy.start()
    for copy in copies:
        copy.wait()
    cf, be, end_f, end_b = columns(df_ref[...], db_ref[...])
    x = x_ref[...].astype(F32)
    b = b_ref[...]
    state_f = dot_left(x * spread(jnp.exp(end_f - cf)), b, 0, 0)
    state_b = dot_left(x * spread(jnp.exp(be)), b, 0, 0)
    put_slices(out_ref, state_f, state_b)
    n = out_ref.shape[0]
    size = WIDTH // n
    total_f, total_b = jnp.exp(end_f), jnp.exp(end_b)
    half = lax.broadcasted_iota(jnp.int32, (8, LANES), 0) < 4
    for j in range(HEADS):
        both = jnp.where(half, total_f[:, j : j + 1], total_b[:, j : j + 1])
        for i in range(j * n // HEADS, (j + 1) * n // HEADS):
            out_ref[i, 2 * size :, :] = both


def totals_at(ref, i, start):
    return ref[i, start : start + 1, :], ref[i, start + 4 : start + 5, :]


def sliced(ref, i, size):
    return ref[i, 0:size, :], ref[i, size : 2 * size, :]


def group_sums(dec_ref, rec_ref, forward_up):
    n = rec_ref.shape[0]
    size = WIDTH // n
    decays = [totals_at(dec_ref, i, 2 * size) for i in range(n)]
    parts = [sliced(rec_ref, i, size) for i in range(n)]
    sums = []
    for branch, up in enumerate((forward_up, not forward_up)):
        order = list(range(n)) if up else list(range(n))[::-1]
        acc = parts[order[0]][branch]
        for i in order[1:]:
            acc = decays[i][branch] * acc + parts[i][branch]
        sums.append(acc)
    return sums, decays


def totals_up(place_ref, rec_ref, out_ref):
    size = WIDTH // rec_ref.shape[0]
    (sum_f, sum_b), decays = group_sums(rec_ref, rec_ref, True)
    all_f, all_b = decays[0]
    for dec_f, dec_b in decays[1:]:
        all_f, all_b = all_f * dec_f, all_b * dec_b
    half = lax.broadcasted_iota(jnp.int32, (8, LANES), 0) < 4
    for k in range(out_ref.shape[0]):
        out_ref[k, 0:size, :] = jnp.where(place_ref[0] < k, sum_f, sum_b)
        out_ref[k, size:, :] = jnp.where(half, all_f, all_b)


def entries_up(place_ref, zrec_ref, rec_ref, out_ref):
    n_g, n = zrec_ref.shape[0], rec_ref.shape[0]
    size = WIDTH // n
    place = place_ref[0]
    for branch, up in enumerate((True, False)):
        entry = jnp.zeros((size, LANES), F32)
        for k in list(range(n_g)) if up else list(range(n_g))[::-1]:
            passed = place > k if up else place < k
            after = totals_at(zrec_ref, k, size)[branch] * entry + zrec_ref[k, 0:size, :]
            entry = jnp.where(passed, after, entry)
        put_entries(out_ref, branch, up, entry, rec_ref, rec_ref)


def put_entries(out_ref, branch, up, entry, dec_ref, rec_ref):
    n = rec_ref.shape[0]
    size = WIDTH // n
    for i in list(range(n)) if up else list(range(n))[::-1]:
        out_ref[i, branch * size : (branch + 1) * size, :] = entry
        entry = totals_at(dec_ref, i, 2 * size)[branch] * entry + sliced(rec_ref, i, size)[branch]


def totals_down(dec_ref, rec_ref, out_ref):
    n, n_g = rec_ref.shape[0], out_ref.shape[0]
    size = WIDTH // n
    sums, _ = group_sums(dec_ref, rec_ref, False)
    both = jnp.concatenate(sums, axis=0)
    weight = rec_ref[0, 2 * size :, :]
    for i in range(1, n):
        weight = weight + rec_ref[i, 2 * size :, :]
    span, part = 2 * size // n_g, weight.shape[0] // n_g
    for k in range(n_g):
        out_ref[k, 0:span, :] = both[k * span : (k + 1) * span, :]
        out_ref[k, span:, :] = weight[k * part : (k + 1) * part, :]


def scan_down(place_ref, dec_ref, rec_ref, out_ref):
    n_g = rec_ref.shape[0]
    span = 2 * (dec_ref.shape[1] - 8) // n_g
    forward = 2 * place_ref[0] < n_g
    states = [rec_ref[k, 0:span, :] for k in range(n_g)]
    decays = [totals_at(dec_ref, k, dec_ref.shape[1] - 8) for k in range(n_g)]
    down, acc = [None] * n_g, jnp.zeros_like(states[0])
    for k in range(n_g)[::-1]:
        down[k] = acc
        acc = decays[k][0] * acc + states[k]
    up, acc = [None] * n_g, jnp.zeros_like(states[0])
    for k in range(n_g):
        up[k] = acc
        acc = decays[k][1] * acc + states[k]
    weight = rec_ref[0, span:, :]
    for k in range(1, n_g):
        weight = weight + rec_ref[k, span:, :]
    for k in range(n_g):
        out_ref[k, 0:span, :] = jnp.where(forward, down[k], up[k])
        out_ref[k, span:, :] = weight


def entries_down(back_ref, dec_ref, rec_ref, out_ref):
    n_g, n = back_ref.shape[0], rec_ref.shape[0]
    size = WIDTH // n
    span = 2 * size // n_g
    half = n_g // 2
    entry_f = jnp.concatenate([back_ref[k, 0:span, :] for k in range(half)], axis=0)
    entry_b = jnp.concatenate([back_ref[k, 0:span, :] for k in range(half, n_g)], axis=0)
    put_entries(out_ref, 0, False, entry_f, dec_ref, rec_ref)
    put_entries(out_ref, 1, True, entry_b, dec_ref, rec_ref)
    part = back_ref.shape[1] - span
    for k in range(n_g):
        weight = back_ref[k, span:, :]
        for i in range(n):
            out_ref[i, 2 * size + k * part : 2 * size + (k + 1) * part, :] = weight


def weight_rows(rec_ref, gw_ref):
    n = rec_ref.shape[0]
    size = WIDTH // n
    for i in range(n):
        for block in range(gw_ref.shape[1] // LANES):
            at = 2 * size + block * size
            gw_ref[i * size : (i + 1) * size, block * LANES : (block + 1) * LANES] = (
                rec_ref[i, at : at + size, :] * WEIGHT_SCALE
            )


def across_rows(cols):
    lane = lax.broadcasted_iota(jnp.int32, (LANES, LANES), 1)
    grid = jnp.zeros((LANES, LANES), F32)
    for i, col in enumerate(cols):
        for part in range(FRAMES // LANES):
            at = i * (FRAMES // LANES) + part
            grid = jnp.where(lane == at, col[part * LANES : (part + 1) * LANES, :], grid)
    return jnp.transpose(grid)[0:8, :]


def near_outputs(
    skip_ref, x_ref, b_ref, c_ref, df_ref, db_ref, gain_ref, w_ref, do_ref, y_ref, m_ref
):
    df, db = df_ref[...], db_ref[...]
    cf, be, end_f, end_b = columns(df, db)
    cf_row, be_row = rows(df, db)
    row, col = places()
    scores = dot(c_ref[...], b_ref[...], 1, 1)
    lane = lax.broadcasted_iota(jnp.int32, (1, LANES), 1)
    for g in range(HEADS // 2):
        at = slice(g * LANES, (g + 1) * LANES)
        pair = x_ref[:, at]
        acc = jnp.where(lane < HEAD_DIM, skip_ref[2 * g], skip_ref[2 * g + 1]) * pair.astype(F32)
        for hh in range(2):
            weights = scores * pair_decay(2 * g + hh, cf, be, cf_row, be_row, row, col)
            acc = acc + dot_left(weights, own_lanes(pair, hh), 1, 0)
        y_ref[:, at] = acc
    m_ref[...] = dot(do_ref[...], w_ref[...], 1, 1) * gain_ref[...]


def outputs(near_ref, m_ref, z_ref, c_ref, df_ref, db_ref, ent_ref, y_ref, sums_ref):
    cf, be, end_f, end_b = columns(df_ref[...], db_ref[...])
    c = c_ref[...]
    entry_f, entry_b = take_slices(ent_ref)
    y = near_ref[...] + spread(jnp.exp(cf)) * dot_right(c, entry_f, 1, 1)
    y = y + spread(jnp.exp(end_b - be)) * dot_right(c, entry_b, 1, 1)
    y_ref[...] = y
    z, m = z_ref[...].astype(F32), m_ref[...]
    u = y * z * jax.nn.sigmoid(z)
    sums = across_rows([jnp.sum(u * u, axis=1, keepdims=True), jnp.sum(u * m, axis=1, keepdims=True)])
    for i in range(sums_ref.shape[0]):
        sums_ref[i, :, :] = sums


def gradients(
    sums_ref, y_ref, m_ref, z_ref, c_ref, df_ref, db_ref, gain_ref, do_ref,
    dy_ref, gz_ref, out_ref, *, inner,
):
    total = sums_ref[0, :, :]
    for i in range(1, sums_ref.shape[0]):
        total = total + sums_ref[i, :, :]
    grid = jnp.transpose(jnp.concatenate([total, jnp.zeros((LANES - 8, LANES), F32)], axis=0))
    square = jnp.concatenate([grid[:, 0:1], grid[:, 1:2]], axis=0) / inner
    cross = jnp.concatenate([grid[:, 2:3], grid[:, 3:4]], axis=0) / inner
    q = lax.rsqrt(square + EPS_NORM)
    y, m, z = y_ref[...], m_ref[...], z_ref[...].astype(F32)
    sig = jax.nn.sigmoid(z)
    silu = z * sig
    u = y * z * sig
    normed = (u * q * gain_ref[...]).astype(BF16)
    du = q * m - u * (q * q * q * cross)
    dy = du * silu
    gz_ref[...] = (du * y * sig * (1.0 + z * (1.0 - sig))).astype(BF16)
    dy_ref[...] = dy
    cf, be, end_f, end_b = columns(df_ref[...], db_ref[...])
    c = c_ref[...]
    back_f = dot_left(dy * spread(jnp.exp(cf)), c, 0, 0)
    back_b = dot_left(dy * spread(jnp.exp(end_b - be)), c, 0, 0)
    put_slices(out_ref, back_f, back_b)
    weight = dot(normed, do_ref[...], 0, 0)
    n = out_ref.shape[0]
    size = WIDTH // n
    for i in range(n):
        for block in range(weight.shape[1] // LANES):
            at = 2 * size + block * size
            out_ref[i, at : at + size, :] = weight[
                i * size : (i + 1) * size, block * LANES : (block + 1) * LANES
            ]


def near_gradients(
    skip_ref, x_ref, b_ref, c_ref, df_ref, db_ref, dy_ref, ent_ref, gx_ref, gb_ref, gc_ref
):
    df, db = df_ref[...], db_ref[...]
    cf, be, end_f, end_b = columns(df, db)
    cf_row, be_row = rows(df, db)
    row, col = places()
    b, c, dy = b_ref[...], c_ref[...], dy_ref[...]
    scores = dot(c, b, 1, 1)
    pair_sum = jnp.zeros((FRAMES, FRAMES), F32)
    lane = lax.broadcasted_iota(jnp.int32, (1, LANES), 1)
    for g in range(HEADS // 2):
        at = slice(g * LANES, (g + 1) * LANES)
        acc = jnp.where(lane < HEAD_DIM, skip_ref[2 * g], skip_ref[2 * g + 1]) * dy[:, at]
        for hh in range(2):
            decay = pair_decay(2 * g + hh, cf, be, cf_row, be_row, row, col)
            dy_own = own_lanes(dy[:, at], hh)
            pair_sum = pair_sum + decay * dot_left(dy_own, x_ref[:, at], 1, 1)
            acc = acc + dot_both(scores * decay, dy_own, 0, 0)
        gx_ref[:, at] = acc
    entry_f, entry_b = take_slices(ent_ref)
    rise_f, rise_b = spread(jnp.exp(cf)), spread(jnp.exp(end_b - be))
    grad_c = dot_left(pair_sum, b, 1, 0)
    gc_ref[...] = grad_c + dot_both(dy * rise_f, entry_f, 1, 0) + dot_both(dy * rise_b, entry_b, 1, 0)
    gb_ref[...] = dot_left(pair_sum, c, 0, 0)


def finish(x_ref, b_ref, df_ref, db_ref, exit_ref, gx_near, gb_near, gc_near, gx_ref, out_ref):
    cf, be, end_f, end_b = columns(df_ref[...], db_ref[...])
    b, x = b_ref[...], x_ref[...].astype(F32)
    tail_f, lead_b = spread(jnp.exp(end_f - cf)), spread(jnp.exp(be))
    exit_f, exit_b = take_slices(exit_ref)
    gx = gx_near[...] + tail_f * dot_right(b, exit_f, 1, 1) + lead_b * dot_right(b, exit_b, 1, 1)
    gx_ref[...] = gx.astype(BF16)
    grad_b = gb_near[...] + dot_both(x * tail_f, exit_f, 1, 0) + dot_both(x * lead_b, exit_b, 1, 0)
    grad_c = gc_near[...]
    n = out_ref.shape[0]
    size = FRAMES // n
    for i in range(n):
        out_ref[i, 0:size, :] = grad_b[i * size : (i + 1) * size, :]
        out_ref[i, size : 2 * size, :] = grad_c[i * size : (i + 1) * size, :]


def add_up(rec_ref, out_ref):
    n = rec_ref.shape[0]
    total = rec_ref[0, :, :]
    for i in range(1, n):
        total = total + rec_ref[i, :, :]
    for i in range(n):
        out_ref[i, :, :] = total


def deal_out(rec_ref, gb_ref, gc_ref):
    n = rec_ref.shape[0]
    size = FRAMES // n
    for i in range(n):
        gb_ref[i * size : (i + 1) * size, :] = rec_ref[i, 0:size, :]
        gc_ref[i * size : (i + 1) * size, :] = rec_ref[i, size : 2 * size, :]


VMEM = pl.BlockSpec(memory_space=pltpu.VMEM)
SMEM = pl.BlockSpec(memory_space=pltpu.SMEM)
HBM = pl.BlockSpec(memory_space=pltpu.MemorySpace.HBM)


def call(kernel, name, out, *args, scalars=0, own=()):
    shapes = [jax.ShapeDtypeStruct(shape, dtype) for shape, dtype in out]
    single = len(shapes) == 1
    return pl.pallas_call(
        kernel,
        name=name,
        out_shape=shapes[0] if single else tuple(shapes),
        in_specs=[SMEM] * scalars + [HBM if own else VMEM] * (len(args) - scalars),
        out_specs=VMEM if single else tuple(VMEM for _ in shapes),
        scratch_shapes=list(own),
        compiler_params=pltpu.CompilerParams(vmem_limit_bytes=48 * 1024 * 1024),
    )(*args)


def exchange(a, axis):
    return lax.all_to_all(a, axis, 0, 0, tiled=True)


def body(x_in, gate_in, b_in, c_in, decay_fwd, decay_bwd, skip_gain, norm_gain, w_out, d_out):
    n_hi, n_lo, n_x, n_h = (lax.axis_size(axis) for axis in ("z_hi", "z_lo", "x", "head"))
    group = ("z_lo", "x")
    n = n_lo * n_x
    model = d_out.shape[1]
    gain = norm_gain.reshape(1, WIDTH)
    size = WIDTH // n
    weights = size * model // LANES
    place = lax.axis_index("z_hi").astype(jnp.int32).reshape(1)
    decays = (decay_fwd, decay_bwd)
    square = (FRAMES, WIDTH)

    firsts = (x_in, b_in, *decays)
    own = [pltpu.VMEM(a.shape, a.dtype) for a in firsts] + [pltpu.SemaphoreType.DMA((4,))]
    sent = call(local_states, "local_states", [((n, 2 * size + 8, LANES), F32)], *firsts, own=own)
    rec1 = exchange(sent, group)
    near, m = call(
        near_outputs, "near_outputs", [(square, F32)] * 2,
        skip_gain, x_in, b_in, c_in, *decays, gain, w_out, d_out, scalars=1,
    )
    sent = call(totals_up, "totals_up", [((n_hi, size + 8, LANES), F32)], place, rec1, scalars=1)
    recz1 = exchange(sent, "z_hi")
    sent = call(entries_up, "entries_up", [((n, 2 * size, LANES), F32)], place, recz1, rec1, scalars=1)
    entries = exchange(sent, group)

    y, sums = call(
        outputs, "outputs", [(square, F32), ((n_h, 8, LANES), F32)],
        near, m, gate_in, c_in, *decays, entries,
    )
    sums = exchange(sums, "head")
    dy, grad_z, sent = call(
        functools.partial(gradients, inner=WIDTH * n_h), "gradients",
        [(square, F32), (square, BF16), ((n, 2 * size + weights, LANES), F32)],
        sums, y, m, gate_in, c_in, *decays, gain, d_out,
    )

    rec2 = exchange(sent, group)
    gx_near, gb_near, gc_near = call(
        near_gradients, "near_gradients", [(square, F32)] + [((FRAMES, STATE), F32)] * 2,
        skip_gain, x_in, b_in, c_in, *decays, dy, entries, scalars=1,
    )
    rows_z = (2 * size + weights) // n_hi
    sent = call(totals_down, "totals_down", [((n_hi, rows_z, LANES), F32)], rec1, rec2)
    recz2 = exchange(sent, "z_hi")
    sent = call(scan_down, "scan_down", [((n_hi, rows_z, LANES), F32)], place, recz1, recz2, scalars=1)
    back = exchange(sent, "z_hi")
    sent = call(entries_down, "entries_down", [((n, 2 * size + weights, LANES), F32)], back, rec1, rec2)
    exits = exchange(sent, group)
    grad_w = call(weight_rows, "weight_rows", [((WIDTH, model), F32)], exits)

    chunk = 2 * FRAMES // n_h
    grad_x, sent = call(
        finish, "finish", [(square, BF16), ((n_h, chunk, LANES), F32)],
        x_in, b_in, *decays, exits, gx_near, gb_near, gc_near,
    )
    rec = exchange(sent, "head")
    sent = call(add_up, "add_up", [((n_h, chunk, LANES), F32)], rec)
    rec = exchange(sent, "head")
    grad_b, grad_c = call(deal_out, "deal_out", [((FRAMES, STATE), F32)] * 2, rec)
    return grad_x, grad_z, grad_b, grad_c, grad_w


def solution(mesh):
    n_seq, n_head = mesh.devices.shape
    n_z = n_seq // HEADS
    n_lo = min(2, n_z // 2)
    split = Mesh(mesh.devices.reshape(n_z // n_lo, n_lo, HEADS, n_head), ("z_hi", "z_lo", "x", "head"))
    seq = ("z_hi", "z_lo", "x")
    in_specs = (
        P(seq, "head"),
        P(seq, "head"),
        P(seq, None),
        P(seq, None),
        P("head", seq),
        P("head", seq),
        P("head"),
        P("head"),
        P("head", None),
        P(seq, None),
    )
    out_specs = (
        P(seq, "head"),
        P(seq, "head"),
        P(seq, None),
        P(seq, None),
        P("head", None),
    )
    return jax.shard_map(body, mesh=split, in_specs=in_specs, out_specs=out_specs, check_vma=False)
```

```python
import functools

import jax
import jax.numpy as jnp
from jax import lax
from jax.experimental import pallas as pl
from jax.experimental.pallas import tpu as pltpu
from jax.sharding import Mesh, PartitionSpec as P

HEADS = 4
HEAD_DIM = 64
STATE = 128
FRAMES = 256
WIDTH = HEADS * HEAD_DIM
LANES = 128
EPS_NORM = 1e-05
WEIGHT_SCALE = 0.0078125
F32, BF16 = jnp.float32, jnp.bfloat16


def dot(a, b, ca, cb):
    return lax.dot_general(a, b, (((ca,), (cb,)), ((), ())), preferred_element_type=F32)


def halves(a):
    high = a.astype(BF16)
    return high, (a - high.astype(F32)).astype(BF16)


def dot_left(a, b, ca, cb):
    ah, al = halves(a)
    return dot(ah, b, ca, cb) + dot(al, b, ca, cb)


def dot_right(a, b, ca, cb):
    bh, bl = halves(b)
    return dot(a, bh, ca, cb) + dot(a, bl, ca, cb)


def dot_both(a, b, ca, cb):
    ah, al = halves(a)
    bh, bl = halves(b)
    return dot(ah, bh, ca, cb) + (dot(ah, bl, ca, cb) + dot(al, bh, ca, cb))


def dot_exact(a, b, ca, cb):
    return lax.dot_general(
        a, b, (((ca,), (cb,)), ((), ())), precision=lax.Precision.HIGHEST, preferred_element_type=F32
    )


def places():
    row = lax.broadcasted_iota(jnp.int32, (FRAMES, FRAMES), 0)
    col = lax.broadcasted_iota(jnp.int32, (FRAMES, FRAMES), 1)
    return row, col


def columns(df, db):
    row, col = places()
    upto = (col <= row).astype(F32)
    before = (col < row).astype(F32)
    cf = dot_exact(upto, df, 1, 1)
    be = dot_exact(before, db, 1, 1)
    end_f = cf[FRAMES - 1 :, :]
    end_b = dot_exact(jnp.ones((8, FRAMES), F32), db, 1, 1)[:1, :]
    return cf, be, end_f, end_b


def rows(df, db):
    row, col = places()
    upto = (row <= col).astype(F32)
    before = (row < col).astype(F32)
    return dot_exact(df, upto, 1, 0), dot_exact(db, before, 1, 0)


def spread(cols):
    lane = lax.broadcasted_iota(jnp.int32, (cols.shape[0], LANES), 1)
    pairs = [
        jnp.where(lane < HEAD_DIM, cols[:, 2 * g : 2 * g + 1], cols[:, 2 * g + 1 : 2 * g + 2])
        for g in range(HEADS // 2)
    ]
    return jnp.concatenate(pairs, axis=1)


def pair_decay(h, cf, be, cf_row, be_row, row, col):
    gap = jnp.where(
        row > col,
        cf[:, h : h + 1] - cf_row[h : h + 1, :],
        be_row[h : h + 1, :] - be[:, h : h + 1],
    )
    return jnp.where(row == col, 2.0, jnp.exp(jnp.minimum(gap, 0.0)))


def own_lanes(pair, hh):
    lane = lax.broadcasted_iota(jnp.int32, pair.shape, 1)
    mine = lane < HEAD_DIM if hh == 0 else lane >= HEAD_DIM
    return jnp.where(mine, pair, jnp.zeros_like(pair))


def put_slices(out_ref, forward, backward):
    n = out_ref.shape[0]
    size = WIDTH // n
    for i in range(n):
        at = slice(i * size, (i + 1) * size)
        out_ref[i, 0:size, :] = forward[at, :]
        out_ref[i, size : 2 * size, :] = backward[at, :]


def take_slices(ref):
    n = ref.shape[0]
    size = WIDTH // n
    forward = jnp.concatenate([ref[i, 0:size, :] for i in range(n)], axis=0)
    backward = jnp.concatenate([ref[i, size : 2 * size, :] for i in range(n)], axis=0)
    return forward, backward


def local_states(x_hbm, b_hbm, df_hbm, db_hbm, out_ref, x_ref, b_ref, df_ref, db_ref, sems):
    sources, targets = (x_hbm, b_hbm, df_hbm, db_hbm), (x_ref, b_ref, df_ref, db_ref)
    copies = [pltpu.make_async_copy(s, t, sems.at[i]) for i, (s, t) in enumerate(zip(sources, targets))]
    for copy in copies:
        copy.start()
    for copy in copies:
        copy.wait()
    cf, be, end_f, end_b = columns(df_ref[...], db_ref[...])
    x = x_ref[...].astype(F32)
    b = b_ref[...]
    state_f = dot_left(x * spread(jnp.exp(end_f - cf)), b, 0, 0)
    state_b = dot_left(x * spread(jnp.exp(be)), b, 0, 0)
    put_slices(out_ref, state_f, state_b)
    n = out_ref.shape[0]
    size = WIDTH // n
    total_f, total_b = jnp.exp(end_f), jnp.exp(end_b)
    half = lax.broadcasted_iota(jnp.int32, (8, LANES), 0) < 4
    for j in range(HEADS):
        both = jnp.where(half, total_f[:, j : j + 1], total_b[:, j : j + 1])
        for i in range(j * n // HEADS, (j + 1) * n // HEADS):
            out_ref[i, 2 * size :, :] = both


def totals_at(ref, i, start):
    return ref[i, start : start + 1, :], ref[i, start + 4 : start + 5, :]


def sliced(ref, i, size):
    return ref[i, 0:size, :], ref[i, size : 2 * size, :]


def group_sums(dec_ref, rec_ref, forward_up):
    n = rec_ref.shape[0]
    size = WIDTH // n
    decays = [totals_at(dec_ref, i, 2 * size) for i in range(n)]
    parts = [sliced(rec_ref, i, size) for i in range(n)]
    sums = []
    for branch, up in enumerate((forward_up, not forward_up)):
        order = list(range(n)) if up else list(range(n))[::-1]
        acc = parts[order[0]][branch]
        for i in order[1:]:
            acc = decays[i][branch] * acc + parts[i][branch]
        sums.append(acc)
    return sums, decays


def totals_up(place_ref, rec_ref, out_ref):
    size = WIDTH // rec_ref.shape[0]
    (sum_f, sum_b), decays = group_sums(rec_ref, rec_ref, True)
    all_f, all_b = decays[0]
    for dec_f, dec_b in decays[1:]:
        all_f, all_b = all_f * dec_f, all_b * dec_b
    half = lax.broadcasted_iota(jnp.int32, (8, LANES), 0) < 4
    for k in range(out_ref.shape[0]):
        out_ref[k, 0:size, :] = jnp.where(place_ref[0] < k, sum_f, sum_b)
        out_ref[k, size:, :] = jnp.where(half, all_f, all_b)


def entries_up(place_ref, zrec_ref, rec_ref, out_ref):
    n_g, n = zrec_ref.shape[0], rec_ref.shape[0]
    size = WIDTH // n
    place = place_ref[0]
    for branch, up in enumerate((True, False)):
        entry = jnp.zeros((size, LANES), F32)
        for k in list(range(n_g)) if up else list(range(n_g))[::-1]:
            passed = place > k if up else place < k
            after = totals_at(zrec_ref, k, size)[branch] * entry + zrec_ref[k, 0:size, :]
            entry = jnp.where(passed, after, entry)
        put_entries(out_ref, branch, up, entry, rec_ref, rec_ref)


def put_entries(out_ref, branch, up, entry, dec_ref, rec_ref):
    n = rec_ref.shape[0]
    size = WIDTH // n
    for i in list(range(n)) if up else list(range(n))[::-1]:
        out_ref[i, branch * size : (branch + 1) * size, :] = entry
        entry = totals_at(dec_ref, i, 2 * size)[branch] * entry + sliced(rec_ref, i, size)[branch]


def totals_down(dec_ref, rec_ref, out_ref):
    n, n_g = rec_ref.shape[0], out_ref.shape[0]
    size = WIDTH // n
    sums, _ = group_sums(dec_ref, rec_ref, False)
    both = jnp.concatenate(sums, axis=0)
    weight = rec_ref[0, 2 * size :, :]
    for i in range(1, n):
        weight = weight + rec_ref[i, 2 * size :, :]
    span, part = 2 * size // n_g, weight.shape[0] // n_g
    for k in range(n_g):
        out_ref[k, 0:span, :] = both[k * span : (k + 1) * span, :]
        out_ref[k, span:, :] = weight[k * part : (k + 1) * part, :]


def scan_down(place_ref, dec_ref, rec_ref, out_ref):
    n_g = rec_ref.shape[0]
    span = 2 * (dec_ref.shape[1] - 8) // n_g
    forward = 2 * place_ref[0] < n_g
    states = [rec_ref[k, 0:span, :] for k in range(n_g)]
    decays = [totals_at(dec_ref, k, dec_ref.shape[1] - 8) for k in range(n_g)]
    down, acc = [None] * n_g, jnp.zeros_like(states[0])
    for k in range(n_g)[::-1]:
        down[k] = acc
        acc = decays[k][0] * acc + states[k]
    up, acc = [None] * n_g, jnp.zeros_like(states[0])
    for k in range(n_g):
        up[k] = acc
        acc = decays[k][1] * acc + states[k]
    weight = rec_ref[0, span:, :]
    for k in range(1, n_g):
        weight = weight + rec_ref[k, span:, :]
    for k in range(n_g):
        out_ref[k, 0:span, :] = jnp.where(forward, down[k], up[k])
        out_ref[k, span:, :] = weight


def entries_down(back_ref, dec_ref, rec_ref, out_ref):
    n_g, n = back_ref.shape[0], rec_ref.shape[0]
    size = WIDTH // n
    span = 2 * size // n_g
    half = n_g // 2
    entry_f = jnp.concatenate([back_ref[k, 0:span, :] for k in range(half)], axis=0)
    entry_b = jnp.concatenate([back_ref[k, 0:span, :] for k in range(half, n_g)], axis=0)
    put_entries(out_ref, 0, False, entry_f, dec_ref, rec_ref)
    put_entries(out_ref, 1, True, entry_b, dec_ref, rec_ref)
    part = back_ref.shape[1] - span
    for k in range(n_g):
        weight = back_ref[k, span:, :]
        for i in range(n):
            out_ref[i, 2 * size + k * part : 2 * size + (k + 1) * part, :] = weight


def weight_rows(rec_ref, gw_ref):
    n = rec_ref.shape[0]
    size = WIDTH // n
    for i in range(n):
        for block in range(gw_ref.shape[1] // LANES):
            at = 2 * size + block * size
            gw_ref[i * size : (i + 1) * size, block * LANES : (block + 1) * LANES] = (
                rec_ref[i, at : at + size, :] * WEIGHT_SCALE
            )


def across_rows(cols):
    lane = lax.broadcasted_iota(jnp.int32, (LANES, LANES), 1)
    grid = jnp.zeros((LANES, LANES), F32)
    for i, col in enumerate(cols):
        for part in range(FRAMES // LANES):
            at = i * (FRAMES // LANES) + part
            grid = jnp.where(lane == at, col[part * LANES : (part + 1) * LANES, :], grid)
    return jnp.transpose(grid)[0:8, :]


def near_outputs(
    skip_ref, x_ref, b_ref, c_ref, df_ref, db_ref, gain_ref, w_ref, do_ref, y_ref, m_ref
):
    df, db = df_ref[...], db_ref[...]
    cf, be, end_f, end_b = columns(df, db)
    cf_row, be_row = rows(df, db)
    row, col = places()
    scores = dot(c_ref[...], b_ref[...], 1, 1)
    lane = lax.broadcasted_iota(jnp.int32, (1, LANES), 1)
    for g in range(HEADS // 2):
        at = slice(g * LANES, (g + 1) * LANES)
        pair = x_ref[:, at]
        acc = jnp.where(lane < HEAD_DIM, skip_ref[2 * g], skip_ref[2 * g + 1]) * pair.astype(F32)
        for hh in range(2):
            weights = scores * pair_decay(2 * g + hh, cf, be, cf_row, be_row, row, col)
            acc = acc + dot_left(weights, own_lanes(pair, hh), 1, 0)
        y_ref[:, at] = acc
    m_ref[...] = dot(do_ref[...], w_ref[...], 1, 1) * gain_ref[...]


def outputs(near_ref, m_ref, z_ref, c_ref, df_ref, db_ref, ent_ref, y_ref, sums_ref):
    cf, be, end_f, end_b = columns(df_ref[...], db_ref[...])
    c = c_ref[...]
    entry_f, entry_b = take_slices(ent_ref)
    y = near_ref[...] + spread(jnp.exp(cf)) * dot_right(c, entry_f, 1, 1)
    y = y + spread(jnp.exp(end_b - be)) * dot_right(c, entry_b, 1, 1)
    y_ref[...] = y
    z, m = z_ref[...].astype(F32), m_ref[...]
    u = y * z * jax.nn.sigmoid(z)
    sums = across_rows([jnp.sum(u * u, axis=1, keepdims=True), jnp.sum(u * m, axis=1, keepdims=True)])
    for i in range(sums_ref.shape[0]):
        sums_ref[i, :, :] = sums


def gradients(
    sums_ref, y_ref, m_ref, z_ref, c_ref, df_ref, db_ref, gain_ref, do_ref,
    dy_ref, du_ref, out_ref, *, inner,
):
    total = sums_ref[0, :, :]
    for i in range(1, sums_ref.shape[0]):
        total = total + sums_ref[i, :, :]
    grid = jnp.transpose(jnp.concatenate([total, jnp.zeros((LANES - 8, LANES), F32)], axis=0))
    square = jnp.concatenate([grid[:, 0:1], grid[:, 1:2]], axis=0) / inner
    cross = jnp.concatenate([grid[:, 2:3], grid[:, 3:4]], axis=0) / inner
    q = lax.rsqrt(square + EPS_NORM)
    y, m, z = y_ref[...], m_ref[...], z_ref[...].astype(F32)
    sig = jax.nn.sigmoid(z)
    silu = z * sig
    u = y * z * sig
    normed = (u * q * gain_ref[...]).astype(BF16)
    du = q * m - u * (q * q * q * cross)
    dy = du * silu
    dy_ref[...] = dy
    du_ref[...] = du
    cf, be, end_f, end_b = columns(df_ref[...], db_ref[...])
    c = c_ref[...]
    back_f = dot_left(dy * spread(jnp.exp(cf)), c, 0, 0)
    back_b = dot_left(dy * spread(jnp.exp(end_b - be)), c, 0, 0)
    put_slices(out_ref, back_f, back_b)
    weight = dot(normed, do_ref[...], 0, 0)
    n = out_ref.shape[0]
    size = WIDTH // n
    for i in range(n):
        for block in range(weight.shape[1] // LANES):
            at = 2 * size + block * size
            out_ref[i, at : at + size, :] = weight[
                i * size : (i + 1) * size, block * LANES : (block + 1) * LANES
            ]


def near_gradients(
    skip_ref, x_ref, b_ref, c_ref, df_ref, db_ref, dy_ref, ent_ref, gx_ref, gb_ref, gc_ref
):
    df, db = df_ref[...], db_ref[...]
    cf, be, end_f, end_b = columns(df, db)
    cf_row, be_row = rows(df, db)
    row, col = places()
    b, c, dy = b_ref[...], c_ref[...], dy_ref[...]
    scores = dot(c, b, 1, 1)
    pair_sum = jnp.zeros((FRAMES, FRAMES), F32)
    lane = lax.broadcasted_iota(jnp.int32, (1, LANES), 1)
    for g in range(HEADS // 2):
        at = slice(g * LANES, (g + 1) * LANES)
        acc = jnp.where(lane < HEAD_DIM, skip_ref[2 * g], skip_ref[2 * g + 1]) * dy[:, at]
        for hh in range(2):
            decay = pair_decay(2 * g + hh, cf, be, cf_row, be_row, row, col)
            dy_own = own_lanes(dy[:, at], hh)
            pair_sum = pair_sum + decay * dot_left(dy_own, x_ref[:, at], 1, 1)
            acc = acc + dot_both(scores * decay, dy_own, 0, 0)
        gx_ref[:, at] = acc
    entry_f, entry_b = take_slices(ent_ref)
    rise_f, rise_b = spread(jnp.exp(cf)), spread(jnp.exp(end_b - be))
    grad_c = dot_left(pair_sum, b, 1, 0)
    gc_ref[...] = grad_c + dot_both(dy * rise_f, entry_f, 1, 0) + dot_both(dy * rise_b, entry_b, 1, 0)
    gb_ref[...] = dot_left(pair_sum, c, 0, 0)


def gate_gradient(du_ref, y_ref, z_ref, gz_ref):
    z = z_ref[...].astype(F32)
    sig = jax.nn.sigmoid(z)
    gz_ref[...] = (du_ref[...] * y_ref[...] * sig * (1.0 + z * (1.0 - sig))).astype(BF16)


def finish(x_ref, df_ref, db_ref, exit_ref, gb_near, gc_near, out_ref):
    cf, be, end_f, end_b = columns(df_ref[...], db_ref[...])
    x = x_ref[...].astype(F32)
    exit_f, exit_b = take_slices(exit_ref)
    grad_b = gb_near[...] + dot_both(x * spread(jnp.exp(end_f - cf)), exit_f, 1, 0)
    grad_b = grad_b + dot_both(x * spread(jnp.exp(be)), exit_b, 1, 0)
    grad_c = gc_near[...]
    n = out_ref.shape[0]
    size = FRAMES // n
    for i in range(n):
        out_ref[i, 0:size, :] = grad_b[i * size : (i + 1) * size, :]
        out_ref[i, size : 2 * size, :] = grad_c[i * size : (i + 1) * size, :]


def finish_x(b_ref, df_ref, db_ref, exit_ref, gx_near, gx_ref):
    cf, be, end_f, end_b = columns(df_ref[...], db_ref[...])
    b = b_ref[...]
    exit_f, exit_b = take_slices(exit_ref)
    gx = gx_near[...] + spread(jnp.exp(end_f - cf)) * dot_right(b, exit_f, 1, 1)
    gx_ref[...] = (gx + spread(jnp.exp(be)) * dot_right(b, exit_b, 1, 1)).astype(BF16)


def add_up(rec_ref, out_ref):
    n = rec_ref.shape[0]
    total = rec_ref[0, :, :]
    for i in range(1, n):
        total = total + rec_ref[i, :, :]
    for i in range(n):
        out_ref[i, :, :] = total


def deal_out(rec_ref, gb_ref, gc_ref):
    n = rec_ref.shape[0]
    size = FRAMES // n
    for i in range(n):
        gb_ref[i * size : (i + 1) * size, :] = rec_ref[i, 0:size, :]
        gc_ref[i * size : (i + 1) * size, :] = rec_ref[i, size : 2 * size, :]


VMEM = pl.BlockSpec(memory_space=pltpu.VMEM)
SMEM = pl.BlockSpec(memory_space=pltpu.SMEM)
HBM = pl.BlockSpec(memory_space=pltpu.MemorySpace.HBM)


def call(kernel, name, out, *args, scalars=0, own=()):
    shapes = [jax.ShapeDtypeStruct(shape, dtype) for shape, dtype in out]
    single = len(shapes) == 1
    return pl.pallas_call(
        kernel,
        name=name,
        out_shape=shapes[0] if single else tuple(shapes),
        in_specs=[SMEM] * scalars + [HBM if own else VMEM] * (len(args) - scalars),
        out_specs=VMEM if single else tuple(VMEM for _ in shapes),
        scratch_shapes=list(own),
        compiler_params=pltpu.CompilerParams(vmem_limit_bytes=48 * 1024 * 1024),
    )(*args)


def exchange(a, axis):
    return lax.all_to_all(a, axis, 0, 0, tiled=True)


def body(x_in, gate_in, b_in, c_in, decay_fwd, decay_bwd, skip_gain, norm_gain, w_out, d_out):
    n_hi, n_lo, n_x, n_h = (lax.axis_size(axis) for axis in ("z_hi", "z_lo", "x", "head"))
    group = ("z_lo", "x")
    n = n_lo * n_x
    model = d_out.shape[1]
    gain = norm_gain.reshape(1, WIDTH)
    size = WIDTH // n
    weights = size * model // LANES
    place = lax.axis_index("z_hi").astype(jnp.int32).reshape(1)
    decays = (decay_fwd, decay_bwd)
    square = (FRAMES, WIDTH)

    firsts = tuple(pltpu.with_memory_space_constraint(a, pltpu.MemorySpace.HBM) for a in (x_in, b_in, *decays))
    own = [pltpu.VMEM(a.shape, a.dtype) for a in firsts] + [pltpu.SemaphoreType.DMA((4,))]
    sent = call(local_states, "local_states", [((n, 2 * size + 8, LANES), F32)], *firsts, own=own)
    rec1 = exchange(sent, group)
    near, m = call(
        near_outputs, "near_outputs", [(square, F32)] * 2,
        skip_gain, x_in, b_in, c_in, *decays, gain, w_out, d_out, scalars=1,
    )
    sent = call(totals_up, "totals_up", [((n_hi, size + 8, LANES), F32)], place, rec1, scalars=1)
    recz1 = exchange(sent, "z_hi")
    sent = call(entries_up, "entries_up", [((n, 2 * size, LANES), F32)], place, recz1, rec1, scalars=1)
    entries = exchange(sent, group)

    y, sums = call(
        outputs, "outputs", [(square, F32), ((n_h, 8, LANES), F32)],
        near, m, gate_in, c_in, *decays, entries,
    )
    sums = exchange(sums, "head")
    dy, du, sent = call(
        functools.partial(gradients, inner=WIDTH * n_h), "gradients",
        [(square, F32), (square, F32), ((n, 2 * size + weights, LANES), F32)],
        sums, y, m, gate_in, c_in, *decays, gain, d_out,
    )

    rec2 = exchange(sent, group)
    gx_near, gb_near, gc_near = call(
        near_gradients, "near_gradients", [(square, F32)] + [((FRAMES, STATE), F32)] * 2,
        skip_gain, x_in, b_in, c_in, *decays, dy, entries, scalars=1,
    )
    grad_z = call(gate_gradient, "gate_gradient", [(square, BF16)], du, y, gate_in)
    rows_z = (2 * size + weights) // n_hi
    sent = call(totals_down, "totals_down", [((n_hi, rows_z, LANES), F32)], rec1, rec2)
    recz2 = exchange(sent, "z_hi")
    sent = call(scan_down, "scan_down", [((n_hi, rows_z, LANES), F32)], place, recz1, recz2, scalars=1)
    back = exchange(sent, "z_hi")
    sent = call(entries_down, "entries_down", [((n, 2 * size + weights, LANES), F32)], back, rec1, rec2)
    exits = exchange(sent, group)
    grad_w = call(weight_rows, "weight_rows", [((WIDTH, model), F32)], exits)

    chunk = 2 * FRAMES // n_h
    sent = call(
        finish, "finish", [((n_h, chunk, LANES), F32)], x_in, *decays, exits, gb_near, gc_near
    )
    grad_x = call(finish_x, "finish_x", [(square, BF16)], b_in, *decays, exits, gx_near)
    rec = exchange(sent, "head")
    sent = call(add_up, "add_up", [((n_h, chunk, LANES), F32)], rec)
    rec = exchange(sent, "head")
    grad_b, grad_c = call(deal_out, "deal_out", [((FRAMES, STATE), F32)] * 2, rec)
    return grad_x, grad_z, grad_b, grad_c, grad_w


def solution(mesh):
    n_seq, n_head = mesh.devices.shape
    n_z = n_seq // HEADS
    n_lo = min(2, n_z // 2)
    split = Mesh(mesh.devices.reshape(n_z // n_lo, n_lo, HEADS, n_head), ("z_hi", "z_lo", "x", "head"))
    seq = ("z_hi", "z_lo", "x")
    in_specs = (
        P(seq, "head"),
        P(seq, "head"),
        P(seq, None),
        P(seq, None),
        P("head", seq),
        P("head", seq),
        P("head"),
        P("head"),
        P("head", None),
        P(seq, None),
    )
    out_specs = (
        P(seq, "head"),
        P(seq, "head"),
        P(seq, None),
        P(seq, None),
        P("head", None),
    )
    return jax.shard_map(body, mesh=split, in_specs=in_specs, out_specs=out_specs, check_vma=False)
```

```python
import functools

import jax
import jax.numpy as jnp
from jax import lax
from jax.experimental import pallas as pl
from jax.experimental.pallas import tpu as pltpu
from jax.sharding import Mesh, PartitionSpec as P

HEADS = 4
HEAD_DIM = 64
STATE = 128
FRAMES = 256
WIDTH = HEADS * HEAD_DIM
LANES = 128
EPS_NORM = 1e-05
WEIGHT_SCALE = 0.0078125
F32, BF16 = jnp.float32, jnp.bfloat16


def dot(a, b, ca, cb):
    return lax.dot_general(a, b, (((ca,), (cb,)), ((), ())), preferred_element_type=F32)


def halves(a):
    high = a.astype(BF16)
    return high, (a - high.astype(F32)).astype(BF16)


def dot_left(a, b, ca, cb):
    ah, al = halves(a)
    return dot(ah, b, ca, cb) + dot(al, b, ca, cb)


def dot_right(a, b, ca, cb):
    bh, bl = halves(b)
    return dot(a, bh, ca, cb) + dot(a, bl, ca, cb)


def dot_both(a, b, ca, cb):
    ah, al = halves(a)
    bh, bl = halves(b)
    return dot(ah, bh, ca, cb) + (dot(ah, bl, ca, cb) + dot(al, bh, ca, cb))


def dot_exact(a, b, ca, cb):
    return lax.dot_general(
        a, b, (((ca,), (cb,)), ((), ())), precision=lax.Precision.HIGHEST, preferred_element_type=F32
    )


def places():
    row = lax.broadcasted_iota(jnp.int32, (FRAMES, FRAMES), 0)
    col = lax.broadcasted_iota(jnp.int32, (FRAMES, FRAMES), 1)
    return row, col


def columns(df, db):
    row, col = places()
    upto = (col <= row).astype(F32)
    before = (col < row).astype(F32)
    cf = dot_exact(upto, df, 1, 1)
    be = dot_exact(before, db, 1, 1)
    end_f = cf[FRAMES - 1 :, :]
    end_b = dot_exact(jnp.ones((8, FRAMES), F32), db, 1, 1)[:1, :]
    return cf, be, end_f, end_b


def rows(df, db):
    row, col = places()
    upto = (row <= col).astype(F32)
    before = (row < col).astype(F32)
    return dot_exact(df, upto, 1, 0), dot_exact(db, before, 1, 0)


def spread(cols):
    lane = lax.broadcasted_iota(jnp.int32, (cols.shape[0], LANES), 1)
    pairs = [
        jnp.where(lane < HEAD_DIM, cols[:, 2 * g : 2 * g + 1], cols[:, 2 * g + 1 : 2 * g + 2])
        for g in range(HEADS // 2)
    ]
    return jnp.concatenate(pairs, axis=1)


def pair_decay(h, cf, be, cf_row, be_row, row, col):
    gap = jnp.where(
        row > col,
        cf[:, h : h + 1] - cf_row[h : h + 1, :],
        be_row[h : h + 1, :] - be[:, h : h + 1],
    )
    return jnp.where(row == col, 2.0, jnp.exp(jnp.minimum(gap, 0.0)))


def own_lanes(pair, hh):
    lane = lax.broadcasted_iota(jnp.int32, pair.shape, 1)
    mine = lane < HEAD_DIM if hh == 0 else lane >= HEAD_DIM
    return jnp.where(mine, pair, jnp.zeros_like(pair))


def put_slices(out_ref, forward, backward):
    n = out_ref.shape[0]
    size = WIDTH // n
    for i in range(n):
        at = slice(i * size, (i + 1) * size)
        out_ref[i, 0:size, :] = forward[at, :]
        out_ref[i, size : 2 * size, :] = backward[at, :]


def take_slices(ref):
    n = ref.shape[0]
    size = WIDTH // n
    forward = jnp.concatenate([ref[i, 0:size, :] for i in range(n)], axis=0)
    backward = jnp.concatenate([ref[i, size : 2 * size, :] for i in range(n)], axis=0)
    return forward, backward


def local_states(x_hbm, b_hbm, df_hbm, db_hbm, out_ref, x_ref, b_ref, df_ref, db_ref, sems):
    sources, targets = (x_hbm, b_hbm, df_hbm, db_hbm), (x_ref, b_ref, df_ref, db_ref)
    copies = [pltpu.make_async_copy(s, t, sems.at[i]) for i, (s, t) in enumerate(zip(sources, targets))]
    for copy in copies[::-1]:
        copy.start()
    copies[2].wait()
    copies[3].wait()
    cf, be, end_f, end_b = columns(df_ref[...], db_ref[...])
    copies[0].wait()
    copies[1].wait()
    x = x_ref[...].astype(F32)
    b = b_ref[...]
    state_f = dot_left(x * spread(jnp.exp(end_f - cf)), b, 0, 0)
    state_b = dot_left(x * spread(jnp.exp(be)), b, 0, 0)
    put_slices(out_ref, state_f, state_b)
    n = out_ref.shape[0]
    size = WIDTH // n
    total_f, total_b = jnp.exp(end_f), jnp.exp(end_b)
    half = lax.broadcasted_iota(jnp.int32, (8, LANES), 0) < 4
    for j in range(HEADS):
        both = jnp.where(half, total_f[:, j : j + 1], total_b[:, j : j + 1])
        for i in range(j * n // HEADS, (j + 1) * n // HEADS):
            out_ref[i, 2 * size :, :] = both


def totals_at(ref, i, start):
    return ref[i, start : start + 1, :], ref[i, start + 4 : start + 5, :]


def sliced(ref, i, size):
    return ref[i, 0:size, :], ref[i, size : 2 * size, :]


def group_sums(dec_ref, rec_ref, forward_up):
    n = rec_ref.shape[0]
    size = WIDTH // n
    decays = [totals_at(dec_ref, i, 2 * size) for i in range(n)]
    parts = [sliced(rec_ref, i, size) for i in range(n)]
    sums = []
    for branch, up in enumerate((forward_up, not forward_up)):
        order = list(range(n)) if up else list(range(n))[::-1]
        acc = parts[order[0]][branch]
        for i in order[1:]:
            acc = decays[i][branch] * acc + parts[i][branch]
        sums.append(acc)
    return sums, decays


def totals_up(place_ref, rec_ref, out_ref):
    size = WIDTH // rec_ref.shape[0]
    (sum_f, sum_b), decays = group_sums(rec_ref, rec_ref, True)
    all_f, all_b = decays[0]
    for dec_f, dec_b in decays[1:]:
        all_f, all_b = all_f * dec_f, all_b * dec_b
    half = lax.broadcasted_iota(jnp.int32, (8, LANES), 0) < 4
    for k in range(out_ref.shape[0]):
        out_ref[k, 0:size, :] = jnp.where(place_ref[0] < k, sum_f, sum_b)
        out_ref[k, size:, :] = jnp.where(half, all_f, all_b)


def entries_up(place_ref, zrec_ref, rec_ref, out_ref):
    n_g, n = zrec_ref.shape[0], rec_ref.shape[0]
    size = WIDTH // n
    place = place_ref[0]
    for branch, up in enumerate((True, False)):
        entry = jnp.zeros((size, LANES), F32)
        for k in list(range(n_g)) if up else list(range(n_g))[::-1]:
            passed = place > k if up else place < k
            after = totals_at(zrec_ref, k, size)[branch] * entry + zrec_ref[k, 0:size, :]
            entry = jnp.where(passed, after, entry)
        put_entries(out_ref, branch, up, entry, rec_ref, rec_ref)


def put_entries(out_ref, branch, up, entry, dec_ref, rec_ref):
    n = rec_ref.shape[0]
    size = WIDTH // n
    for i in list(range(n)) if up else list(range(n))[::-1]:
        out_ref[i, branch * size : (branch + 1) * size, :] = entry
        entry = totals_at(dec_ref, i, 2 * size)[branch] * entry + sliced(rec_ref, i, size)[branch]


def totals_down(dec_ref, rec_ref, out_ref):
    n, n_g = rec_ref.shape[0], out_ref.shape[0]
    size = WIDTH // n
    sums, _ = group_sums(dec_ref, rec_ref, False)
    both = jnp.concatenate(sums, axis=0)
    weight = rec_ref[0, 2 * size :, :]
    for i in range(1, n):
        weight = weight + rec_ref[i, 2 * size :, :]
    span, part = 2 * size // n_g, weight.shape[0] // n_g
    for k in range(n_g):
        out_ref[k, 0:span, :] = both[k * span : (k + 1) * span, :]
        out_ref[k, span:, :] = weight[k * part : (k + 1) * part, :]


def scan_down(place_ref, dec_ref, rec_ref, out_ref):
    n_g = rec_ref.shape[0]
    span = 2 * (dec_ref.shape[1] - 8) // n_g
    forward = 2 * place_ref[0] < n_g
    states = [rec_ref[k, 0:span, :] for k in range(n_g)]
    decays = [totals_at(dec_ref, k, dec_ref.shape[1] - 8) for k in range(n_g)]
    down, acc = [None] * n_g, jnp.zeros_like(states[0])
    for k in range(n_g)[::-1]:
        down[k] = acc
        acc = decays[k][0] * acc + states[k]
    up, acc = [None] * n_g, jnp.zeros_like(states[0])
    for k in range(n_g):
        up[k] = acc
        acc = decays[k][1] * acc + states[k]
    weight = rec_ref[0, span:, :]
    for k in range(1, n_g):
        weight = weight + rec_ref[k, span:, :]
    for k in range(n_g):
        out_ref[k, 0:span, :] = jnp.where(forward, down[k], up[k])
        out_ref[k, span:, :] = weight


def entries_down(back_ref, dec_ref, rec_ref, out_ref, w_ref):
    n_g, n = back_ref.shape[0], rec_ref.shape[0]
    size = WIDTH // n
    span = 2 * size // n_g
    half = n_g // 2
    entry_f = jnp.concatenate([back_ref[k, 0:span, :] for k in range(half)], axis=0)
    entry_b = jnp.concatenate([back_ref[k, 0:span, :] for k in range(half, n_g)], axis=0)
    put_entries(out_ref, 0, False, entry_f, dec_ref, rec_ref)
    put_entries(out_ref, 1, True, entry_b, dec_ref, rec_ref)
    part = back_ref.shape[1] - span
    for k in range(n_g):
        w_ref[k * part : (k + 1) * part, :] = back_ref[k, span:, :]


def pair_up(own_ref, other_ref, out_ref):
    out_ref[0, :, :] = own_ref[...]
    out_ref[1, :, :] = other_ref[...]


def weight_rows(at_ref, own_ref, *refs):
    *other_refs, gw_ref = refs
    blocks = gw_ref.shape[1] // LANES
    size = own_ref.shape[1] // blocks
    for i, ref in enumerate((own_ref, *other_refs)):
        for j in range(2):
            at = pl.multiple_of(at_ref[2 * i + j], size)
            for block in range(blocks):
                gw_ref[pl.ds(at, size), block * LANES : (block + 1) * LANES] = (
                    ref[j, block * size : (block + 1) * size, :] * WEIGHT_SCALE
                )


def across_rows(cols):
    lane = lax.broadcasted_iota(jnp.int32, (LANES, LANES), 1)
    grid = jnp.zeros((LANES, LANES), F32)
    for i, col in enumerate(cols):
        for part in range(FRAMES // LANES):
            at = i * (FRAMES // LANES) + part
            grid = jnp.where(lane == at, col[part * LANES : (part + 1) * LANES, :], grid)
    return jnp.transpose(grid)[0:8, :]


def near_outputs(
    skip_ref, x_ref, b_ref, c_ref, df_ref, db_ref, gain_ref, w_ref, do_ref, y_ref, m_ref
):
    df, db = df_ref[...], db_ref[...]
    cf, be, end_f, end_b = columns(df, db)
    cf_row, be_row = rows(df, db)
    row, col = places()
    scores = dot(c_ref[...], b_ref[...], 1, 1)
    lane = lax.broadcasted_iota(jnp.int32, (1, LANES), 1)
    for g in range(HEADS // 2):
        at = slice(g * LANES, (g + 1) * LANES)
        pair = x_ref[:, at]
        acc = jnp.where(lane < HEAD_DIM, skip_ref[2 * g], skip_ref[2 * g + 1]) * pair.astype(F32)
        for hh in range(2):
            weights = scores * pair_decay(2 * g + hh, cf, be, cf_row, be_row, row, col)
            acc = acc + dot_left(weights, own_lanes(pair, hh), 1, 0)
        y_ref[:, at] = acc
    m_ref[...] = dot(do_ref[...], w_ref[...], 1, 1) * gain_ref[...]


def outputs(near_ref, m_ref, z_ref, c_ref, df_ref, db_ref, ent_ref, y_ref, sums_ref):
    cf, be, end_f, end_b = columns(df_ref[...], db_ref[...])
    c = c_ref[...]
    entry_f, entry_b = take_slices(ent_ref)
    y = near_ref[...] + spread(jnp.exp(cf)) * dot_right(c, entry_f, 1, 1)
    y = y + spread(jnp.exp(end_b - be)) * dot_right(c, entry_b, 1, 1)
    y_ref[...] = y
    z, m = z_ref[...].astype(F32), m_ref[...]
    u = y * z * jax.nn.sigmoid(z)
    sums = across_rows([jnp.sum(u * u, axis=1, keepdims=True), jnp.sum(u * m, axis=1, keepdims=True)])
    for i in range(sums_ref.shape[0]):
        sums_ref[i, :, :] = sums


def gradients(
    sums_ref, y_ref, m_ref, z_ref, c_ref, df_ref, db_ref, gain_ref, do_ref,
    dy_ref, du_ref, out_ref, *, inner,
):
    total = sums_ref[0, :, :]
    for i in range(1, sums_ref.shape[0]):
        total = total + sums_ref[i, :, :]
    grid = jnp.transpose(jnp.concatenate([total, jnp.zeros((LANES - 8, LANES), F32)], axis=0))
    square = jnp.concatenate([grid[:, 0:1], grid[:, 1:2]], axis=0) / inner
    cross = jnp.concatenate([grid[:, 2:3], grid[:, 3:4]], axis=0) / inner
    q = lax.rsqrt(square + EPS_NORM)
    y, m, z = y_ref[...], m_ref[...], z_ref[...].astype(F32)
    sig = jax.nn.sigmoid(z)
    silu = z * sig
    u = y * z * sig
    normed = (u * q * gain_ref[...]).astype(BF16)
    du = q * m - u * (q * q * q * cross)
    dy = du * silu
    dy_ref[...] = dy
    du_ref[...] = du
    cf, be, end_f, end_b = columns(df_ref[...], db_ref[...])
    c = c_ref[...]
    back_f = dot_left(dy * spread(jnp.exp(cf)), c, 0, 0)
    back_b = dot_left(dy * spread(jnp.exp(end_b - be)), c, 0, 0)
    put_slices(out_ref, back_f, back_b)
    weight = dot(normed, do_ref[...], 0, 0)
    n = out_ref.shape[0]
    size = WIDTH // n
    for i in range(n):
        for block in range(weight.shape[1] // LANES):
            at = 2 * size + block * size
            out_ref[i, at : at + size, :] = weight[
                i * size : (i + 1) * size, block * LANES : (block + 1) * LANES
            ]


def near_gradients(
    skip_ref, x_ref, b_ref, c_ref, df_ref, db_ref, dy_ref, ent_ref, gx_ref, gb_ref, gc_ref
):
    df, db = df_ref[...], db_ref[...]
    cf, be, end_f, end_b = columns(df, db)
    cf_row, be_row = rows(df, db)
    row, col = places()
    b, c, dy = b_ref[...], c_ref[...], dy_ref[...]
    scores = dot(c, b, 1, 1)
    pair_sum = jnp.zeros((FRAMES, FRAMES), F32)
    lane = lax.broadcasted_iota(jnp.int32, (1, LANES), 1)
    for g in range(HEADS // 2):
        at = slice(g * LANES, (g + 1) * LANES)
        acc = jnp.where(lane < HEAD_DIM, skip_ref[2 * g], skip_ref[2 * g + 1]) * dy[:, at]
        for hh in range(2):
            decay = pair_decay(2 * g + hh, cf, be, cf_row, be_row, row, col)
            dy_own = own_lanes(dy[:, at], hh)
            pair_sum = pair_sum + decay * dot_left(dy_own, x_ref[:, at], 1, 1)
            acc = acc + dot_both(scores * decay, dy_own, 0, 0)
        gx_ref[:, at] = acc
    entry_f, entry_b = take_slices(ent_ref)
    rise_f, rise_b = spread(jnp.exp(cf)), spread(jnp.exp(end_b - be))
    grad_c = dot_left(pair_sum, b, 1, 0)
    gc_ref[...] = grad_c + dot_both(dy * rise_f, entry_f, 1, 0) + dot_both(dy * rise_b, entry_b, 1, 0)
    gb_ref[...] = dot_left(pair_sum, c, 0, 0)


def gate_gradient(du_ref, y_ref, z_ref, gz_ref):
    z = z_ref[...].astype(F32)
    sig = jax.nn.sigmoid(z)
    gz_ref[...] = (du_ref[...] * y_ref[...] * sig * (1.0 + z * (1.0 - sig))).astype(BF16)


def finish(x_ref, df_ref, db_ref, exit_ref, gb_near, gc_near, out_ref):
    cf, be, end_f, end_b = columns(df_ref[...], db_ref[...])
    x = x_ref[...].astype(F32)
    exit_f, exit_b = take_slices(exit_ref)
    grad_b = gb_near[...] + dot_both(x * spread(jnp.exp(end_f - cf)), exit_f, 1, 0)
    grad_b = grad_b + dot_both(x * spread(jnp.exp(be)), exit_b, 1, 0)
    grad_c = gc_near[...]
    n = out_ref.shape[0]
    size = FRAMES // n
    for i in range(n):
        out_ref[i, 0:size, :] = grad_b[i * size : (i + 1) * size, :]
        out_ref[i, size : 2 * size, :] = grad_c[i * size : (i + 1) * size, :]


def finish_x(b_ref, df_ref, db_ref, exit_ref, gx_near, gx_ref):
    cf, be, end_f, end_b = columns(df_ref[...], db_ref[...])
    b = b_ref[...]
    exit_f, exit_b = take_slices(exit_ref)
    gx = gx_near[...] + spread(jnp.exp(end_f - cf)) * dot_right(b, exit_f, 1, 1)
    gx_ref[...] = (gx + spread(jnp.exp(be)) * dot_right(b, exit_b, 1, 1)).astype(BF16)


def add_up(rec_ref, out_ref):
    n = rec_ref.shape[0]
    total = rec_ref[0, :, :]
    for i in range(1, n):
        total = total + rec_ref[i, :, :]
    for i in range(n):
        out_ref[i, :, :] = total


def deal_out(rec_ref, gb_ref, gc_ref):
    n = rec_ref.shape[0]
    size = FRAMES // n
    for i in range(n):
        gb_ref[i * size : (i + 1) * size, :] = rec_ref[i, 0:size, :]
        gc_ref[i * size : (i + 1) * size, :] = rec_ref[i, size : 2 * size, :]


VMEM = pl.BlockSpec(memory_space=pltpu.VMEM)
SMEM = pl.BlockSpec(memory_space=pltpu.SMEM)
HBM = pl.BlockSpec(memory_space=pltpu.MemorySpace.HBM)


def call(kernel, name, out, *args, scalars=0, own=()):
    shapes = [jax.ShapeDtypeStruct(shape, dtype) for shape, dtype in out]
    single = len(shapes) == 1
    return pl.pallas_call(
        kernel,
        name=name,
        out_shape=shapes[0] if single else tuple(shapes),
        in_specs=[SMEM] * scalars + [HBM if own else VMEM] * (len(args) - scalars),
        out_specs=VMEM if single else tuple(VMEM for _ in shapes),
        scratch_shapes=list(own),
        compiler_params=pltpu.CompilerParams(vmem_limit_bytes=48 * 1024 * 1024),
    )(*args)


def exchange(a, axis):
    return lax.all_to_all(a, axis, 0, 0, tiled=True)


def body(x_in, gate_in, b_in, c_in, decay_fwd, decay_bwd, skip_gain, norm_gain, w_out, d_out):
    n_hi, n_lo, n_x, n_h = (lax.axis_size(axis) for axis in ("z_hi", "z_lo", "x", "head"))
    group = ("z_lo", "x")
    n = n_lo * n_x
    model = d_out.shape[1]
    gain = norm_gain.reshape(1, WIDTH)
    size = WIDTH // n
    weights = size * model // LANES
    place = lax.axis_index("z_hi").astype(jnp.int32).reshape(1)
    decays = (decay_fwd, decay_bwd)
    square = (FRAMES, WIDTH)

    firsts = tuple(pltpu.with_memory_space_constraint(a, pltpu.MemorySpace.HBM) for a in (x_in, b_in, *decays))
    own = [pltpu.VMEM(a.shape, a.dtype) for a in firsts] + [pltpu.SemaphoreType.DMA((4,))]
    sent = call(local_states, "local_states", [((n, 2 * size + 8, LANES), F32)], *firsts, own=own)
    rec1 = exchange(sent, group)
    near, m = call(
        near_outputs, "near_outputs", [(square, F32)] * 2,
        skip_gain, x_in, b_in, c_in, *decays, gain, w_out, d_out, scalars=1,
    )
    sent = call(totals_up, "totals_up", [((n_hi, size + 8, LANES), F32)], place, rec1, scalars=1)
    recz1 = exchange(sent, "z_hi")
    sent = call(entries_up, "entries_up", [((n, 2 * size, LANES), F32)], place, recz1, rec1, scalars=1)
    entries = exchange(sent, group)

    y, sums = call(
        outputs, "outputs", [(square, F32), ((n_h, 8, LANES), F32)],
        near, m, gate_in, c_in, *decays, entries,
    )
    sums = exchange(sums, "head")
    dy, du, sent = call(
        functools.partial(gradients, inner=WIDTH * n_h), "gradients",
        [(square, F32), (square, F32), ((n, 2 * size + weights, LANES), F32)],
        sums, y, m, gate_in, c_in, *decays, gain, d_out,
    )

    rec2 = exchange(sent, group)
    gx_near, gb_near, gc_near = call(
        near_gradients, "near_gradients", [(square, F32)] + [((FRAMES, STATE), F32)] * 2,
        skip_gain, x_in, b_in, c_in, *decays, dy, entries, scalars=1,
    )
    grad_z = call(gate_gradient, "gate_gradient", [(square, BF16)], du, y, gate_in)
    rows_z = (2 * size + weights) // n_hi
    sent = call(totals_down, "totals_down", [((n_hi, rows_z, LANES), F32)], rec1, rec2)
    recz2 = exchange(sent, "z_hi")
    recz2, gx_near, gb_near, gc_near, grad_z = lax.optimization_barrier(
        (recz2, gx_near, gb_near, gc_near, grad_z)
    )
    sent = call(scan_down, "scan_down", [((n_hi, rows_z, LANES), F32)], place, recz1, recz2, scalars=1)
    back = exchange(sent, "z_hi")
    sent, weight = call(
        entries_down, "entries_down", [((n, 2 * size, LANES), F32), ((weights, LANES), F32)], back, rec1, rec2
    )
    exits = exchange(sent, group)

    other = lax.ppermute(weight, "z_lo", [(0, 1), (1, 0)])
    pair = call(pair_up, "pair_up", [((2, weights, LANES), F32)], weight, other)
    exits, pair = lax.optimization_barrier((exits, pair))
    z_lo, x = lax.axis_index("z_lo"), lax.axis_index("x")
    turns = (2, 1, n_x - 1)
    at = [size * (z * n_x + (x - turn) % n_x) for turn in (0, *turns) for z in (z_lo, 1 - z_lo)]
    at = jnp.stack(at).astype(jnp.int32)

    def turned(a, turn):
        return lax.ppermute(a, "x", [(i, (i + turn) % n_x) for i in range(n_x)])

    chunk = 2 * FRAMES // n_h
    sent = call(
        finish, "finish", [((n_h, chunk, LANES), F32)], x_in, *decays, exits, gb_near, gc_near
    )
    grad_x = call(finish_x, "finish_x", [(square, BF16)], b_in, *decays, exits, gx_near)
    rec = exchange(sent, "head")
    pairs = [turned(pair, turn) for turn in turns[:2]]
    sent = call(add_up, "add_up", [((n_h, chunk, LANES), F32)], rec)
    sent, late = lax.optimization_barrier((sent, pair))
    rec = exchange(sent, "head")
    pairs.append(turned(late, turns[2]))
    grad_w = call(weight_rows, "weight_rows", [((WIDTH, model), F32)], at, pair, *pairs, scalars=1)
    rec, grad_w, grad_x = lax.optimization_barrier((rec, grad_w, grad_x))
    grad_b, grad_c = call(deal_out, "deal_out", [((FRAMES, STATE), F32)] * 2, rec)
    return grad_x, grad_z, grad_b, grad_c, grad_w


def solution(mesh):
    n_seq, n_head = mesh.devices.shape
    n_z = n_seq // HEADS
    n_lo = 2
    split = Mesh(mesh.devices.reshape(n_z // n_lo, n_lo, HEADS, n_head), ("z_hi", "z_lo", "x", "head"))
    seq = ("z_hi", "z_lo", "x")
    in_specs = (
        P(seq, "head"),
        P(seq, "head"),
        P(seq, None),
        P(seq, None),
        P("head", seq),
        P("head", seq),
        P("head"),
        P("head"),
        P("head", None),
        P(seq, None),
    )
    out_specs = (
        P(seq, "head"),
        P(seq, "head"),
        P(seq, None),
        P(seq, None),
        P("head", None),
    )
    return jax.shard_map(body, mesh=split, in_specs=in_specs, out_specs=out_specs, check_vma=False)
```

```python
import functools

import jax
import jax.numpy as jnp
from jax import lax
from jax.experimental import pallas as pl
from jax.experimental.pallas import tpu as pltpu
from jax.sharding import Mesh, PartitionSpec as P

HEADS = 4
HEAD_DIM = 64
STATE = 128
FRAMES = 256
WIDTH = HEADS * HEAD_DIM
LANES = 128
EPS_NORM = 1e-05
WEIGHT_SCALE = 0.0078125
F32, BF16 = jnp.float32, jnp.bfloat16


def dot(a, b, ca, cb):
    return lax.dot_general(a, b, (((ca,), (cb,)), ((), ())), preferred_element_type=F32)


def halves(a):
    high = a.astype(BF16)
    return high, (a - high.astype(F32)).astype(BF16)


def dot_left(a, b, ca, cb):
    ah, al = halves(a)
    return dot(ah, b, ca, cb) + dot(al, b, ca, cb)


def dot_right(a, b, ca, cb):
    bh, bl = halves(b)
    return dot(a, bh, ca, cb) + dot(a, bl, ca, cb)


def dot_both(a, b, ca, cb):
    ah, al = halves(a)
    bh, bl = halves(b)
    return dot(ah, bh, ca, cb) + (dot(ah, bl, ca, cb) + dot(al, bh, ca, cb))


def dot_exact(a, b, ca, cb):
    return lax.dot_general(
        a, b, (((ca,), (cb,)), ((), ())), precision=lax.Precision.HIGHEST, preferred_element_type=F32
    )


def places():
    row = lax.broadcasted_iota(jnp.int32, (FRAMES, FRAMES), 0)
    col = lax.broadcasted_iota(jnp.int32, (FRAMES, FRAMES), 1)
    return row, col


def columns(df, db):
    row, col = places()
    upto = (col <= row).astype(F32)
    before = (col < row).astype(F32)
    cf = dot_exact(upto, df, 1, 1)
    be = dot_exact(before, db, 1, 1)
    end_f = cf[FRAMES - 1 :, :]
    end_b = dot_exact(jnp.ones((8, FRAMES), F32), db, 1, 1)[:1, :]
    return cf, be, end_f, end_b


def rows(df, db):
    row, col = places()
    upto = (row <= col).astype(F32)
    before = (row < col).astype(F32)
    return dot_exact(df, upto, 1, 0), dot_exact(db, before, 1, 0)


def spread(cols):
    lane = lax.broadcasted_iota(jnp.int32, (cols.shape[0], LANES), 1)
    pairs = [
        jnp.where(lane < HEAD_DIM, cols[:, 2 * g : 2 * g + 1], cols[:, 2 * g + 1 : 2 * g + 2])
        for g in range(HEADS // 2)
    ]
    return jnp.concatenate(pairs, axis=1)


def pair_decay(h, cf, be, cf_row, be_row, row, col):
    gap = jnp.where(
        row > col,
        cf[:, h : h + 1] - cf_row[h : h + 1, :],
        be_row[h : h + 1, :] - be[:, h : h + 1],
    )
    return jnp.where(row == col, 2.0, jnp.exp(jnp.minimum(gap, 0.0)))


def own_lanes(pair, hh):
    lane = lax.broadcasted_iota(jnp.int32, pair.shape, 1)
    mine = lane < HEAD_DIM if hh == 0 else lane >= HEAD_DIM
    return jnp.where(mine, pair, jnp.zeros_like(pair))


def put_slices(out_ref, forward, backward):
    n = out_ref.shape[0]
    size = WIDTH // n
    for i in range(n):
        at = slice(i * size, (i + 1) * size)
        out_ref[i, 0:size, :] = forward[at, :]
        out_ref[i, size : 2 * size, :] = backward[at, :]


def take_slices(ref):
    n = ref.shape[0]
    size = WIDTH // n
    forward = jnp.concatenate([ref[i, 0:size, :] for i in range(n)], axis=0)
    backward = jnp.concatenate([ref[i, size : 2 * size, :] for i in range(n)], axis=0)
    return forward, backward


def local_states(x_hbm, b_hbm, df_hbm, db_hbm, out_ref, x_ref, b_ref, df_ref, db_ref, sems):
    sources, targets = (x_hbm, b_hbm, df_hbm, db_hbm), (x_ref, b_ref, df_ref, db_ref)
    copies = [pltpu.make_async_copy(s, t, sems.at[i]) for i, (s, t) in enumerate(zip(sources, targets))]
    for copy in copies[::-1]:
        copy.start()
    copies[2].wait()
    copies[3].wait()
    cf, be, end_f, end_b = columns(df_ref[...], db_ref[...])
    copies[0].wait()
    copies[1].wait()
    x = x_ref[...].astype(F32)
    b = b_ref[...]
    state_f = dot_left(x * spread(jnp.exp(end_f - cf)), b, 0, 0)
    state_b = dot_left(x * spread(jnp.exp(be)), b, 0, 0)
    put_slices(out_ref, state_f, state_b)
    n = out_ref.shape[0]
    size = WIDTH // n
    total_f, total_b = jnp.exp(end_f), jnp.exp(end_b)
    half = lax.broadcasted_iota(jnp.int32, (8, LANES), 0) < 4
    for j in range(HEADS):
        both = jnp.where(half, total_f[:, j : j + 1], total_b[:, j : j + 1])
        for i in range(j * n // HEADS, (j + 1) * n // HEADS):
            out_ref[i, 2 * size :, :] = both


def totals_at(ref, i, start):
    return ref[i, start : start + 1, :], ref[i, start + 4 : start + 5, :]


def sliced(ref, i, size):
    return ref[i, 0:size, :], ref[i, size : 2 * size, :]


def group_sums(dec_ref, rec_ref, forward_up):
    n = rec_ref.shape[0]
    size = WIDTH // n
    decays = [totals_at(dec_ref, i, 2 * size) for i in range(n)]
    parts = [sliced(rec_ref, i, size) for i in range(n)]
    sums = []
    for branch, up in enumerate((forward_up, not forward_up)):
        order = list(range(n)) if up else list(range(n))[::-1]
        acc = parts[order[0]][branch]
        for i in order[1:]:
            acc = decays[i][branch] * acc + parts[i][branch]
        sums.append(acc)
    return sums, decays


def totals_up(place_ref, rec_ref, out_ref):
    size = WIDTH // rec_ref.shape[0]
    (sum_f, sum_b), decays = group_sums(rec_ref, rec_ref, True)
    all_f, all_b = decays[0]
    for dec_f, dec_b in decays[1:]:
        all_f, all_b = all_f * dec_f, all_b * dec_b
    half = lax.broadcasted_iota(jnp.int32, (8, LANES), 0) < 4
    for k in range(out_ref.shape[0]):
        out_ref[k, 0:size, :] = jnp.where(place_ref[0] < k, sum_f, sum_b)
        out_ref[k, size:, :] = jnp.where(half, all_f, all_b)


def entries_up(place_ref, zrec_ref, rec_ref, out_ref):
    n_g, n = zrec_ref.shape[0], rec_ref.shape[0]
    size = WIDTH // n
    place = place_ref[0]
    for branch, up in enumerate((True, False)):
        entry = jnp.zeros((size, LANES), F32)
        for k in list(range(n_g)) if up else list(range(n_g))[::-1]:
            passed = place > k if up else place < k
            after = totals_at(zrec_ref, k, size)[branch] * entry + zrec_ref[k, 0:size, :]
            entry = jnp.where(passed, after, entry)
        put_entries(out_ref, branch, up, entry, rec_ref, rec_ref)


def put_entries(out_ref, branch, up, entry, dec_ref, rec_ref):
    n = rec_ref.shape[0]
    size = WIDTH // n
    for i in list(range(n)) if up else list(range(n))[::-1]:
        out_ref[i, branch * size : (branch + 1) * size, :] = entry
        entry = totals_at(dec_ref, i, 2 * size)[branch] * entry + sliced(rec_ref, i, size)[branch]


def totals_down(dec_ref, rec_ref, out_ref):
    n, n_g = rec_ref.shape[0], out_ref.shape[0]
    size = WIDTH // n
    sums, _ = group_sums(dec_ref, rec_ref, False)
    both = jnp.concatenate(sums, axis=0)
    weight = rec_ref[0, 2 * size :, :]
    for i in range(1, n):
        weight = weight + rec_ref[i, 2 * size :, :]
    span, part = 2 * size // n_g, weight.shape[0] // n_g
    for k in range(n_g):
        out_ref[k, 0:span, :] = both[k * span : (k + 1) * span, :]
        out_ref[k, span:, :] = weight[k * part : (k + 1) * part, :]


def scan_down(place_ref, dec_ref, rec_ref, out_ref):
    n_g = rec_ref.shape[0]
    span = 2 * (dec_ref.shape[1] - 8) // n_g
    forward = 2 * place_ref[0] < n_g
    states = [rec_ref[k, 0:span, :] for k in range(n_g)]
    decays = [totals_at(dec_ref, k, dec_ref.shape[1] - 8) for k in range(n_g)]
    down, acc = [None] * n_g, jnp.zeros_like(states[0])
    for k in range(n_g)[::-1]:
        down[k] = acc
        acc = decays[k][0] * acc + states[k]
    up, acc = [None] * n_g, jnp.zeros_like(states[0])
    for k in range(n_g):
        up[k] = acc
        acc = decays[k][1] * acc + states[k]
    weight = rec_ref[0, span:, :]
    for k in range(1, n_g):
        weight = weight + rec_ref[k, span:, :]
    for k in range(n_g):
        out_ref[k, 0:span, :] = jnp.where(forward, down[k], up[k])
        out_ref[k, span:, :] = weight


def entries_down(back_ref, dec_ref, rec_ref, out_ref):
    n_g, n = back_ref.shape[0], rec_ref.shape[0]
    size = WIDTH // n
    span = 2 * size // n_g
    half = n_g // 2
    entry_f = jnp.concatenate([back_ref[k, 0:span, :] for k in range(half)], axis=0)
    entry_b = jnp.concatenate([back_ref[k, 0:span, :] for k in range(half, n_g)], axis=0)
    put_entries(out_ref, 0, False, entry_f, dec_ref, rec_ref)
    put_entries(out_ref, 1, True, entry_b, dec_ref, rec_ref)
    part = back_ref.shape[1] - span
    for k in range(n_g):
        weight = back_ref[k, span:, :]
        for i in range(n):
            out_ref[i, 2 * size + k * part : 2 * size + (k + 1) * part, :] = weight


def weight_rows(rec_ref, gw_ref):
    n = rec_ref.shape[0]
    size = WIDTH // n
    for i in range(n):
        for block in range(gw_ref.shape[1] // LANES):
            at = 2 * size + block * size
            gw_ref[i * size : (i + 1) * size, block * LANES : (block + 1) * LANES] = (
                rec_ref[i, at : at + size, :] * WEIGHT_SCALE
            )


def across_rows(cols):
    lane = lax.broadcasted_iota(jnp.int32, (LANES, LANES), 1)
    grid = jnp.zeros((LANES, LANES), F32)
    for i, col in enumerate(cols):
        for part in range(FRAMES // LANES):
            at = i * (FRAMES // LANES) + part
            grid = jnp.where(lane == at, col[part * LANES : (part + 1) * LANES, :], grid)
    return jnp.transpose(grid)[0:8, :]


def near_outputs(
    skip_ref, x_ref, b_ref, c_ref, df_ref, db_ref, gain_ref, w_ref, do_ref, y_ref, m_ref
):
    df, db = df_ref[...], db_ref[...]
    cf, be, end_f, end_b = columns(df, db)
    cf_row, be_row = rows(df, db)
    row, col = places()
    scores = dot(c_ref[...], b_ref[...], 1, 1)
    lane = lax.broadcasted_iota(jnp.int32, (1, LANES), 1)
    for g in range(HEADS // 2):
        at = slice(g * LANES, (g + 1) * LANES)
        pair = x_ref[:, at]
        acc = jnp.where(lane < HEAD_DIM, skip_ref[2 * g], skip_ref[2 * g + 1]) * pair.astype(F32)
        for hh in range(2):
            weights = scores * pair_decay(2 * g + hh, cf, be, cf_row, be_row, row, col)
            acc = acc + dot_left(weights, own_lanes(pair, hh), 1, 0)
        y_ref[:, at] = acc
    m_ref[...] = dot(do_ref[...], w_ref[...], 1, 1) * gain_ref[...]


def outputs(near_ref, m_ref, z_ref, c_ref, df_ref, db_ref, ent_ref, y_ref, sums_ref):
    cf, be, end_f, end_b = columns(df_ref[...], db_ref[...])
    c = c_ref[...]
    entry_f, entry_b = take_slices(ent_ref)
    y = near_ref[...] + spread(jnp.exp(cf)) * dot_right(c, entry_f, 1, 1)
    y = y + spread(jnp.exp(end_b - be)) * dot_right(c, entry_b, 1, 1)
    y_ref[...] = y
    z, m = z_ref[...].astype(F32), m_ref[...]
    u = y * z * jax.nn.sigmoid(z)
    sums = across_rows([jnp.sum(u * u, axis=1, keepdims=True), jnp.sum(u * m, axis=1, keepdims=True)])
    for i in range(sums_ref.shape[0]):
        sums_ref[i, :, :] = sums


def gradients(
    sums_ref, y_ref, m_ref, z_ref, c_ref, df_ref, db_ref, gain_ref, do_ref,
    dy_ref, du_ref, out_ref, *, inner,
):
    total = sums_ref[0, :, :]
    for i in range(1, sums_ref.shape[0]):
        total = total + sums_ref[i, :, :]
    grid = jnp.transpose(jnp.concatenate([total, jnp.zeros((LANES - 8, LANES), F32)], axis=0))
    square = jnp.concatenate([grid[:, 0:1], grid[:, 1:2]], axis=0) / inner
    cross = jnp.concatenate([grid[:, 2:3], grid[:, 3:4]], axis=0) / inner
    q = lax.rsqrt(square + EPS_NORM)
    y, m, z = y_ref[...], m_ref[...], z_ref[...].astype(F32)
    sig = jax.nn.sigmoid(z)
    silu = z * sig
    u = y * z * sig
    normed = (u * q * gain_ref[...]).astype(BF16)
    du = q * m - u * (q * q * q * cross)
    dy = du * silu
    dy_ref[...] = dy
    du_ref[...] = du
    cf, be, end_f, end_b = columns(df_ref[...], db_ref[...])
    c = c_ref[...]
    back_f = dot_left(dy * spread(jnp.exp(cf)), c, 0, 0)
    back_b = dot_left(dy * spread(jnp.exp(end_b - be)), c, 0, 0)
    put_slices(out_ref, back_f, back_b)
    weight = dot(normed, do_ref[...], 0, 0)
    n = out_ref.shape[0]
    size = WIDTH // n
    for i in range(n):
        for block in range(weight.shape[1] // LANES):
            at = 2 * size + block * size
            out_ref[i, at : at + size, :] = weight[
                i * size : (i + 1) * size, block * LANES : (block + 1) * LANES
            ]


def near_gradients(
    skip_ref, x_ref, b_ref, c_ref, df_ref, db_ref, dy_ref, ent_ref, gx_ref, gb_ref, gc_ref
):
    df, db = df_ref[...], db_ref[...]
    cf, be, end_f, end_b = columns(df, db)
    cf_row, be_row = rows(df, db)
    row, col = places()
    b, c, dy = b_ref[...], c_ref[...], dy_ref[...]
    scores = dot(c, b, 1, 1)
    pair_sum = jnp.zeros((FRAMES, FRAMES), F32)
    lane = lax.broadcasted_iota(jnp.int32, (1, LANES), 1)
    for g in range(HEADS // 2):
        at = slice(g * LANES, (g + 1) * LANES)
        acc = jnp.where(lane < HEAD_DIM, skip_ref[2 * g], skip_ref[2 * g + 1]) * dy[:, at]
        for hh in range(2):
            decay = pair_decay(2 * g + hh, cf, be, cf_row, be_row, row, col)
            dy_own = own_lanes(dy[:, at], hh)
            pair_sum = pair_sum + decay * dot_left(dy_own, x_ref[:, at], 1, 1)
            acc = acc + dot_both(scores * decay, dy_own, 0, 0)
        gx_ref[:, at] = acc
    entry_f, entry_b = take_slices(ent_ref)
    rise_f, rise_b = spread(jnp.exp(cf)), spread(jnp.exp(end_b - be))
    grad_c = dot_left(pair_sum, b, 1, 0)
    gc_ref[...] = grad_c + dot_both(dy * rise_f, entry_f, 1, 0) + dot_both(dy * rise_b, entry_b, 1, 0)
    gb_ref[...] = dot_left(pair_sum, c, 0, 0)


def gate_gradient(du_ref, y_ref, z_ref, gz_ref):
    z = z_ref[...].astype(F32)
    sig = jax.nn.sigmoid(z)
    gz_ref[...] = (du_ref[...] * y_ref[...] * sig * (1.0 + z * (1.0 - sig))).astype(BF16)


def finish(x_ref, df_ref, db_ref, exit_ref, gb_near, gc_near, out_ref):
    cf, be, end_f, end_b = columns(df_ref[...], db_ref[...])
    x = x_ref[...].astype(F32)
    exit_f, exit_b = take_slices(exit_ref)
    grad_b = gb_near[...] + dot_both(x * spread(jnp.exp(end_f - cf)), exit_f, 1, 0)
    grad_b = grad_b + dot_both(x * spread(jnp.exp(be)), exit_b, 1, 0)
    grad_c = gc_near[...]
    n = out_ref.shape[0]
    size = FRAMES // n
    for i in range(n):
        out_ref[i, 0:size, :] = grad_b[i * size : (i + 1) * size, :]
        out_ref[i, size : 2 * size, :] = grad_c[i * size : (i + 1) * size, :]


def finish_x(b_ref, df_ref, db_ref, exit_ref, gx_near, gx_ref):
    cf, be, end_f, end_b = columns(df_ref[...], db_ref[...])
    b = b_ref[...]
    exit_f, exit_b = take_slices(exit_ref)
    gx = gx_near[...] + spread(jnp.exp(end_f - cf)) * dot_right(b, exit_f, 1, 1)
    gx_ref[...] = (gx + spread(jnp.exp(be)) * dot_right(b, exit_b, 1, 1)).astype(BF16)


def add_up(rec_ref, out_ref):
    n = rec_ref.shape[0]
    total = rec_ref[0, :, :]
    for i in range(1, n):
        total = total + rec_ref[i, :, :]
    for i in range(n):
        out_ref[i, :, :] = total


def deal_out(rec_ref, gb_ref, gc_ref):
    n = rec_ref.shape[0]
    size = FRAMES // n
    for i in range(n):
        gb_ref[i * size : (i + 1) * size, :] = rec_ref[i, 0:size, :]
        gc_ref[i * size : (i + 1) * size, :] = rec_ref[i, size : 2 * size, :]


VMEM = pl.BlockSpec(memory_space=pltpu.VMEM)
SMEM = pl.BlockSpec(memory_space=pltpu.SMEM)
HBM = pl.BlockSpec(memory_space=pltpu.MemorySpace.HBM)


def call(kernel, name, out, *args, scalars=0, own=()):
    shapes = [jax.ShapeDtypeStruct(shape, dtype) for shape, dtype in out]
    single = len(shapes) == 1
    return pl.pallas_call(
        kernel,
        name=name,
        out_shape=shapes[0] if single else tuple(shapes),
        in_specs=[SMEM] * scalars + [HBM if own else VMEM] * (len(args) - scalars),
        out_specs=VMEM if single else tuple(VMEM for _ in shapes),
        scratch_shapes=list(own),
        compiler_params=pltpu.CompilerParams(vmem_limit_bytes=48 * 1024 * 1024),
    )(*args)


def exchange(a, axis):
    return lax.all_to_all(a, axis, 0, 0, tiled=True)


def body(x_in, gate_in, b_in, c_in, decay_fwd, decay_bwd, skip_gain, norm_gain, w_out, d_out):
    n_hi, n_lo, n_x, n_h = (lax.axis_size(axis) for axis in ("z_hi", "z_lo", "x", "head"))
    group = ("z_lo", "x")
    n = n_lo * n_x
    model = d_out.shape[1]
    gain = norm_gain.reshape(1, WIDTH)
    size = WIDTH // n
    weights = size * model // LANES
    place = lax.axis_index("z_hi").astype(jnp.int32).reshape(1)
    decays = (decay_fwd, decay_bwd)
    square = (FRAMES, WIDTH)

    firsts = tuple(pltpu.with_memory_space_constraint(a, pltpu.MemorySpace.HBM) for a in (x_in, b_in, *decays))
    own = [pltpu.VMEM(a.shape, a.dtype) for a in firsts] + [pltpu.SemaphoreType.DMA((4,))]
    sent = call(local_states, "local_states", [((n, 2 * size + 8, LANES), F32)], *firsts, own=own)
    rec1 = exchange(sent, group)
    near, m = call(
        near_outputs, "near_outputs", [(square, F32)] * 2,
        skip_gain, x_in, b_in, c_in, *decays, gain, w_out, d_out, scalars=1,
    )
    sent = call(totals_up, "totals_up", [((n_hi, size + 8, LANES), F32)], place, rec1, scalars=1)
    recz1 = exchange(sent, "z_hi")
    sent = call(entries_up, "entries_up", [((n, 2 * size, LANES), F32)], place, recz1, rec1, scalars=1)
    entries = exchange(sent, group)

    y, sums = call(
        outputs, "outputs", [(square, F32), ((n_h, 8, LANES), F32)],
        near, m, gate_in, c_in, *decays, entries,
    )
    sums = exchange(sums, "head")
    dy, du, sent = call(
        functools.partial(gradients, inner=WIDTH * n_h), "gradients",
        [(square, F32), (square, F32), ((n, 2 * size + weights, LANES), F32)],
        sums, y, m, gate_in, c_in, *decays, gain, d_out,
    )

    rec2 = exchange(sent, group)
    gx_near, gb_near, gc_near = call(
        near_gradients, "near_gradients", [(square, F32)] + [((FRAMES, STATE), F32)] * 2,
        skip_gain, x_in, b_in, c_in, *decays, dy, entries, scalars=1,
    )
    grad_z = call(gate_gradient, "gate_gradient", [(square, BF16)], du, y, gate_in)
    rows_z = (2 * size + weights) // n_hi
    sent = call(totals_down, "totals_down", [((n_hi, rows_z, LANES), F32)], rec1, rec2)
    recz2 = exchange(sent, "z_hi")
    recz2, gx_near, gb_near, gc_near, grad_z = lax.optimization_barrier(
        (recz2, gx_near, gb_near, gc_near, grad_z)
    )
    sent = call(scan_down, "scan_down", [((n_hi, rows_z, LANES), F32)], place, recz1, recz2, scalars=1)
    back = exchange(sent, "z_hi")
    sent = call(entries_down, "entries_down", [((n, 2 * size + weights, LANES), F32)], back, rec1, rec2)
    exits = exchange(sent, group)
    grad_w = call(weight_rows, "weight_rows", [((WIDTH, model), F32)], exits)

    chunk = 2 * FRAMES // n_h
    sent = call(
        finish, "finish", [((n_h, chunk, LANES), F32)], x_in, *decays, exits, gb_near, gc_near
    )
    grad_x = call(finish_x, "finish_x", [(square, BF16)], b_in, *decays, exits, gx_near)
    rec = exchange(sent, "head")
    sent = call(add_up, "add_up", [((n_h, chunk, LANES), F32)], rec)
    rec = exchange(sent, "head")
    grad_b, grad_c = call(deal_out, "deal_out", [((FRAMES, STATE), F32)] * 2, rec)
    return grad_x, grad_z, grad_b, grad_c, grad_w


def solution(mesh):
    n_seq, n_head = mesh.devices.shape
    n_z = n_seq // HEADS
    n_lo = min(2, n_z // 2)
    split = Mesh(mesh.devices.reshape(n_z // n_lo, n_lo, HEADS, n_head), ("z_hi", "z_lo", "x", "head"))
    seq = ("z_hi", "z_lo", "x")
    in_specs = (
        P(seq, "head"),
        P(seq, "head"),
        P(seq, None),
        P(seq, None),
        P("head", seq),
        P("head", seq),
        P("head"),
        P("head"),
        P("head", None),
        P(seq, None),
    )
    out_specs = (
        P(seq, "head"),
        P(seq, "head"),
        P(seq, None),
        P(seq, None),
        P("head", None),
    )
    return jax.shard_map(body, mesh=split, in_specs=in_specs, out_specs=out_specs, check_vma=False)
```

```python
import functools

import jax
import jax.numpy as jnp
from jax import lax
from jax.experimental import pallas as pl
from jax.experimental.pallas import tpu as pltpu
from jax.sharding import Mesh, PartitionSpec as P

HEADS = 4
HEAD_DIM = 64
STATE = 128
FRAMES = 256
WIDTH = HEADS * HEAD_DIM
LANES = 128
EPS_NORM = 1e-05
WEIGHT_SCALE = 0.0078125
F32, BF16 = jnp.float32, jnp.bfloat16


def dot(a, b, ca, cb):
    return lax.dot_general(a, b, (((ca,), (cb,)), ((), ())), preferred_element_type=F32)


def halves(a):
    high = a.astype(BF16)
    return high, (a - high.astype(F32)).astype(BF16)


def dot_left(a, b, ca, cb):
    ah, al = halves(a)
    return dot(ah, b, ca, cb) + dot(al, b, ca, cb)


def dot_right(a, b, ca, cb):
    bh, bl = halves(b)
    return dot(a, bh, ca, cb) + dot(a, bl, ca, cb)


def dot_both(a, b, ca, cb):
    ah, al = halves(a)
    bh, bl = halves(b)
    return dot(ah, bh, ca, cb) + (dot(ah, bl, ca, cb) + dot(al, bh, ca, cb))


def dot_exact(a, b, ca, cb):
    return lax.dot_general(
        a, b, (((ca,), (cb,)), ((), ())), precision=lax.Precision.HIGHEST, preferred_element_type=F32
    )


def places():
    row = lax.broadcasted_iota(jnp.int32, (FRAMES, FRAMES), 0)
    col = lax.broadcasted_iota(jnp.int32, (FRAMES, FRAMES), 1)
    return row, col


def columns(df, db):
    row, col = places()
    upto = (col <= row).astype(F32)
    before = (col < row).astype(F32)
    cf = dot_exact(upto, df, 1, 1)
    be = dot_exact(before, db, 1, 1)
    end_f = cf[FRAMES - 1 :, :]
    end_b = dot_exact(jnp.ones((8, FRAMES), F32), db, 1, 1)[:1, :]
    return cf, be, end_f, end_b


def rows(df, db):
    row, col = places()
    upto = (row <= col).astype(F32)
    before = (row < col).astype(F32)
    return dot_exact(df, upto, 1, 0), dot_exact(db, before, 1, 0)


def spread(cols):
    lane = lax.broadcasted_iota(jnp.int32, (cols.shape[0], LANES), 1)
    pairs = [
        jnp.where(lane < HEAD_DIM, cols[:, 2 * g : 2 * g + 1], cols[:, 2 * g + 1 : 2 * g + 2])
        for g in range(HEADS // 2)
    ]
    return jnp.concatenate(pairs, axis=1)


def pair_decay(h, cf, be, cf_row, be_row, row, col):
    gap = jnp.where(
        row > col,
        cf[:, h : h + 1] - cf_row[h : h + 1, :],
        be_row[h : h + 1, :] - be[:, h : h + 1],
    )
    return jnp.where(row == col, 2.0, jnp.exp(jnp.minimum(gap, 0.0)))


def own_lanes(pair, hh):
    lane = lax.broadcasted_iota(jnp.int32, pair.shape, 1)
    mine = lane < HEAD_DIM if hh == 0 else lane >= HEAD_DIM
    return jnp.where(mine, pair, jnp.zeros_like(pair))


def put_slices(out_ref, forward, backward):
    n = out_ref.shape[0]
    size = WIDTH // n
    for i in range(n):
        at = slice(i * size, (i + 1) * size)
        out_ref[i, 0:size, :] = forward[at, :]
        out_ref[i, size : 2 * size, :] = backward[at, :]


def take_slices(ref):
    n = ref.shape[0]
    size = WIDTH // n
    forward = jnp.concatenate([ref[i, 0:size, :] for i in range(n)], axis=0)
    backward = jnp.concatenate([ref[i, size : 2 * size, :] for i in range(n)], axis=0)
    return forward, backward


def local_states(x_hbm, b_hbm, df_hbm, db_hbm, out_ref, x_ref, b_ref, df_ref, db_ref, sems):
    sources, targets = (x_hbm, b_hbm, df_hbm, db_hbm), (x_ref, b_ref, df_ref, db_ref)
    copies = [pltpu.make_async_copy(s, t, sems.at[i]) for i, (s, t) in enumerate(zip(sources, targets))]
    for copy in copies[::-1]:
        copy.start()
    copies[2].wait()
    copies[3].wait()
    cf, be, end_f, end_b = columns(df_ref[...], db_ref[...])
    copies[0].wait()
    copies[1].wait()
    x = x_ref[...].astype(F32)
    b = b_ref[...]
    state_f = dot_left(x * spread(jnp.exp(end_f - cf)), b, 0, 0)
    state_b = dot_left(x * spread(jnp.exp(be)), b, 0, 0)
    put_slices(out_ref, state_f, state_b)
    n = out_ref.shape[0]
    size = WIDTH // n
    total_f, total_b = jnp.exp(end_f), jnp.exp(end_b)
    half = lax.broadcasted_iota(jnp.int32, (8, LANES), 0) < 4
    for j in range(HEADS):
        both = jnp.where(half, total_f[:, j : j + 1], total_b[:, j : j + 1])
        for i in range(j * n // HEADS, (j + 1) * n // HEADS):
            out_ref[i, 2 * size :, :] = both


def totals_at(ref, i, start):
    return ref[i, start : start + 1, :], ref[i, start + 4 : start + 5, :]


def sliced(ref, i, size):
    return ref[i, 0:size, :], ref[i, size : 2 * size, :]


def group_sums(dec_ref, rec_ref, forward_up):
    n = rec_ref.shape[0]
    size = WIDTH // n
    decays = [totals_at(dec_ref, i, 2 * size) for i in range(n)]
    parts = [sliced(rec_ref, i, size) for i in range(n)]
    sums = []
    for branch, up in enumerate((forward_up, not forward_up)):
        order = list(range(n)) if up else list(range(n))[::-1]
        acc = parts[order[0]][branch]
        for i in order[1:]:
            acc = decays[i][branch] * acc + parts[i][branch]
        sums.append(acc)
    return sums, decays


def totals_up(place_ref, rec_ref, out_ref):
    size = WIDTH // rec_ref.shape[0]
    (sum_f, sum_b), decays = group_sums(rec_ref, rec_ref, True)
    all_f, all_b = decays[0]
    for dec_f, dec_b in decays[1:]:
        all_f, all_b = all_f * dec_f, all_b * dec_b
    half = lax.broadcasted_iota(jnp.int32, (8, LANES), 0) < 4
    for k in range(out_ref.shape[0]):
        out_ref[k, 0:size, :] = jnp.where(place_ref[0] < k, sum_f, sum_b)
        out_ref[k, size:, :] = jnp.where(half, all_f, all_b)


def entries_up(place_ref, zrec_ref, rec_ref, out_ref):
    n_g, n = zrec_ref.shape[0], rec_ref.shape[0]
    size = WIDTH // n
    place = place_ref[0]
    for branch, up in enumerate((True, False)):
        entry = jnp.zeros((size, LANES), F32)
        for k in list(range(n_g)) if up else list(range(n_g))[::-1]:
            passed = place > k if up else place < k
            after = totals_at(zrec_ref, k, size)[branch] * entry + zrec_ref[k, 0:size, :]
            entry = jnp.where(passed, after, entry)
        put_entries(out_ref, branch, up, entry, rec_ref, rec_ref)


def put_entries(out_ref, branch, up, entry, dec_ref, rec_ref):
    n = rec_ref.shape[0]
    size = WIDTH // n
    for i in list(range(n)) if up else list(range(n))[::-1]:
        out_ref[i, branch * size : (branch + 1) * size, :] = entry
        entry = totals_at(dec_ref, i, 2 * size)[branch] * entry + sliced(rec_ref, i, size)[branch]


def totals_down(place_ref, dec_ref, rec_ref, out_ref):
    n, n_g = rec_ref.shape[0], out_ref.shape[0]
    size = WIDTH // n
    (sum_f, sum_b), _ = group_sums(dec_ref, rec_ref, False)
    weight = rec_ref[0, 2 * size :, :]
    for i in range(1, n):
        weight = weight + rec_ref[i, 2 * size :, :]
    part = weight.shape[0] // n_g
    for k in range(n_g):
        out_ref[k, 0:size, :] = jnp.where(place_ref[0] > k, sum_f, sum_b)
        out_ref[k, size:, :] = weight[k * part : (k + 1) * part, :]


def entries_down(place_ref, zdec_ref, zrec_ref, dec_ref, rec_ref, out_ref, w_ref):
    n_g, n = zrec_ref.shape[0], rec_ref.shape[0]
    size = WIDTH // n
    place = place_ref[0]
    for branch, up in enumerate((False, True)):
        entry = jnp.zeros((size, LANES), F32)
        for k in list(range(n_g)) if up else list(range(n_g))[::-1]:
            passed = place > k if up else place < k
            after = totals_at(zdec_ref, k, size)[branch] * entry + zrec_ref[k, 0:size, :]
            entry = jnp.where(passed, after, entry)
        put_entries(out_ref, branch, up, entry, dec_ref, rec_ref)
    weight = zrec_ref[0, size:, :]
    for k in range(1, n_g):
        weight = weight + zrec_ref[k, size:, :]
    for k in range(n_g):
        w_ref[k, :, :] = weight


def weight_copy(rec_ref, out_ref):
    n_g, part = rec_ref.shape[0], rec_ref.shape[1]
    for k in range(n_g):
        rows = rec_ref[k, :, :]
        for i in range(out_ref.shape[0]):
            out_ref[i, k * part : (k + 1) * part, :] = rows


def weight_rows(rec_ref, gw_ref):
    n = rec_ref.shape[0]
    size = WIDTH // n
    for i in range(n):
        for block in range(gw_ref.shape[1] // LANES):
            gw_ref[i * size : (i + 1) * size, block * LANES : (block + 1) * LANES] = (
                rec_ref[i, block * size : (block + 1) * size, :] * WEIGHT_SCALE
            )


def across_rows(cols):
    lane = lax.broadcasted_iota(jnp.int32, (LANES, LANES), 1)
    grid = jnp.zeros((LANES, LANES), F32)
    for i, col in enumerate(cols):
        for part in range(FRAMES // LANES):
            at = i * (FRAMES // LANES) + part
            grid = jnp.where(lane == at, col[part * LANES : (part + 1) * LANES, :], grid)
    return jnp.transpose(grid)[0:8, :]


def near_outputs(
    skip_ref, x_ref, b_ref, c_ref, df_ref, db_ref, gain_ref, w_ref, do_ref, y_ref, m_ref
):
    df, db = df_ref[...], db_ref[...]
    cf, be, end_f, end_b = columns(df, db)
    cf_row, be_row = rows(df, db)
    row, col = places()
    scores = dot(c_ref[...], b_ref[...], 1, 1)
    lane = lax.broadcasted_iota(jnp.int32, (1, LANES), 1)
    for g in range(HEADS // 2):
        at = slice(g * LANES, (g + 1) * LANES)
        pair = x_ref[:, at]
        acc = jnp.where(lane < HEAD_DIM, skip_ref[2 * g], skip_ref[2 * g + 1]) * pair.astype(F32)
        for hh in range(2):
            weights = scores * pair_decay(2 * g + hh, cf, be, cf_row, be_row, row, col)
            acc = acc + dot_left(weights, own_lanes(pair, hh), 1, 0)
        y_ref[:, at] = acc
    m_ref[...] = dot(do_ref[...], w_ref[...], 1, 1) * gain_ref[...]


def outputs(near_ref, m_ref, z_ref, c_ref, df_ref, db_ref, ent_ref, y_ref, sums_ref):
    cf, be, end_f, end_b = columns(df_ref[...], db_ref[...])
    c = c_ref[...]
    entry_f, entry_b = take_slices(ent_ref)
    y = near_ref[...] + spread(jnp.exp(cf)) * dot_right(c, entry_f, 1, 1)
    y = y + spread(jnp.exp(end_b - be)) * dot_right(c, entry_b, 1, 1)
    y_ref[...] = y
    z, m = z_ref[...].astype(F32), m_ref[...]
    u = y * z * jax.nn.sigmoid(z)
    sums = across_rows([jnp.sum(u * u, axis=1, keepdims=True), jnp.sum(u * m, axis=1, keepdims=True)])
    for i in range(sums_ref.shape[0]):
        sums_ref[i, :, :] = sums


def gradients(
    sums_ref, y_ref, m_ref, z_ref, c_ref, df_ref, db_ref, gain_ref, do_ref,
    dy_ref, du_ref, out_ref, *, inner,
):
    total = sums_ref[0, :, :]
    for i in range(1, sums_ref.shape[0]):
        total = total + sums_ref[i, :, :]
    grid = jnp.transpose(jnp.concatenate([total, jnp.zeros((LANES - 8, LANES), F32)], axis=0))
    square = jnp.concatenate([grid[:, 0:1], grid[:, 1:2]], axis=0) / inner
    cross = jnp.concatenate([grid[:, 2:3], grid[:, 3:4]], axis=0) / inner
    q = lax.rsqrt(square + EPS_NORM)
    y, m, z = y_ref[...], m_ref[...], z_ref[...].astype(F32)
    sig = jax.nn.sigmoid(z)
    silu = z * sig
    u = y * z * sig
    normed = (u * q * gain_ref[...]).astype(BF16)
    du = q * m - u * (q * q * q * cross)
    dy = du * silu
    dy_ref[...] = dy
    du_ref[...] = du
    cf, be, end_f, end_b = columns(df_ref[...], db_ref[...])
    c = c_ref[...]
    back_f = dot_left(dy * spread(jnp.exp(cf)), c, 0, 0)
    back_b = dot_left(dy * spread(jnp.exp(end_b - be)), c, 0, 0)
    put_slices(out_ref, back_f, back_b)
    weight = dot(normed, do_ref[...], 0, 0)
    n = out_ref.shape[0]
    size = WIDTH // n
    for i in range(n):
        for block in range(weight.shape[1] // LANES):
            at = 2 * size + block * size
            out_ref[i, at : at + size, :] = weight[
                i * size : (i + 1) * size, block * LANES : (block + 1) * LANES
            ]


def near_gradients(
    skip_ref, x_ref, b_ref, c_ref, df_ref, db_ref, dy_ref, ent_ref, gx_ref, gb_ref, gc_ref
):
    df, db = df_ref[...], db_ref[...]
    cf, be, end_f, end_b = columns(df, db)
    cf_row, be_row = rows(df, db)
    row, col = places()
    b, c, dy = b_ref[...], c_ref[...], dy_ref[...]
    scores = dot(c, b, 1, 1)
    pair_sum = jnp.zeros((FRAMES, FRAMES), F32)
    lane = lax.broadcasted_iota(jnp.int32, (1, LANES), 1)
    for g in range(HEADS // 2):
        at = slice(g * LANES, (g + 1) * LANES)
        acc = jnp.where(lane < HEAD_DIM, skip_ref[2 * g], skip_ref[2 * g + 1]) * dy[:, at]
        for hh in range(2):
            decay = pair_decay(2 * g + hh, cf, be, cf_row, be_row, row, col)
            dy_own = own_lanes(dy[:, at], hh)
            pair_sum = pair_sum + decay * dot_left(dy_own, x_ref[:, at], 1, 1)
            acc = acc + dot_both(scores * decay, dy_own, 0, 0)
        gx_ref[:, at] = acc
    entry_f, entry_b = take_slices(ent_ref)
    rise_f, rise_b = spread(jnp.exp(cf)), spread(jnp.exp(end_b - be))
    grad_c = dot_left(pair_sum, b, 1, 0)
    gc_ref[...] = grad_c + dot_both(dy * rise_f, entry_f, 1, 0) + dot_both(dy * rise_b, entry_b, 1, 0)
    gb_ref[...] = dot_left(pair_sum, c, 0, 0)


def gate_gradient(du_ref, y_ref, z_ref, gz_ref):
    z = z_ref[...].astype(F32)
    sig = jax.nn.sigmoid(z)
    gz_ref[...] = (du_ref[...] * y_ref[...] * sig * (1.0 + z * (1.0 - sig))).astype(BF16)


def finish(core_ref, x_ref, df_ref, db_ref, exit_ref, gb_near, gc_near, keep_ref, give_ref):
    cf, be, end_f, end_b = columns(df_ref[...], db_ref[...])
    x = x_ref[...].astype(F32)
    exit_f, exit_b = take_slices(exit_ref)
    grad_b = gb_near[...] + dot_both(x * spread(jnp.exp(end_f - cf)), exit_f, 1, 0)
    grad_b = grad_b + dot_both(x * spread(jnp.exp(be)), exit_b, 1, 0)
    half = FRAMES // 2
    first = core_ref[0] == 0
    for i, grad in enumerate((grad_b, gc_near[...])):
        at = slice(i * half, (i + 1) * half)
        keep_ref[at, :] = jnp.where(first, grad[:half, :], grad[half:, :])
        give_ref[at, :] = jnp.where(first, grad[half:, :], grad[:half, :])


def finish_x(b_ref, df_ref, db_ref, exit_ref, gx_near, gx_ref):
    cf, be, end_f, end_b = columns(df_ref[...], db_ref[...])
    b = b_ref[...]
    exit_f, exit_b = take_slices(exit_ref)
    gx = gx_near[...] + spread(jnp.exp(end_f - cf)) * dot_right(b, exit_f, 1, 1)
    gx_ref[...] = (gx + spread(jnp.exp(be)) * dot_right(b, exit_b, 1, 1)).astype(BF16)


def add_two(a_ref, b_ref, out_ref):
    out_ref[...] = a_ref[...] + b_ref[...]


def deal_out(core_ref, own_ref, other_ref, gb_ref, gc_ref):
    half = FRAMES // 2
    first = core_ref[0] == 0
    for i, ref in enumerate((gb_ref, gc_ref)):
        at = slice(i * half, (i + 1) * half)
        ref[0:half, :] = jnp.where(first, own_ref[at, :], other_ref[at, :])
        ref[half:, :] = jnp.where(first, other_ref[at, :], own_ref[at, :])


VMEM = pl.BlockSpec(memory_space=pltpu.VMEM)
SMEM = pl.BlockSpec(memory_space=pltpu.SMEM)
HBM = pl.BlockSpec(memory_space=pltpu.MemorySpace.HBM)


def call(kernel, name, out, *args, scalars=0, own=()):
    shapes = [jax.ShapeDtypeStruct(shape, dtype) for shape, dtype in out]
    single = len(shapes) == 1
    return pl.pallas_call(
        kernel,
        name=name,
        out_shape=shapes[0] if single else tuple(shapes),
        in_specs=[SMEM] * scalars + [HBM if own else VMEM] * (len(args) - scalars),
        out_specs=VMEM if single else tuple(VMEM for _ in shapes),
        scratch_shapes=list(own),
        compiler_params=pltpu.CompilerParams(vmem_limit_bytes=48 * 1024 * 1024),
    )(*args)


def exchange(a, axis):
    return lax.all_to_all(a, axis, 0, 0, tiled=True)


def swapped(a, mask, n_h):
    return lax.ppermute(a, "head", [(i, i ^ mask) for i in range(n_h)])


def body(x_in, gate_in, b_in, c_in, decay_fwd, decay_bwd, skip_gain, norm_gain, w_out, d_out):
    n_hi, n_lo, n_x, n_h = (lax.axis_size(axis) for axis in ("z_hi", "z_lo", "x", "head"))
    group = ("z_lo", "x")
    n = n_lo * n_x
    model = d_out.shape[1]
    gain = norm_gain.reshape(1, WIDTH)
    size = WIDTH // n
    weights = size * model // LANES
    place = lax.axis_index("z_hi").astype(jnp.int32).reshape(1)
    decays = (decay_fwd, decay_bwd)
    square = (FRAMES, WIDTH)

    firsts = tuple(pltpu.with_memory_space_constraint(a, pltpu.MemorySpace.HBM) for a in (x_in, b_in, *decays))
    own = [pltpu.VMEM(a.shape, a.dtype) for a in firsts] + [pltpu.SemaphoreType.DMA((4,))]
    sent = call(local_states, "local_states", [((n, 2 * size + 8, LANES), F32)], *firsts, own=own)
    rec1 = exchange(sent, group)
    near, m = call(
        near_outputs, "near_outputs", [(square, F32)] * 2,
        skip_gain, x_in, b_in, c_in, *decays, gain, w_out, d_out, scalars=1,
    )
    sent = call(totals_up, "totals_up", [((n_hi, size + 8, LANES), F32)], place, rec1, scalars=1)
    recz1 = exchange(sent, "z_hi")
    sent = call(entries_up, "entries_up", [((n, 2 * size, LANES), F32)], place, recz1, rec1, scalars=1)
    entries = exchange(sent, group)

    y, sums = call(
        outputs, "outputs", [(square, F32), ((n_h, 8, LANES), F32)],
        near, m, gate_in, c_in, *decays, entries,
    )
    sums = exchange(sums, "head")
    dy, du, sent = call(
        functools.partial(gradients, inner=WIDTH * n_h), "gradients",
        [(square, F32), (square, F32), ((n, 2 * size + weights, LANES), F32)],
        sums, y, m, gate_in, c_in, *decays, gain, d_out,
    )

    rec2 = exchange(sent, group)
    gx_near, gb_near, gc_near = call(
        near_gradients, "near_gradients", [(square, F32)] + [((FRAMES, STATE), F32)] * 2,
        skip_gain, x_in, b_in, c_in, *decays, dy, entries, scalars=1,
    )
    grad_z = call(gate_gradient, "gate_gradient", [(square, BF16)], du, y, gate_in)
    part = weights // n_hi
    sent = call(totals_down, "totals_down", [((n_hi, size + part, LANES), F32)], place, rec1, rec2, scalars=1)
    recz2 = exchange(sent, "z_hi")
    recz2, gx_near, gb_near, gc_near, grad_z = lax.optimization_barrier(
        (recz2, gx_near, gb_near, gc_near, grad_z)
    )
    sent, weight = call(
        entries_down, "entries_down", [((n, 2 * size, LANES), F32), ((n_hi, part, LANES), F32)],
        place, recz1, recz2, rec1, rec2, scalars=1,
    )
    exits = exchange(sent, group)

    exits, weight = lax.optimization_barrier((exits, weight))
    weight = exchange(weight, "z_hi")

    core = (lax.axis_index("head") % 2).astype(jnp.int32).reshape(1)
    half = [((FRAMES, STATE), F32)]
    own, give = call(finish, "finish", half * 2, core, x_in, *decays, exits, gb_near, gc_near, scalars=1)
    own = call(add_two, "add_core", half, own, swapped(give, 1, n_h))
    own = call(add_two, "add_y", half, own, swapped(own, 2, n_h))
    weight, own = lax.optimization_barrier((weight, own))

    weight = call(weight_copy, "weight_copy", [((n, weights, LANES), F32)], weight)
    weight = exchange(weight, group)
    grad_w = call(weight_rows, "weight_rows", [((WIDTH, model), F32)], weight)

    own = call(add_two, "add_y", half, own, swapped(own, 6, n_h))
    other = swapped(own, 1, n_h)
    grad_x = call(finish_x, "finish_x", [(square, BF16)], b_in, *decays, exits, gx_near)
    grad_b, grad_c = call(deal_out, "deal_out", half * 2, core, own, other, scalars=1)
    return grad_x, grad_z, grad_b, grad_c, grad_w


def solution(mesh):
    n_seq, n_head = mesh.devices.shape
    n_z = n_seq // HEADS
    n_lo = min(2, n_z // 2)
    split = Mesh(mesh.devices.reshape(n_z // n_lo, n_lo, HEADS, n_head), ("z_hi", "z_lo", "x", "head"))
    seq = ("z_hi", "z_lo", "x")
    in_specs = (
        P(seq, "head"),
        P(seq, "head"),
        P(seq, None),
        P(seq, None),
        P("head", seq),
        P("head", seq),
        P("head"),
        P("head"),
        P("head", None),
        P(seq, None),
    )
    out_specs = (
        P(seq, "head"),
        P(seq, "head"),
        P(seq, None),
        P(seq, None),
        P("head", None),
    )
    return jax.shard_map(body, mesh=split, in_specs=in_specs, out_specs=out_specs, check_vma=False)
```

```python
import functools

import jax
import jax.numpy as jnp
from jax import lax
from jax.experimental import pallas as pl
from jax.experimental.pallas import tpu as pltpu
from jax.sharding import Mesh, PartitionSpec as P

HEADS = 4
HEAD_DIM = 64
STATE = 128
FRAMES = 256
WIDTH = HEADS * HEAD_DIM
LANES = 128
EPS_NORM = 1e-05
WEIGHT_SCALE = 0.0078125
F32, BF16 = jnp.float32, jnp.bfloat16


def dot(a, b, ca, cb):
    return lax.dot_general(a, b, (((ca,), (cb,)), ((), ())), preferred_element_type=F32)


def halves(a):
    high = a.astype(BF16)
    return high, (a - high.astype(F32)).astype(BF16)


def dot_left(a, b, ca, cb):
    ah, al = halves(a)
    return dot(ah, b, ca, cb) + dot(al, b, ca, cb)


def dot_right(a, b, ca, cb):
    bh, bl = halves(b)
    return dot(a, bh, ca, cb) + dot(a, bl, ca, cb)


def dot_both(a, b, ca, cb):
    ah, al = halves(a)
    bh, bl = halves(b)
    return dot(ah, bh, ca, cb) + (dot(ah, bl, ca, cb) + dot(al, bh, ca, cb))


def dot_exact(a, b, ca, cb):
    return lax.dot_general(
        a, b, (((ca,), (cb,)), ((), ())), precision=lax.Precision.HIGHEST, preferred_element_type=F32
    )


def places():
    row = lax.broadcasted_iota(jnp.int32, (FRAMES, FRAMES), 0)
    col = lax.broadcasted_iota(jnp.int32, (FRAMES, FRAMES), 1)
    return row, col


def columns(df, db):
    row, col = places()
    upto = (col <= row).astype(F32)
    before = (col < row).astype(F32)
    cf = dot_exact(upto, df, 1, 1)
    be = dot_exact(before, db, 1, 1)
    end_f = cf[FRAMES - 1 :, :]
    end_b = dot_exact(jnp.ones((8, FRAMES), F32), db, 1, 1)[:1, :]
    return cf, be, end_f, end_b


def rows(df, db):
    row, col = places()
    upto = (row <= col).astype(F32)
    before = (row < col).astype(F32)
    return dot_exact(df, upto, 1, 0), dot_exact(db, before, 1, 0)


def spread(cols):
    lane = lax.broadcasted_iota(jnp.int32, (cols.shape[0], LANES), 1)
    pairs = [
        jnp.where(lane < HEAD_DIM, cols[:, 2 * g : 2 * g + 1], cols[:, 2 * g + 1 : 2 * g + 2])
        for g in range(HEADS // 2)
    ]
    return jnp.concatenate(pairs, axis=1)


def pair_decay(h, cf, be, cf_row, be_row, row, col):
    gap = jnp.where(
        row > col,
        cf[:, h : h + 1] - cf_row[h : h + 1, :],
        be_row[h : h + 1, :] - be[:, h : h + 1],
    )
    return jnp.where(row == col, 2.0, jnp.exp(jnp.minimum(gap, 0.0)))


def own_lanes(pair, hh):
    lane = lax.broadcasted_iota(jnp.int32, pair.shape, 1)
    mine = lane < HEAD_DIM if hh == 0 else lane >= HEAD_DIM
    return jnp.where(mine, pair, jnp.zeros_like(pair))


def put_slices(out_ref, forward, backward):
    n = out_ref.shape[0]
    size = WIDTH // n
    for i in range(n):
        at = slice(i * size, (i + 1) * size)
        out_ref[i, 0:size, :] = forward[at, :]
        out_ref[i, size : 2 * size, :] = backward[at, :]


def take_slices(ref):
    n = ref.shape[0]
    size = WIDTH // n
    forward = jnp.concatenate([ref[i, 0:size, :] for i in range(n)], axis=0)
    backward = jnp.concatenate([ref[i, size : 2 * size, :] for i in range(n)], axis=0)
    return forward, backward


def local_states(x_hbm, b_hbm, df_hbm, db_hbm, out_ref, x_ref, b_ref, df_ref, db_ref, sems):
    sources, targets = (x_hbm, b_hbm, df_hbm, db_hbm), (x_ref, b_ref, df_ref, db_ref)
    copies = [pltpu.make_async_copy(s, t, sems.at[i]) for i, (s, t) in enumerate(zip(sources, targets))]
    for copy in copies[::-1]:
        copy.start()
    copies[2].wait()
    copies[3].wait()
    cf, be, end_f, end_b = columns(df_ref[...], db_ref[...])
    copies[0].wait()
    copies[1].wait()
    x = x_ref[...].astype(F32)
    b = b_ref[...]
    state_f = dot_left(x * spread(jnp.exp(end_f - cf)), b, 0, 0)
    state_b = dot_left(x * spread(jnp.exp(be)), b, 0, 0)
    put_slices(out_ref, state_f, state_b)
    n = out_ref.shape[0]
    size = WIDTH // n
    total_f, total_b = jnp.exp(end_f), jnp.exp(end_b)
    half = lax.broadcasted_iota(jnp.int32, (8, LANES), 0) < 4
    for j in range(HEADS):
        both = jnp.where(half, total_f[:, j : j + 1], total_b[:, j : j + 1])
        for i in range(j * n // HEADS, (j + 1) * n // HEADS):
            out_ref[i, 2 * size :, :] = both


def totals_at(ref, i, start):
    return ref[i, start : start + 1, :], ref[i, start + 4 : start + 5, :]


def sliced(ref, i, size):
    return ref[i, 0:size, :], ref[i, size : 2 * size, :]


def group_sums(dec_ref, rec_ref, forward_up):
    n = rec_ref.shape[0]
    size = WIDTH // n
    decays = [totals_at(dec_ref, i, 2 * size) for i in range(n)]
    parts = [sliced(rec_ref, i, size) for i in range(n)]
    sums = []
    for branch, up in enumerate((forward_up, not forward_up)):
        order = list(range(n)) if up else list(range(n))[::-1]
        acc = parts[order[0]][branch]
        for i in order[1:]:
            acc = decays[i][branch] * acc + parts[i][branch]
        sums.append(acc)
    return sums, decays


def totals_up(place_ref, rec_ref, out_ref):
    size = WIDTH // rec_ref.shape[0]
    (sum_f, sum_b), decays = group_sums(rec_ref, rec_ref, True)
    all_f, all_b = decays[0]
    for dec_f, dec_b in decays[1:]:
        all_f, all_b = all_f * dec_f, all_b * dec_b
    half = lax.broadcasted_iota(jnp.int32, (8, LANES), 0) < 4
    for k in range(out_ref.shape[0]):
        out_ref[k, 0:size, :] = jnp.where(place_ref[0] < k, sum_f, sum_b)
        out_ref[k, size:, :] = jnp.where(half, all_f, all_b)


def entries_up(place_ref, zrec_ref, rec_ref, out_ref):
    n_g, n = zrec_ref.shape[0], rec_ref.shape[0]
    size = WIDTH // n
    place = place_ref[0]
    for branch, up in enumerate((True, False)):
        entry = jnp.zeros((size, LANES), F32)
        for k in list(range(n_g)) if up else list(range(n_g))[::-1]:
            passed = place > k if up else place < k
            after = totals_at(zrec_ref, k, size)[branch] * entry + zrec_ref[k, 0:size, :]
            entry = jnp.where(passed, after, entry)
        put_entries(out_ref, branch, up, entry, rec_ref, rec_ref)


def put_entries(out_ref, branch, up, entry, dec_ref, rec_ref):
    n = rec_ref.shape[0]
    size = WIDTH // n
    for i in list(range(n)) if up else list(range(n))[::-1]:
        out_ref[i, branch * size : (branch + 1) * size, :] = entry
        entry = totals_at(dec_ref, i, 2 * size)[branch] * entry + sliced(rec_ref, i, size)[branch]


def totals_down(place_ref, dec_ref, rec_ref, out_ref):
    n, n_g = rec_ref.shape[0], out_ref.shape[0]
    size = WIDTH // n
    (sum_f, sum_b), _ = group_sums(dec_ref, rec_ref, False)
    weight = rec_ref[0, 2 * size :, :]
    for i in range(1, n):
        weight = weight + rec_ref[i, 2 * size :, :]
    part = weight.shape[0] // n_g
    for k in range(n_g):
        out_ref[k, 0:size, :] = jnp.where(place_ref[0] > k, sum_f, sum_b)
        out_ref[k, size:, :] = weight[k * part : (k + 1) * part, :]


def entries_down(place_ref, zdec_ref, zrec_ref, dec_ref, rec_ref, out_ref, w_ref):
    n_g, n = zrec_ref.shape[0], rec_ref.shape[0]
    size = WIDTH // n
    place = place_ref[0]
    for branch, up in enumerate((False, True)):
        entry = jnp.zeros((size, LANES), F32)
        for k in list(range(n_g)) if up else list(range(n_g))[::-1]:
            passed = place > k if up else place < k
            after = totals_at(zdec_ref, k, size)[branch] * entry + zrec_ref[k, 0:size, :]
            entry = jnp.where(passed, after, entry)
        put_entries(out_ref, branch, up, entry, dec_ref, rec_ref)
    weight = zrec_ref[0, size:, :]
    for k in range(1, n_g):
        weight = weight + zrec_ref[k, size:, :]
    for k in range(n_g):
        w_ref[k, :, :] = weight


def weight_copy(rec_ref, out_ref):
    n_g, part = rec_ref.shape[0], rec_ref.shape[1]
    for k in range(n_g):
        rows = rec_ref[k, :, :]
        for i in range(out_ref.shape[0]):
            out_ref[i, k * part : (k + 1) * part, :] = rows


def weight_rows(rec_ref, gw_ref):
    n = rec_ref.shape[0]
    size = WIDTH // n
    for i in range(n):
        for block in range(gw_ref.shape[1] // LANES):
            gw_ref[i * size : (i + 1) * size, block * LANES : (block + 1) * LANES] = (
                rec_ref[i, block * size : (block + 1) * size, :] * WEIGHT_SCALE
            )


def across_rows(cols):
    lane = lax.broadcasted_iota(jnp.int32, (LANES, LANES), 1)
    grid = jnp.zeros((LANES, LANES), F32)
    for i, col in enumerate(cols):
        for part in range(FRAMES // LANES):
            at = i * (FRAMES // LANES) + part
            grid = jnp.where(lane == at, col[part * LANES : (part + 1) * LANES, :], grid)
    return jnp.transpose(grid)[0:8, :]


def near_outputs(
    skip_ref, x_ref, b_ref, c_ref, df_ref, db_ref, gain_ref, w_ref, do_ref, y_ref, m_ref
):
    df, db = df_ref[...], db_ref[...]
    cf, be, end_f, end_b = columns(df, db)
    cf_row, be_row = rows(df, db)
    row, col = places()
    scores = dot(c_ref[...], b_ref[...], 1, 1)
    lane = lax.broadcasted_iota(jnp.int32, (1, LANES), 1)
    for g in range(HEADS // 2):
        at = slice(g * LANES, (g + 1) * LANES)
        pair = x_ref[:, at]
        acc = jnp.where(lane < HEAD_DIM, skip_ref[2 * g], skip_ref[2 * g + 1]) * pair.astype(F32)
        for hh in range(2):
            weights = scores * pair_decay(2 * g + hh, cf, be, cf_row, be_row, row, col)
            acc = acc + dot_left(weights, own_lanes(pair, hh), 1, 0)
        y_ref[:, at] = acc
    m_ref[...] = dot(do_ref[...], w_ref[...], 1, 1) * gain_ref[...]


def outputs(near_ref, m_ref, z_ref, c_ref, df_ref, db_ref, ent_ref, y_ref, sums_ref):
    cf, be, end_f, end_b = columns(df_ref[...], db_ref[...])
    c = c_ref[...]
    entry_f, entry_b = take_slices(ent_ref)
    y = near_ref[...] + spread(jnp.exp(cf)) * dot_right(c, entry_f, 1, 1)
    y = y + spread(jnp.exp(end_b - be)) * dot_right(c, entry_b, 1, 1)
    y_ref[...] = y
    z, m = z_ref[...].astype(F32), m_ref[...]
    u = y * z * jax.nn.sigmoid(z)
    sums = across_rows([jnp.sum(u * u, axis=1, keepdims=True), jnp.sum(u * m, axis=1, keepdims=True)])
    for i in range(sums_ref.shape[0]):
        sums_ref[i, :, :] = sums


def gradients(
    sums_ref, y_ref, m_ref, z_ref, c_ref, df_ref, db_ref, gain_ref, do_ref,
    dy_ref, du_ref, out_ref, *, inner,
):
    total = sums_ref[0, :, :]
    for i in range(1, sums_ref.shape[0]):
        total = total + sums_ref[i, :, :]
    grid = jnp.transpose(jnp.concatenate([total, jnp.zeros((LANES - 8, LANES), F32)], axis=0))
    square = jnp.concatenate([grid[:, 0:1], grid[:, 1:2]], axis=0) / inner
    cross = jnp.concatenate([grid[:, 2:3], grid[:, 3:4]], axis=0) / inner
    q = lax.rsqrt(square + EPS_NORM)
    y, m, z = y_ref[...], m_ref[...], z_ref[...].astype(F32)
    sig = jax.nn.sigmoid(z)
    silu = z * sig
    u = y * z * sig
    normed = (u * q * gain_ref[...]).astype(BF16)
    du = q * m - u * (q * q * q * cross)
    dy = du * silu
    dy_ref[...] = dy
    du_ref[...] = du
    cf, be, end_f, end_b = columns(df_ref[...], db_ref[...])
    c = c_ref[...]
    back_f = dot_left(dy * spread(jnp.exp(cf)), c, 0, 0)
    back_b = dot_left(dy * spread(jnp.exp(end_b - be)), c, 0, 0)
    put_slices(out_ref, back_f, back_b)
    weight = dot(normed, do_ref[...], 0, 0)
    n = out_ref.shape[0]
    size = WIDTH // n
    for i in range(n):
        for block in range(weight.shape[1] // LANES):
            at = 2 * size + block * size
            out_ref[i, at : at + size, :] = weight[
                i * size : (i + 1) * size, block * LANES : (block + 1) * LANES
            ]


def near_gradients(
    skip_ref, x_ref, b_ref, c_ref, df_ref, db_ref, dy_ref, ent_ref, gx_ref, gb_ref, gc_ref
):
    df, db = df_ref[...], db_ref[...]
    cf, be, end_f, end_b = columns(df, db)
    cf_row, be_row = rows(df, db)
    row, col = places()
    b, c, dy = b_ref[...], c_ref[...], dy_ref[...]
    scores = dot(c, b, 1, 1)
    pair_sum = jnp.zeros((FRAMES, FRAMES), F32)
    lane = lax.broadcasted_iota(jnp.int32, (1, LANES), 1)
    for g in range(HEADS // 2):
        at = slice(g * LANES, (g + 1) * LANES)
        acc = jnp.where(lane < HEAD_DIM, skip_ref[2 * g], skip_ref[2 * g + 1]) * dy[:, at]
        for hh in range(2):
            decay = pair_decay(2 * g + hh, cf, be, cf_row, be_row, row, col)
            dy_own = own_lanes(dy[:, at], hh)
            pair_sum = pair_sum + decay * dot_left(dy_own, x_ref[:, at], 1, 1)
            acc = acc + dot_both(scores * decay, dy_own, 0, 0)
        gx_ref[:, at] = acc
    entry_f, entry_b = take_slices(ent_ref)
    rise_f, rise_b = spread(jnp.exp(cf)), spread(jnp.exp(end_b - be))
    grad_c = dot_left(pair_sum, b, 1, 0)
    gc_ref[...] = grad_c + dot_both(dy * rise_f, entry_f, 1, 0) + dot_both(dy * rise_b, entry_b, 1, 0)
    gb_ref[...] = dot_left(pair_sum, c, 0, 0)


def gate_gradient(du_ref, y_ref, z_ref, gz_ref):
    z = z_ref[...].astype(F32)
    sig = jax.nn.sigmoid(z)
    gz_ref[...] = (du_ref[...] * y_ref[...] * sig * (1.0 + z * (1.0 - sig))).astype(BF16)


def finish(core_ref, x_ref, df_ref, db_ref, exit_ref, gb_near, gc_near, keep_ref, give_ref):
    cf, be, end_f, end_b = columns(df_ref[...], db_ref[...])
    x = x_ref[...].astype(F32)
    exit_f, exit_b = take_slices(exit_ref)
    grad_b = gb_near[...] + dot_both(x * spread(jnp.exp(end_f - cf)), exit_f, 1, 0)
    grad_b = grad_b + dot_both(x * spread(jnp.exp(be)), exit_b, 1, 0)
    half = FRAMES // 2
    first = core_ref[0] == 0
    for i, grad in enumerate((grad_b, gc_near[...])):
        at = slice(i * half, (i + 1) * half)
        keep_ref[at, :] = jnp.where(first, grad[:half, :], grad[half:, :])
        give_ref[at, :] = jnp.where(first, grad[half:, :], grad[:half, :])


def finish_x(b_ref, df_ref, db_ref, exit_ref, gx_near, gx_ref):
    cf, be, end_f, end_b = columns(df_ref[...], db_ref[...])
    b = b_ref[...]
    exit_f, exit_b = take_slices(exit_ref)
    gx = gx_near[...] + spread(jnp.exp(end_f - cf)) * dot_right(b, exit_f, 1, 1)
    gx_ref[...] = (gx + spread(jnp.exp(be)) * dot_right(b, exit_b, 1, 1)).astype(BF16)


def add_two(a_ref, b_ref, out_ref):
    out_ref[...] = a_ref[...] + b_ref[...]


def add_four(a_ref, b_ref, c_ref, d_ref, out_ref):
    out_ref[...] = (a_ref[...] + b_ref[...]) + (c_ref[...] + d_ref[...])


def deal_out(core_ref, own_ref, other_ref, gb_ref, gc_ref):
    half = FRAMES // 2
    first = core_ref[0] == 0
    for i, ref in enumerate((gb_ref, gc_ref)):
        at = slice(i * half, (i + 1) * half)
        ref[0:half, :] = jnp.where(first, own_ref[at, :], other_ref[at, :])
        ref[half:, :] = jnp.where(first, other_ref[at, :], own_ref[at, :])


VMEM = pl.BlockSpec(memory_space=pltpu.VMEM)
SMEM = pl.BlockSpec(memory_space=pltpu.SMEM)
HBM = pl.BlockSpec(memory_space=pltpu.MemorySpace.HBM)


def call(kernel, name, out, *args, scalars=0, own=()):
    shapes = [jax.ShapeDtypeStruct(shape, dtype) for shape, dtype in out]
    single = len(shapes) == 1
    return pl.pallas_call(
        kernel,
        name=name,
        out_shape=shapes[0] if single else tuple(shapes),
        in_specs=[SMEM] * scalars + [HBM if own else VMEM] * (len(args) - scalars),
        out_specs=VMEM if single else tuple(VMEM for _ in shapes),
        scratch_shapes=list(own),
        compiler_params=pltpu.CompilerParams(vmem_limit_bytes=48 * 1024 * 1024),
    )(*args)


def exchange(a, axis):
    return lax.all_to_all(a, axis, 0, 0, tiled=True)


def swapped(a, mask, n_h):
    return lax.ppermute(a, "head", [(i, i ^ mask) for i in range(n_h)])


def body(x_in, gate_in, b_in, c_in, decay_fwd, decay_bwd, skip_gain, norm_gain, w_out, d_out):
    n_hi, n_lo, n_x, n_h = (lax.axis_size(axis) for axis in ("z_hi", "z_lo", "x", "head"))
    group = ("z_lo", "x")
    n = n_lo * n_x
    model = d_out.shape[1]
    gain = norm_gain.reshape(1, WIDTH)
    size = WIDTH // n
    weights = size * model // LANES
    place = lax.axis_index("z_hi").astype(jnp.int32).reshape(1)
    decays = (decay_fwd, decay_bwd)
    square = (FRAMES, WIDTH)

    firsts = tuple(pltpu.with_memory_space_constraint(a, pltpu.MemorySpace.HBM) for a in (x_in, b_in, *decays))
    own = [pltpu.VMEM(a.shape, a.dtype) for a in firsts] + [pltpu.SemaphoreType.DMA((4,))]
    sent = call(local_states, "local_states", [((n, 2 * size + 8, LANES), F32)], *firsts, own=own)
    rec1 = exchange(sent, group)
    near, m = call(
        near_outputs, "near_outputs", [(square, F32)] * 2,
        skip_gain, x_in, b_in, c_in, *decays, gain, w_out, d_out, scalars=1,
    )
    sent = call(totals_up, "totals_up", [((n_hi, size + 8, LANES), F32)], place, rec1, scalars=1)
    recz1 = exchange(sent, "z_hi")
    sent = call(entries_up, "entries_up", [((n, 2 * size, LANES), F32)], place, recz1, rec1, scalars=1)
    entries = exchange(sent, group)

    y, sums = call(
        outputs, "outputs", [(square, F32), ((n_h, 8, LANES), F32)],
        near, m, gate_in, c_in, *decays, entries,
    )
    sums = exchange(sums, "head")
    dy, du, sent = call(
        functools.partial(gradients, inner=WIDTH * n_h), "gradients",
        [(square, F32), (square, F32), ((n, 2 * size + weights, LANES), F32)],
        sums, y, m, gate_in, c_in, *decays, gain, d_out,
    )

    rec2 = exchange(sent, group)
    gx_near, gb_near, gc_near = call(
        near_gradients, "near_gradients", [(square, F32)] + [((FRAMES, STATE), F32)] * 2,
        skip_gain, x_in, b_in, c_in, *decays, dy, entries, scalars=1,
    )
    grad_z = call(gate_gradient, "gate_gradient", [(square, BF16)], du, y, gate_in)
    part = weights // n_hi
    sent = call(totals_down, "totals_down", [((n_hi, size + part, LANES), F32)], place, rec1, rec2, scalars=1)
    recz2 = exchange(sent, "z_hi")
    recz2, gx_near, gb_near, gc_near, grad_z = lax.optimization_barrier(
        (recz2, gx_near, gb_near, gc_near, grad_z)
    )
    sent, weight = call(
        entries_down, "entries_down", [((n, 2 * size, LANES), F32), ((n_hi, part, LANES), F32)],
        place, recz1, recz2, rec1, rec2, scalars=1,
    )
    exits = exchange(sent, group)

    exits, weight = lax.optimization_barrier((exits, weight))
    weight = exchange(weight, "z_hi")

    core = (lax.axis_index("head") % 2).astype(jnp.int32).reshape(1)
    half = [((FRAMES, STATE), F32)]
    own, give = call(finish, "finish", half * 2, core, x_in, *decays, exits, gb_near, gc_near, scalars=1)
    own = call(add_two, "add_core", half, own, swapped(give, 1, n_h))
    across = [swapped(own, mask, n_h) for mask in (4, 2)]
    weight, own, *across = lax.optimization_barrier((weight, own, *across))

    weight = call(weight_copy, "weight_copy", [((n, weights, LANES), F32)], weight)
    weight = exchange(weight, group)
    grad_w = call(weight_rows, "weight_rows", [((WIDTH, model), F32)], weight)

    own = call(add_four, "add_y", half, own, across[1], across[0], swapped(own, 6, n_h))
    other = swapped(own, 1, n_h)
    grad_x = call(finish_x, "finish_x", [(square, BF16)], b_in, *decays, exits, gx_near)
    grad_b, grad_c = call(deal_out, "deal_out", half * 2, core, own, other, scalars=1)
    return grad_x, grad_z, grad_b, grad_c, grad_w


def solution(mesh):
    n_seq, n_head = mesh.devices.shape
    n_z = n_seq // HEADS
    n_lo = min(2, n_z // 2)
    split = Mesh(mesh.devices.reshape(n_z // n_lo, n_lo, HEADS, n_head), ("z_hi", "z_lo", "x", "head"))
    seq = ("z_hi", "z_lo", "x")
    in_specs = (
        P(seq, "head"),
        P(seq, "head"),
        P(seq, None),
        P(seq, None),
        P("head", seq),
        P("head", seq),
        P("head"),
        P("head"),
        P("head", None),
        P(seq, None),
    )
    out_specs = (
        P(seq, "head"),
        P(seq, "head"),
        P(seq, None),
        P(seq, None),
        P("head", None),
    )
    return jax.shard_map(body, mesh=split, in_specs=in_specs, out_specs=out_specs, check_vma=False)
```

```python
import functools

import jax
import jax.numpy as jnp
from jax import lax
from jax.experimental import pallas as pl
from jax.experimental.pallas import tpu as pltpu
from jax.sharding import Mesh, PartitionSpec as P

HEADS = 4
HEAD_DIM = 64
STATE = 128
FRAMES = 256
WIDTH = HEADS * HEAD_DIM
LANES = 128
EPS_NORM = 1e-05
WEIGHT_SCALE = 0.0078125
F32, BF16 = jnp.float32, jnp.bfloat16


def dot(a, b, ca, cb):
    return lax.dot_general(a, b, (((ca,), (cb,)), ((), ())), preferred_element_type=F32)


def halves(a):
    high = a.astype(BF16)
    return high, (a - high.astype(F32)).astype(BF16)


def dot_left(a, b, ca, cb):
    ah, al = halves(a)
    return dot(ah, b, ca, cb) + dot(al, b, ca, cb)


def dot_right(a, b, ca, cb):
    bh, bl = halves(b)
    return dot(a, bh, ca, cb) + dot(a, bl, ca, cb)


def dot_both(a, b, ca, cb):
    ah, al = halves(a)
    bh, bl = halves(b)
    return dot(ah, bh, ca, cb) + (dot(ah, bl, ca, cb) + dot(al, bh, ca, cb))


def dot_exact(a, b, ca, cb):
    return lax.dot_general(
        a, b, (((ca,), (cb,)), ((), ())), precision=lax.Precision.HIGHEST, preferred_element_type=F32
    )


def places():
    row = lax.broadcasted_iota(jnp.int32, (FRAMES, FRAMES), 0)
    col = lax.broadcasted_iota(jnp.int32, (FRAMES, FRAMES), 1)
    return row, col


def columns(df, db):
    row, col = places()
    upto = (col <= row).astype(F32)
    before = (col < row).astype(F32)
    cf = dot_exact(upto, df, 1, 1)
    be = dot_exact(before, db, 1, 1)
    end_f = cf[FRAMES - 1 :, :]
    end_b = dot_exact(jnp.ones((8, FRAMES), F32), db, 1, 1)[:1, :]
    return cf, be, end_f, end_b


def rows(df, db):
    row, col = places()
    upto = (row <= col).astype(F32)
    before = (row < col).astype(F32)
    return dot_exact(df, upto, 1, 0), dot_exact(db, before, 1, 0)


def spread(cols):
    lane = lax.broadcasted_iota(jnp.int32, (cols.shape[0], LANES), 1)
    pairs = [
        jnp.where(lane < HEAD_DIM, cols[:, 2 * g : 2 * g + 1], cols[:, 2 * g + 1 : 2 * g + 2])
        for g in range(HEADS // 2)
    ]
    return jnp.concatenate(pairs, axis=1)


def pair_decay(h, cf, be, cf_row, be_row, row, col):
    gap = jnp.where(
        row > col,
        cf[:, h : h + 1] - cf_row[h : h + 1, :],
        be_row[h : h + 1, :] - be[:, h : h + 1],
    )
    return jnp.where(row == col, 2.0, jnp.exp(jnp.minimum(gap, 0.0)))


def own_lanes(pair, hh):
    lane = lax.broadcasted_iota(jnp.int32, pair.shape, 1)
    mine = lane < HEAD_DIM if hh == 0 else lane >= HEAD_DIM
    return jnp.where(mine, pair, jnp.zeros_like(pair))


def put_slices(out_ref, forward, backward):
    n = out_ref.shape[0]
    size = WIDTH // n
    for i in range(n):
        at = slice(i * size, (i + 1) * size)
        out_ref[i, 0:size, :] = forward[at, :]
        out_ref[i, size : 2 * size, :] = backward[at, :]


def take_slices(ref):
    n = ref.shape[0]
    size = WIDTH // n
    forward = jnp.concatenate([ref[i, 0:size, :] for i in range(n)], axis=0)
    backward = jnp.concatenate([ref[i, size : 2 * size, :] for i in range(n)], axis=0)
    return forward, backward


def local_states(x_hbm, b_hbm, df_hbm, db_hbm, out_ref, x_ref, b_ref, df_ref, db_ref, sems):
    sources, targets = (x_hbm, b_hbm, df_hbm, db_hbm), (x_ref, b_ref, df_ref, db_ref)
    copies = [pltpu.make_async_copy(s, t, sems.at[i]) for i, (s, t) in enumerate(zip(sources, targets))]
    for copy in copies[::-1]:
        copy.start()
    copies[2].wait()
    copies[3].wait()
    cf, be, end_f, end_b = columns(df_ref[...], db_ref[...])
    copies[0].wait()
    copies[1].wait()
    x = x_ref[...].astype(F32)
    b = b_ref[...]
    state_f = dot_left(x * spread(jnp.exp(end_f - cf)), b, 0, 0)
    state_b = dot_left(x * spread(jnp.exp(be)), b, 0, 0)
    put_slices(out_ref, state_f, state_b)
    n = out_ref.shape[0]
    size = WIDTH // n
    total_f, total_b = jnp.exp(end_f), jnp.exp(end_b)
    half = lax.broadcasted_iota(jnp.int32, (8, LANES), 0) < 4
    for j in range(HEADS):
        both = jnp.where(half, total_f[:, j : j + 1], total_b[:, j : j + 1])
        for i in range(j * n // HEADS, (j + 1) * n // HEADS):
            out_ref[i, 2 * size :, :] = both


def totals_at(ref, i, start):
    return ref[i, start : start + 1, :], ref[i, start + 4 : start + 5, :]


def sliced(ref, i, size):
    return ref[i, 0:size, :], ref[i, size : 2 * size, :]


def group_sums(dec_ref, rec_ref, forward_up):
    n = rec_ref.shape[0]
    size = WIDTH // n
    decays = [totals_at(dec_ref, i, 2 * size) for i in range(n)]
    parts = [sliced(rec_ref, i, size) for i in range(n)]
    sums = []
    for branch, up in enumerate((forward_up, not forward_up)):
        order = list(range(n)) if up else list(range(n))[::-1]
        acc = parts[order[0]][branch]
        for i in order[1:]:
            acc = decays[i][branch] * acc + parts[i][branch]
        sums.append(acc)
    return sums, decays


def totals_up(place_ref, rec_ref, out_ref):
    size = WIDTH // rec_ref.shape[0]
    (sum_f, sum_b), decays = group_sums(rec_ref, rec_ref, True)
    all_f, all_b = decays[0]
    for dec_f, dec_b in decays[1:]:
        all_f, all_b = all_f * dec_f, all_b * dec_b
    half = lax.broadcasted_iota(jnp.int32, (8, LANES), 0) < 4
    for k in range(out_ref.shape[0]):
        out_ref[k, 0:size, :] = jnp.where(place_ref[0] < k, sum_f, sum_b)
        out_ref[k, size:, :] = jnp.where(half, all_f, all_b)


def entries_up(place_ref, zrec_ref, rec_ref, out_ref):
    n_g, n = zrec_ref.shape[0], rec_ref.shape[0]
    size = WIDTH // n
    place = place_ref[0]
    for branch, up in enumerate((True, False)):
        entry = jnp.zeros((size, LANES), F32)
        for k in list(range(n_g)) if up else list(range(n_g))[::-1]:
            passed = place > k if up else place < k
            after = totals_at(zrec_ref, k, size)[branch] * entry + zrec_ref[k, 0:size, :]
            entry = jnp.where(passed, after, entry)
        put_entries(out_ref, branch, up, entry, rec_ref, rec_ref)


def put_entries(out_ref, branch, up, entry, dec_ref, rec_ref):
    n = rec_ref.shape[0]
    size = WIDTH // n
    for i in list(range(n)) if up else list(range(n))[::-1]:
        out_ref[i, branch * size : (branch + 1) * size, :] = entry
        entry = totals_at(dec_ref, i, 2 * size)[branch] * entry + sliced(rec_ref, i, size)[branch]


def totals_down(place_ref, dec_ref, rec_ref, out_ref):
    n, n_g = rec_ref.shape[0], out_ref.shape[0]
    size = WIDTH // n
    (sum_f, sum_b), _ = group_sums(dec_ref, rec_ref, False)
    weight = rec_ref[0, 2 * size :, :]
    for i in range(1, n):
        weight = weight + rec_ref[i, 2 * size :, :]
    part = weight.shape[0] // n_g
    for k in range(n_g):
        out_ref[k, 0:size, :] = jnp.where(place_ref[0] > k, sum_f, sum_b)
        out_ref[k, size:, :] = weight[k * part : (k + 1) * part, :]


def entries_down(place_ref, zdec_ref, zrec_ref, dec_ref, rec_ref, out_ref, w_ref):
    n_g, n = zrec_ref.shape[0], rec_ref.shape[0]
    size = WIDTH // n
    place = place_ref[0]
    for branch, up in enumerate((False, True)):
        entry = jnp.zeros((size, LANES), F32)
        for k in list(range(n_g)) if up else list(range(n_g))[::-1]:
            passed = place > k if up else place < k
            after = totals_at(zdec_ref, k, size)[branch] * entry + zrec_ref[k, 0:size, :]
            entry = jnp.where(passed, after, entry)
        put_entries(out_ref, branch, up, entry, dec_ref, rec_ref)
    weight = zrec_ref[0, size:, :]
    for k in range(1, n_g):
        weight = weight + zrec_ref[k, size:, :]
    for k in range(n_g):
        w_ref[k, :, :] = weight


def weight_copy(rec_ref, out_ref):
    n_g, part = rec_ref.shape[0], rec_ref.shape[1]
    for k in range(n_g):
        rows = rec_ref[k, :, :]
        for i in range(out_ref.shape[0]):
            out_ref[i, k * part : (k + 1) * part, :] = rows


def weight_rows(rec_ref, gw_ref):
    n = rec_ref.shape[0]
    size = WIDTH // n
    for i in range(n):
        for block in range(gw_ref.shape[1] // LANES):
            gw_ref[i * size : (i + 1) * size, block * LANES : (block + 1) * LANES] = (
                rec_ref[i, block * size : (block + 1) * size, :] * WEIGHT_SCALE
            )


def across_rows(cols):
    lane = lax.broadcasted_iota(jnp.int32, (LANES, LANES), 1)
    grid = jnp.zeros((LANES, LANES), F32)
    for i, col in enumerate(cols):
        for part in range(FRAMES // LANES):
            at = i * (FRAMES // LANES) + part
            grid = jnp.where(lane == at, col[part * LANES : (part + 1) * LANES, :], grid)
    return jnp.transpose(grid)[0:8, :]


def near_outputs(
    skip_ref, x_ref, b_ref, c_ref, df_ref, db_ref, gain_ref, w_ref, do_ref, y_ref, m_ref
):
    df, db = df_ref[...], db_ref[...]
    cf, be, end_f, end_b = columns(df, db)
    cf_row, be_row = rows(df, db)
    row, col = places()
    scores = dot(c_ref[...], b_ref[...], 1, 1)
    lane = lax.broadcasted_iota(jnp.int32, (1, LANES), 1)
    for g in range(HEADS // 2):
        at = slice(g * LANES, (g + 1) * LANES)
        pair = x_ref[:, at]
        acc = jnp.where(lane < HEAD_DIM, skip_ref[2 * g], skip_ref[2 * g + 1]) * pair.astype(F32)
        for hh in range(2):
            weights = scores * pair_decay(2 * g + hh, cf, be, cf_row, be_row, row, col)
            acc = acc + dot_left(weights, own_lanes(pair, hh), 1, 0)
        y_ref[:, at] = acc
    m_ref[...] = dot(do_ref[...], w_ref[...], 1, 1) * gain_ref[...]


def outputs(near_ref, m_ref, z_ref, c_ref, df_ref, db_ref, ent_ref, y_ref, sums_ref):
    cf, be, end_f, end_b = columns(df_ref[...], db_ref[...])
    c = c_ref[...]
    entry_f, entry_b = take_slices(ent_ref)
    y = near_ref[...] + spread(jnp.exp(cf)) * dot_right(c, entry_f, 1, 1)
    y = y + spread(jnp.exp(end_b - be)) * dot_right(c, entry_b, 1, 1)
    y_ref[...] = y
    z, m = z_ref[...].astype(F32), m_ref[...]
    u = y * z * jax.nn.sigmoid(z)
    sums = across_rows([jnp.sum(u * u, axis=1, keepdims=True), jnp.sum(u * m, axis=1, keepdims=True)])
    for i in range(sums_ref.shape[0]):
        sums_ref[i, :, :] = sums


def gradients(
    sums_ref, y_ref, m_ref, z_ref, c_ref, df_ref, db_ref, gain_ref, do_ref,
    dy_ref, du_ref, out_ref, *, inner,
):
    total = sums_ref[0, :, :]
    for i in range(1, sums_ref.shape[0]):
        total = total + sums_ref[i, :, :]
    grid = jnp.transpose(jnp.concatenate([total, jnp.zeros((LANES - 8, LANES), F32)], axis=0))
    square = jnp.concatenate([grid[:, 0:1], grid[:, 1:2]], axis=0) / inner
    cross = jnp.concatenate([grid[:, 2:3], grid[:, 3:4]], axis=0) / inner
    q = lax.rsqrt(square + EPS_NORM)
    y, m, z = y_ref[...], m_ref[...], z_ref[...].astype(F32)
    sig = jax.nn.sigmoid(z)
    silu = z * sig
    u = y * z * sig
    normed = (u * q * gain_ref[...]).astype(BF16)
    du = q * m - u * (q * q * q * cross)
    dy = du * silu
    dy_ref[...] = dy
    du_ref[...] = du
    cf, be, end_f, end_b = columns(df_ref[...], db_ref[...])
    c = c_ref[...]
    back_f = dot_left(dy * spread(jnp.exp(cf)), c, 0, 0)
    back_b = dot_left(dy * spread(jnp.exp(end_b - be)), c, 0, 0)
    put_slices(out_ref, back_f, back_b)
    weight = dot(normed, do_ref[...], 0, 0)
    n = out_ref.shape[0]
    size = WIDTH // n
    for i in range(n):
        for block in range(weight.shape[1] // LANES):
            at = 2 * size + block * size
            out_ref[i, at : at + size, :] = weight[
                i * size : (i + 1) * size, block * LANES : (block + 1) * LANES
            ]


def near_gradients(
    skip_ref, x_ref, b_ref, c_ref, df_ref, db_ref, dy_ref, ent_ref, gx_ref, gb_ref, gc_ref
):
    df, db = df_ref[...], db_ref[...]
    cf, be, end_f, end_b = columns(df, db)
    cf_row, be_row = rows(df, db)
    row, col = places()
    b, c, dy = b_ref[...], c_ref[...], dy_ref[...]
    scores = dot(c, b, 1, 1)
    pair_sum = jnp.zeros((FRAMES, FRAMES), F32)
    lane = lax.broadcasted_iota(jnp.int32, (1, LANES), 1)
    for g in range(HEADS // 2):
        at = slice(g * LANES, (g + 1) * LANES)
        acc = jnp.where(lane < HEAD_DIM, skip_ref[2 * g], skip_ref[2 * g + 1]) * dy[:, at]
        for hh in range(2):
            decay = pair_decay(2 * g + hh, cf, be, cf_row, be_row, row, col)
            dy_own = own_lanes(dy[:, at], hh)
            pair_sum = pair_sum + decay * dot_left(dy_own, x_ref[:, at], 1, 1)
            acc = acc + dot_both(scores * decay, dy_own, 0, 0)
        gx_ref[:, at] = acc
    entry_f, entry_b = take_slices(ent_ref)
    rise_f, rise_b = spread(jnp.exp(cf)), spread(jnp.exp(end_b - be))
    grad_c = dot_left(pair_sum, b, 1, 0)
    gc_ref[...] = grad_c + dot_both(dy * rise_f, entry_f, 1, 0) + dot_both(dy * rise_b, entry_b, 1, 0)
    gb_ref[...] = dot_left(pair_sum, c, 0, 0)


def gate_gradient(du_ref, y_ref, z_ref, gz_ref):
    z = z_ref[...].astype(F32)
    sig = jax.nn.sigmoid(z)
    gz_ref[...] = (du_ref[...] * y_ref[...] * sig * (1.0 + z * (1.0 - sig))).astype(BF16)


def finish(core_ref, x_ref, df_ref, db_ref, exit_ref, gb_near, gc_near, keep_ref, give_ref):
    cf, be, end_f, end_b = columns(df_ref[...], db_ref[...])
    x = x_ref[...].astype(F32)
    exit_f, exit_b = take_slices(exit_ref)
    grad_b = gb_near[...] + dot_both(x * spread(jnp.exp(end_f - cf)), exit_f, 1, 0)
    grad_b = grad_b + dot_both(x * spread(jnp.exp(be)), exit_b, 1, 0)
    half = FRAMES // 2
    first = core_ref[0] == 0
    for i, grad in enumerate((grad_b, gc_near[...])):
        at = slice(i * half, (i + 1) * half)
        keep_ref[at, :] = jnp.where(first, grad[:half, :], grad[half:, :])
        give_ref[at, :] = jnp.where(first, grad[half:, :], grad[:half, :])


def finish_x(b_ref, df_ref, db_ref, exit_ref, gx_near, gx_ref):
    cf, be, end_f, end_b = columns(df_ref[...], db_ref[...])
    b = b_ref[...]
    exit_f, exit_b = take_slices(exit_ref)
    gx = gx_near[...] + spread(jnp.exp(end_f - cf)) * dot_right(b, exit_f, 1, 1)
    gx_ref[...] = (gx + spread(jnp.exp(be)) * dot_right(b, exit_b, 1, 1)).astype(BF16)


def add_two(a_ref, b_ref, out_ref):
    out_ref[...] = a_ref[...] + b_ref[...]


def deal_out(core_ref, own_ref, other_ref, gb_ref, gc_ref):
    half = FRAMES // 2
    first = core_ref[0] == 0
    for i, ref in enumerate((gb_ref, gc_ref)):
        at = slice(i * half, (i + 1) * half)
        ref[0:half, :] = jnp.where(first, own_ref[at, :], other_ref[at, :])
        ref[half:, :] = jnp.where(first, other_ref[at, :], own_ref[at, :])


VMEM = pl.BlockSpec(memory_space=pltpu.VMEM)
SMEM = pl.BlockSpec(memory_space=pltpu.SMEM)
HBM = pl.BlockSpec(memory_space=pltpu.MemorySpace.HBM)


def call(kernel, name, out, *args, scalars=0, own=()):
    shapes = [jax.ShapeDtypeStruct(shape, dtype) for shape, dtype in out]
    single = len(shapes) == 1
    return pl.pallas_call(
        kernel,
        name=name,
        out_shape=shapes[0] if single else tuple(shapes),
        in_specs=[SMEM] * scalars + [HBM if own else VMEM] * (len(args) - scalars),
        out_specs=VMEM if single else tuple(VMEM for _ in shapes),
        scratch_shapes=list(own),
        compiler_params=pltpu.CompilerParams(vmem_limit_bytes=48 * 1024 * 1024),
    )(*args)


def exchange(a, axis):
    return lax.all_to_all(a, axis, 0, 0, tiled=True)


def swapped(a, mask, n_h):
    return lax.ppermute(a, "head", [(i, i ^ mask) for i in range(n_h)])


def body(x_in, gate_in, b_in, c_in, decay_fwd, decay_bwd, skip_gain, norm_gain, w_out, d_out):
    n_hi, n_lo, n_x, n_h = (lax.axis_size(axis) for axis in ("z_hi", "z_lo", "x", "head"))
    group = ("z_lo", "x")
    n = n_lo * n_x
    model = d_out.shape[1]
    gain = norm_gain.reshape(1, WIDTH)
    size = WIDTH // n
    weights = size * model // LANES
    place = lax.axis_index("z_hi").astype(jnp.int32).reshape(1)
    decays = (decay_fwd, decay_bwd)
    square = (FRAMES, WIDTH)

    firsts = tuple(pltpu.with_memory_space_constraint(a, pltpu.MemorySpace.HBM) for a in (x_in, b_in, *decays))
    own = [pltpu.VMEM(a.shape, a.dtype) for a in firsts] + [pltpu.SemaphoreType.DMA((4,))]
    sent = call(local_states, "local_states", [((n, 2 * size + 8, LANES), F32)], *firsts, own=own)
    rec1 = exchange(sent, group)
    near, m = call(
        near_outputs, "near_outputs", [(square, F32)] * 2,
        skip_gain, x_in, b_in, c_in, *decays, gain, w_out, d_out, scalars=1,
    )
    sent = call(totals_up, "totals_up", [((n_hi, size + 8, LANES), F32)], place, rec1, scalars=1)
    recz1 = exchange(sent, "z_hi")
    sent = call(entries_up, "entries_up", [((n, 2 * size, LANES), F32)], place, recz1, rec1, scalars=1)
    entries = exchange(sent, group)

    y, sums = call(
        outputs, "outputs", [(square, F32), ((n_h, 8, LANES), F32)],
        near, m, gate_in, c_in, *decays, entries,
    )
    sums = exchange(sums, "head")
    dy, du, sent = call(
        functools.partial(gradients, inner=WIDTH * n_h), "gradients",
        [(square, F32), (square, F32), ((n, 2 * size + weights, LANES), F32)],
        sums, y, m, gate_in, c_in, *decays, gain, d_out,
    )

    rec2 = exchange(sent, group)
    gx_near, gb_near, gc_near = call(
        near_gradients, "near_gradients", [(square, F32)] + [((FRAMES, STATE), F32)] * 2,
        skip_gain, x_in, b_in, c_in, *decays, dy, entries, scalars=1,
    )
    grad_z = call(gate_gradient, "gate_gradient", [(square, BF16)], du, y, gate_in)
    rec2, gx_near, gb_near, gc_near, grad_z = lax.optimization_barrier(
        (rec2, gx_near, gb_near, gc_near, grad_z)
    )
    part = weights // n_hi
    sent = call(totals_down, "totals_down", [((n_hi, size + part, LANES), F32)], place, rec1, rec2, scalars=1)
    recz2 = exchange(sent, "z_hi")
    sent, weight = call(
        entries_down, "entries_down", [((n, 2 * size, LANES), F32), ((n_hi, part, LANES), F32)],
        place, recz1, recz2, rec1, rec2, scalars=1,
    )
    exits = exchange(sent, group)

    exits, weight = lax.optimization_barrier((exits, weight))
    weight = exchange(weight, "z_hi")

    core = (lax.axis_index("head") % 2).astype(jnp.int32).reshape(1)
    half = [((FRAMES, STATE), F32)]
    own, give = call(finish, "finish", half * 2, core, x_in, *decays, exits, gb_near, gc_near, scalars=1)
    own = call(add_two, "add_core", half, own, swapped(give, 1, n_h))
    own = call(add_two, "add_y", half, own, swapped(own, 2, n_h))
    weight, own = lax.optimization_barrier((weight, own))

    weight = call(weight_copy, "weight_copy", [((n, weights, LANES), F32)], weight)
    weight = exchange(weight, group)
    grad_w = call(weight_rows, "weight_rows", [((WIDTH, model), F32)], weight)

    own = call(add_two, "add_y", half, own, swapped(own, 6, n_h))
    other = swapped(own, 1, n_h)
    grad_x = call(finish_x, "finish_x", [(square, BF16)], b_in, *decays, exits, gx_near)
    grad_b, grad_c = call(deal_out, "deal_out", half * 2, core, own, other, scalars=1)
    return grad_x, grad_z, grad_b, grad_c, grad_w


def solution(mesh):
    n_seq, n_head = mesh.devices.shape
    n_z = n_seq // HEADS
    n_lo = min(2, n_z // 2)
    split = Mesh(mesh.devices.reshape(n_z // n_lo, n_lo, HEADS, n_head), ("z_hi", "z_lo", "x", "head"))
    seq = ("z_hi", "z_lo", "x")
    in_specs = (
        P(seq, "head"),
        P(seq, "head"),
        P(seq, None),
        P(seq, None),
        P("head", seq),
        P("head", seq),
        P("head"),
        P("head"),
        P("head", None),
        P(seq, None),
    )
    out_specs = (
        P(seq, "head"),
        P(seq, "head"),
        P(seq, None),
        P(seq, None),
        P("head", None),
    )
    return jax.shard_map(body, mesh=split, in_specs=in_specs, out_specs=out_specs, check_vma=False)
```

```python
import functools

import jax
import jax.numpy as jnp
from jax import lax
from jax.experimental import pallas as pl
from jax.experimental.pallas import tpu as pltpu
from jax.sharding import Mesh, PartitionSpec as P

HEADS = 4
HEAD_DIM = 64
STATE = 128
FRAMES = 256
WIDTH = HEADS * HEAD_DIM
LANES = 128
EPS_NORM = 1e-05
WEIGHT_SCALE = 0.0078125
F32, BF16 = jnp.float32, jnp.bfloat16


def dot(a, b, ca, cb):
    return lax.dot_general(a, b, (((ca,), (cb,)), ((), ())), preferred_element_type=F32)


def halves(a):
    high = a.astype(BF16)
    return high, (a - high.astype(F32)).astype(BF16)


def dot_left(a, b, ca, cb):
    ah, al = halves(a)
    return dot(ah, b, ca, cb) + dot(al, b, ca, cb)


def dot_right(a, b, ca, cb):
    bh, bl = halves(b)
    return dot(a, bh, ca, cb) + dot(a, bl, ca, cb)


def dot_both(a, b, ca, cb):
    ah, al = halves(a)
    bh, bl = halves(b)
    return dot(ah, bh, ca, cb) + (dot(ah, bl, ca, cb) + dot(al, bh, ca, cb))


def dot_exact(a, b, ca, cb):
    return lax.dot_general(
        a, b, (((ca,), (cb,)), ((), ())), precision=lax.Precision.HIGHEST, preferred_element_type=F32
    )


def places():
    row = lax.broadcasted_iota(jnp.int32, (FRAMES, FRAMES), 0)
    col = lax.broadcasted_iota(jnp.int32, (FRAMES, FRAMES), 1)
    return row, col


def columns(df, db):
    row, col = places()
    upto = (col <= row).astype(F32)
    before = (col < row).astype(F32)
    cf = dot_exact(upto, df, 1, 1)
    be = dot_exact(before, db, 1, 1)
    end_f = cf[FRAMES - 1 :, :]
    end_b = dot_exact(jnp.ones((8, FRAMES), F32), db, 1, 1)[:1, :]
    return cf, be, end_f, end_b


def rows(df, db):
    row, col = places()
    upto = (row <= col).astype(F32)
    before = (row < col).astype(F32)
    return dot_exact(df, upto, 1, 0), dot_exact(db, before, 1, 0)


def spread(cols):
    lane = lax.broadcasted_iota(jnp.int32, (cols.shape[0], LANES), 1)
    pairs = [
        jnp.where(lane < HEAD_DIM, cols[:, 2 * g : 2 * g + 1], cols[:, 2 * g + 1 : 2 * g + 2])
        for g in range(HEADS // 2)
    ]
    return jnp.concatenate(pairs, axis=1)


def pair_decay(h, cf, be, cf_row, be_row, row, col):
    gap = jnp.where(
        row > col,
        cf[:, h : h + 1] - cf_row[h : h + 1, :],
        be_row[h : h + 1, :] - be[:, h : h + 1],
    )
    return jnp.where(row == col, 2.0, jnp.exp(jnp.minimum(gap, 0.0)))


def own_lanes(pair, hh):
    lane = lax.broadcasted_iota(jnp.int32, pair.shape, 1)
    mine = lane < HEAD_DIM if hh == 0 else lane >= HEAD_DIM
    return jnp.where(mine, pair, jnp.zeros_like(pair))


def put_slices(out_ref, forward, backward):
    n = out_ref.shape[0]
    size = WIDTH // n
    for i in range(n):
        at = slice(i * size, (i + 1) * size)
        out_ref[i, 0:size, :] = forward[at, :]
        out_ref[i, size : 2 * size, :] = backward[at, :]


def take_slices(ref):
    n = ref.shape[0]
    size = WIDTH // n
    forward = jnp.concatenate([ref[i, 0:size, :] for i in range(n)], axis=0)
    backward = jnp.concatenate([ref[i, size : 2 * size, :] for i in range(n)], axis=0)
    return forward, backward


def local_states(_, x_hbm, b_hbm, df_hbm, db_hbm, out_ref, x_ref, b_ref, df_ref, db_ref, sems):
    sources, targets = (x_hbm, b_hbm, df_hbm, db_hbm), (x_ref, b_ref, df_ref, db_ref)
    copies = [pltpu.make_async_copy(s, t, sems.at[i]) for i, (s, t) in enumerate(zip(sources, targets))]
    for copy in copies[::-1]:
        copy.start()
    copies[2].wait()
    copies[3].wait()
    cf, be, end_f, end_b = columns(df_ref[...], db_ref[...])
    copies[0].wait()
    copies[1].wait()
    x = x_ref[...].astype(F32)
    b = b_ref[...]
    state_f = dot_left(x * spread(jnp.exp(end_f - cf)), b, 0, 0)
    state_b = dot_left(x * spread(jnp.exp(be)), b, 0, 0)
    put_slices(out_ref, state_f, state_b)
    n = out_ref.shape[0]
    size = WIDTH // n
    total_f, total_b = jnp.exp(end_f), jnp.exp(end_b)
    half = lax.broadcasted_iota(jnp.int32, (8, LANES), 0) < 4
    for j in range(HEADS):
        both = jnp.where(half, total_f[:, j : j + 1], total_b[:, j : j + 1])
        for i in range(j * n // HEADS, (j + 1) * n // HEADS):
            out_ref[i, 2 * size :, :] = both


def totals_at(ref, i, start):
    return ref[i, start : start + 1, :], ref[i, start + 4 : start + 5, :]


def sliced(ref, i, size):
    return ref[i, 0:size, :], ref[i, size : 2 * size, :]


def group_sums(dec_ref, rec_ref, forward_up):
    n = rec_ref.shape[0]
    size = WIDTH // n
    decays = [totals_at(dec_ref, i, 2 * size) for i in range(n)]
    parts = [sliced(rec_ref, i, size) for i in range(n)]
    sums = []
    for branch, up in enumerate((forward_up, not forward_up)):
        order = list(range(n)) if up else list(range(n))[::-1]
        acc = parts[order[0]][branch]
        for i in order[1:]:
            acc = decays[i][branch] * acc + parts[i][branch]
        sums.append(acc)
    return sums, decays


def totals_up(place_ref, rec_ref, out_ref):
    size = WIDTH // rec_ref.shape[0]
    (sum_f, sum_b), decays = group_sums(rec_ref, rec_ref, True)
    all_f, all_b = decays[0]
    for dec_f, dec_b in decays[1:]:
        all_f, all_b = all_f * dec_f, all_b * dec_b
    half = lax.broadcasted_iota(jnp.int32, (8, LANES), 0) < 4
    for k in range(out_ref.shape[0]):
        out_ref[k, 0:size, :] = jnp.where(place_ref[0] < k, sum_f, sum_b)
        out_ref[k, size:, :] = jnp.where(half, all_f, all_b)


def entries_up(place_ref, zrec_ref, rec_ref, out_ref):
    n_g, n = zrec_ref.shape[0], rec_ref.shape[0]
    size = WIDTH // n
    place = place_ref[0]
    for branch, up in enumerate((True, False)):
        entry = jnp.zeros((size, LANES), F32)
        for k in list(range(n_g)) if up else list(range(n_g))[::-1]:
            passed = place > k if up else place < k
            after = totals_at(zrec_ref, k, size)[branch] * entry + zrec_ref[k, 0:size, :]
            entry = jnp.where(passed, after, entry)
        put_entries(out_ref, branch, up, entry, rec_ref, rec_ref)


def put_entries(out_ref, branch, up, entry, dec_ref, rec_ref):
    n = rec_ref.shape[0]
    size = WIDTH // n
    for i in list(range(n)) if up else list(range(n))[::-1]:
        out_ref[i, branch * size : (branch + 1) * size, :] = entry
        entry = totals_at(dec_ref, i, 2 * size)[branch] * entry + sliced(rec_ref, i, size)[branch]


def totals_down(place_ref, dec_ref, rec_ref, out_ref):
    n, n_g = rec_ref.shape[0], out_ref.shape[0]
    size = WIDTH // n
    (sum_f, sum_b), _ = group_sums(dec_ref, rec_ref, False)
    weight = rec_ref[0, 2 * size :, :]
    for i in range(1, n):
        weight = weight + rec_ref[i, 2 * size :, :]
    part = weight.shape[0] // n_g
    for k in range(n_g):
        out_ref[k, 0:size, :] = jnp.where(place_ref[0] > k, sum_f, sum_b)
        out_ref[k, size:, :] = weight[k * part : (k + 1) * part, :]


def entries_down(place_ref, zdec_ref, zrec_ref, dec_ref, rec_ref, out_ref, w_ref):
    n_g, n = zrec_ref.shape[0], rec_ref.shape[0]
    size = WIDTH // n
    place = place_ref[0]
    for branch, up in enumerate((False, True)):
        entry = jnp.zeros((size, LANES), F32)
        for k in list(range(n_g)) if up else list(range(n_g))[::-1]:
            passed = place > k if up else place < k
            after = totals_at(zdec_ref, k, size)[branch] * entry + zrec_ref[k, 0:size, :]
            entry = jnp.where(passed, after, entry)
        put_entries(out_ref, branch, up, entry, dec_ref, rec_ref)
    weight = zrec_ref[0, size:, :]
    for k in range(1, n_g):
        weight = weight + zrec_ref[k, size:, :]
    for k in range(n_g):
        w_ref[k, :, :] = weight


def weight_copy(rec_ref, out_ref):
    n_g, part = rec_ref.shape[0], rec_ref.shape[1]
    for k in range(n_g):
        rows = rec_ref[k, :, :]
        for i in range(out_ref.shape[0]):
            out_ref[i, k * part : (k + 1) * part, :] = rows


def weight_rows(rec_ref, gw_ref):
    n = rec_ref.shape[0]
    size = WIDTH // n
    for i in range(n):
        for block in range(gw_ref.shape[1] // LANES):
            gw_ref[i * size : (i + 1) * size, block * LANES : (block + 1) * LANES] = (
                rec_ref[i, block * size : (block + 1) * size, :] * WEIGHT_SCALE
            )


def across_rows(cols):
    lane = lax.broadcasted_iota(jnp.int32, (LANES, LANES), 1)
    grid = jnp.zeros((LANES, LANES), F32)
    for i, col in enumerate(cols):
        for part in range(FRAMES // LANES):
            at = i * (FRAMES // LANES) + part
            grid = jnp.where(lane == at, col[part * LANES : (part + 1) * LANES, :], grid)
    return jnp.transpose(grid)[0:8, :]


def near_outputs(
    skip_ref, x_ref, b_ref, c_ref, df_ref, db_ref, gain_ref, w_ref, do_ref, y_ref, m_ref
):
    df, db = df_ref[...], db_ref[...]
    cf, be, end_f, end_b = columns(df, db)
    cf_row, be_row = rows(df, db)
    row, col = places()
    scores = dot(c_ref[...], b_ref[...], 1, 1)
    lane = lax.broadcasted_iota(jnp.int32, (1, LANES), 1)
    for g in range(HEADS // 2):
        at = slice(g * LANES, (g + 1) * LANES)
        pair = x_ref[:, at]
        acc = jnp.where(lane < HEAD_DIM, skip_ref[2 * g], skip_ref[2 * g + 1]) * pair.astype(F32)
        for hh in range(2):
            weights = scores * pair_decay(2 * g + hh, cf, be, cf_row, be_row, row, col)
            acc = acc + dot_left(weights, own_lanes(pair, hh), 1, 0)
        y_ref[:, at] = acc
    m_ref[...] = dot(do_ref[...], w_ref[...], 1, 1) * gain_ref[...]


def outputs(near_ref, m_ref, z_ref, c_ref, df_ref, db_ref, ent_ref, y_ref, sums_ref):
    cf, be, end_f, end_b = columns(df_ref[...], db_ref[...])
    c = c_ref[...]
    entry_f, entry_b = take_slices(ent_ref)
    y = near_ref[...] + spread(jnp.exp(cf)) * dot_right(c, entry_f, 1, 1)
    y = y + spread(jnp.exp(end_b - be)) * dot_right(c, entry_b, 1, 1)
    y_ref[...] = y
    z, m = z_ref[...].astype(F32), m_ref[...]
    u = y * z * jax.nn.sigmoid(z)
    sums = across_rows([jnp.sum(u * u, axis=1, keepdims=True), jnp.sum(u * m, axis=1, keepdims=True)])
    for i in range(sums_ref.shape[0]):
        sums_ref[i, :, :] = sums


def gradients(
    sums_ref, y_ref, m_ref, z_ref, c_ref, df_ref, db_ref, gain_ref, do_ref,
    dy_ref, du_ref, out_ref, *, inner,
):
    total = sums_ref[0, :, :]
    for i in range(1, sums_ref.shape[0]):
        total = total + sums_ref[i, :, :]
    grid = jnp.transpose(jnp.concatenate([total, jnp.zeros((LANES - 8, LANES), F32)], axis=0))
    square = jnp.concatenate([grid[:, 0:1], grid[:, 1:2]], axis=0) / inner
    cross = jnp.concatenate([grid[:, 2:3], grid[:, 3:4]], axis=0) / inner
    q = lax.rsqrt(square + EPS_NORM)
    y, m, z = y_ref[...], m_ref[...], z_ref[...].astype(F32)
    sig = jax.nn.sigmoid(z)
    silu = z * sig
    u = y * z * sig
    normed = (u * q * gain_ref[...]).astype(BF16)
    du = q * m - u * (q * q * q * cross)
    dy = du * silu
    dy_ref[...] = dy
    du_ref[...] = du
    cf, be, end_f, end_b = columns(df_ref[...], db_ref[...])
    c = c_ref[...]
    back_f = dot_left(dy * spread(jnp.exp(cf)), c, 0, 0)
    back_b = dot_left(dy * spread(jnp.exp(end_b - be)), c, 0, 0)
    put_slices(out_ref, back_f, back_b)
    weight = dot(normed, do_ref[...], 0, 0)
    n = out_ref.shape[0]
    size = WIDTH // n
    for i in range(n):
        for block in range(weight.shape[1] // LANES):
            at = 2 * size + block * size
            out_ref[i, at : at + size, :] = weight[
                i * size : (i + 1) * size, block * LANES : (block + 1) * LANES
            ]


def near_gradients(
    skip_ref, x_ref, b_ref, c_ref, df_ref, db_ref, dy_ref, ent_ref, gx_ref, gb_ref, gc_ref
):
    df, db = df_ref[...], db_ref[...]
    cf, be, end_f, end_b = columns(df, db)
    cf_row, be_row = rows(df, db)
    row, col = places()
    b, c, dy = b_ref[...], c_ref[...], dy_ref[...]
    scores = dot(c, b, 1, 1)
    pair_sum = jnp.zeros((FRAMES, FRAMES), F32)
    lane = lax.broadcasted_iota(jnp.int32, (1, LANES), 1)
    for g in range(HEADS // 2):
        at = slice(g * LANES, (g + 1) * LANES)
        acc = jnp.where(lane < HEAD_DIM, skip_ref[2 * g], skip_ref[2 * g + 1]) * dy[:, at]
        for hh in range(2):
            decay = pair_decay(2 * g + hh, cf, be, cf_row, be_row, row, col)
            dy_own = own_lanes(dy[:, at], hh)
            pair_sum = pair_sum + decay * dot_left(dy_own, x_ref[:, at], 1, 1)
            acc = acc + dot_both(scores * decay, dy_own, 0, 0)
        gx_ref[:, at] = acc
    entry_f, entry_b = take_slices(ent_ref)
    rise_f, rise_b = spread(jnp.exp(cf)), spread(jnp.exp(end_b - be))
    grad_c = dot_left(pair_sum, b, 1, 0)
    gc_ref[...] = grad_c + dot_both(dy * rise_f, entry_f, 1, 0) + dot_both(dy * rise_b, entry_b, 1, 0)
    gb_ref[...] = dot_left(pair_sum, c, 0, 0)


def gate_gradient(du_ref, y_ref, z_ref, gz_ref):
    z = z_ref[...].astype(F32)
    sig = jax.nn.sigmoid(z)
    gz_ref[...] = (du_ref[...] * y_ref[...] * sig * (1.0 + z * (1.0 - sig))).astype(BF16)


def finish(core_ref, x_ref, df_ref, db_ref, exit_ref, gb_near, gc_near, keep_ref, give_ref):
    cf, be, end_f, end_b = columns(df_ref[...], db_ref[...])
    x = x_ref[...].astype(F32)
    exit_f, exit_b = take_slices(exit_ref)
    grad_b = gb_near[...] + dot_both(x * spread(jnp.exp(end_f - cf)), exit_f, 1, 0)
    grad_b = grad_b + dot_both(x * spread(jnp.exp(be)), exit_b, 1, 0)
    half = FRAMES // 2
    first = core_ref[0] == 0
    for i, grad in enumerate((grad_b, gc_near[...])):
        at = slice(i * half, (i + 1) * half)
        keep_ref[at, :] = jnp.where(first, grad[:half, :], grad[half:, :])
        give_ref[at, :] = jnp.where(first, grad[half:, :], grad[:half, :])


def finish_x(b_ref, df_ref, db_ref, exit_ref, gx_near, gx_ref):
    cf, be, end_f, end_b = columns(df_ref[...], db_ref[...])
    b = b_ref[...]
    exit_f, exit_b = take_slices(exit_ref)
    gx = gx_near[...] + spread(jnp.exp(end_f - cf)) * dot_right(b, exit_f, 1, 1)
    gx_ref[...] = (gx + spread(jnp.exp(be)) * dot_right(b, exit_b, 1, 1)).astype(BF16)


def add_two(a_ref, b_ref, out_ref):
    out_ref[...] = a_ref[...] + b_ref[...]


def deal_out(core_ref, own_ref, other_ref, gb_ref, gc_ref):
    half = FRAMES // 2
    first = core_ref[0] == 0
    for i, ref in enumerate((gb_ref, gc_ref)):
        at = slice(i * half, (i + 1) * half)
        ref[0:half, :] = jnp.where(first, own_ref[at, :], other_ref[at, :])
        ref[half:, :] = jnp.where(first, other_ref[at, :], own_ref[at, :])


VMEM = pl.BlockSpec(memory_space=pltpu.VMEM)
SMEM = pl.BlockSpec(memory_space=pltpu.SMEM)
HBM = pl.BlockSpec(memory_space=pltpu.MemorySpace.HBM)


def call(kernel, name, out, *args, scalars=0, own=()):
    shapes = [jax.ShapeDtypeStruct(shape, dtype) for shape, dtype in out]
    single = len(shapes) == 1
    return pl.pallas_call(
        kernel,
        name=name,
        out_shape=shapes[0] if single else tuple(shapes),
        in_specs=[SMEM] * scalars + [HBM if own else VMEM] * (len(args) - scalars),
        out_specs=VMEM if single else tuple(VMEM for _ in shapes),
        scratch_shapes=list(own),
        compiler_params=pltpu.CompilerParams(vmem_limit_bytes=48 * 1024 * 1024),
    )(*args)


def exchange(a, axis):
    return lax.all_to_all(a, axis, 0, 0, tiled=True)


def swapped(a, mask, n_h):
    return lax.ppermute(a, "head", [(i, i ^ mask) for i in range(n_h)])


def body(x_in, gate_in, b_in, c_in, decay_fwd, decay_bwd, skip_gain, norm_gain, w_out, d_out):
    n_hi, n_lo, n_x, n_h = (lax.axis_size(axis) for axis in ("z_hi", "z_lo", "x", "head"))
    group = ("z_lo", "x")
    n = n_lo * n_x
    model = d_out.shape[1]
    gain = norm_gain.reshape(1, WIDTH)
    size = WIDTH // n
    weights = size * model // LANES
    place = lax.axis_index("z_hi").astype(jnp.int32).reshape(1)
    decays = (decay_fwd, decay_bwd)
    square = (FRAMES, WIDTH)

    firsts = tuple(pltpu.with_memory_space_constraint(a, pltpu.MemorySpace.HBM) for a in (x_in, b_in, *decays))
    own = [pltpu.VMEM(a.shape, a.dtype) for a in firsts] + [pltpu.SemaphoreType.DMA((4,))]
    sent = call(
        local_states, "local_states", [((n, 2 * size + 8, LANES), F32)], place, *firsts, scalars=1, own=own
    )
    rec1 = exchange(sent, group)
    near, m = call(
        near_outputs, "near_outputs", [(square, F32)] * 2,
        skip_gain, x_in, b_in, c_in, *decays, gain, w_out, d_out, scalars=1,
    )
    sent = call(totals_up, "totals_up", [((n_hi, size + 8, LANES), F32)], place, rec1, scalars=1)
    recz1 = exchange(sent, "z_hi")
    recz1, near, m = lax.optimization_barrier((recz1, near, m))
    sent = call(entries_up, "entries_up", [((n, 2 * size, LANES), F32)], place, recz1, rec1, scalars=1)
    entries = exchange(sent, group)

    y, sums = call(
        outputs, "outputs", [(square, F32), ((n_h, 8, LANES), F32)],
        near, m, gate_in, c_in, *decays, entries,
    )
    sums = exchange(sums, "head")
    dy, du, sent = call(
        functools.partial(gradients, inner=WIDTH * n_h), "gradients",
        [(square, F32), (square, F32), ((n, 2 * size + weights, LANES), F32)],
        sums, y, m, gate_in, c_in, *decays, gain, d_out,
    )

    rec2 = exchange(sent, group)
    gx_near, gb_near, gc_near = call(
        near_gradients, "near_gradients", [(square, F32)] + [((FRAMES, STATE), F32)] * 2,
        skip_gain, x_in, b_in, c_in, *decays, dy, entries, scalars=1,
    )
    grad_z = call(gate_gradient, "gate_gradient", [(square, BF16)], du, y, gate_in)
    part = weights // n_hi
    sent = call(totals_down, "totals_down", [((n_hi, size + part, LANES), F32)], place, rec1, rec2, scalars=1)
    recz2 = exchange(sent, "z_hi")
    recz2, gx_near, gb_near, gc_near, grad_z = lax.optimization_barrier(
        (recz2, gx_near, gb_near, gc_near, grad_z)
    )
    sent, weight = call(
        entries_down, "entries_down", [((n, 2 * size, LANES), F32), ((n_hi, part, LANES), F32)],
        place, recz1, recz2, rec1, rec2, scalars=1,
    )
    exits = exchange(sent, group)

    exits, weight = lax.optimization_barrier((exits, weight))
    weight = exchange(weight, "z_hi")

    core = (lax.axis_index("head") % 2).astype(jnp.int32).reshape(1)
    half = [((FRAMES, STATE), F32)]
    own, give = call(finish, "finish", half * 2, core, x_in, *decays, exits, gb_near, gc_near, scalars=1)
    own = call(add_two, "add_core", half, own, swapped(give, 1, n_h))
    own = call(add_two, "add_y", half, own, swapped(own, 2, n_h))
    weight, own = lax.optimization_barrier((weight, own))

    weight = call(weight_copy, "weight_copy", [((n, weights, LANES), F32)], weight)
    weight = exchange(weight, group)
    grad_w = call(weight_rows, "weight_rows", [((WIDTH, model), F32)], weight)

    own = call(add_two, "add_y", half, own, swapped(own, 6, n_h))
    other = swapped(own, 1, n_h)
    grad_x = call(finish_x, "finish_x", [(square, BF16)], b_in, *decays, exits, gx_near)
    grad_b, grad_c = call(deal_out, "deal_out", half * 2, core, own, other, scalars=1)
    return grad_x, grad_z, grad_b, grad_c, grad_w


def solution(mesh):
    n_seq, n_head = mesh.devices.shape
    n_z = n_seq // HEADS
    n_lo = min(2, n_z // 2)
    split = Mesh(mesh.devices.reshape(n_z // n_lo, n_lo, HEADS, n_head), ("z_hi", "z_lo", "x", "head"))
    seq = ("z_hi", "z_lo", "x")
    in_specs = (
        P(seq, "head"),
        P(seq, "head"),
        P(seq, None),
        P(seq, None),
        P("head", seq),
        P("head", seq),
        P("head"),
        P("head"),
        P("head", None),
        P(seq, None),
    )
    out_specs = (
        P(seq, "head"),
        P(seq, "head"),
        P(seq, None),
        P(seq, None),
        P("head", None),
    )
    return jax.shard_map(body, mesh=split, in_specs=in_specs, out_specs=out_specs, check_vma=False)
```

```python
import functools

import jax
import jax.numpy as jnp
from jax import lax
from jax.experimental import pallas as pl
from jax.experimental.pallas import tpu as pltpu
from jax.sharding import Mesh, PartitionSpec as P

HEADS = 4
HEAD_DIM = 64
STATE = 128
FRAMES = 256
WIDTH = HEADS * HEAD_DIM
LANES = 128
EPS_NORM = 1e-05
WEIGHT_SCALE = 0.0078125
F32, BF16 = jnp.float32, jnp.bfloat16


def dot(a, b, ca, cb):
    return lax.dot_general(a, b, (((ca,), (cb,)), ((), ())), preferred_element_type=F32)


def halves(a):
    high = a.astype(BF16)
    return high, (a - high.astype(F32)).astype(BF16)


def dot_left(a, b, ca, cb):
    ah, al = halves(a)
    return dot(ah, b, ca, cb) + dot(al, b, ca, cb)


def dot_right(a, b, ca, cb):
    bh, bl = halves(b)
    return dot(a, bh, ca, cb) + dot(a, bl, ca, cb)


def dot_both(a, b, ca, cb):
    ah, al = halves(a)
    bh, bl = halves(b)
    return dot(ah, bh, ca, cb) + (dot(ah, bl, ca, cb) + dot(al, bh, ca, cb))


def dot_exact(a, b, ca, cb):
    return lax.dot_general(
        a, b, (((ca,), (cb,)), ((), ())), precision=lax.Precision.HIGHEST, preferred_element_type=F32
    )


def places():
    row = lax.broadcasted_iota(jnp.int32, (FRAMES, FRAMES), 0)
    col = lax.broadcasted_iota(jnp.int32, (FRAMES, FRAMES), 1)
    return row, col


def columns(df, db):
    row, col = places()
    upto = (col <= row).astype(F32)
    before = (col < row).astype(F32)
    cf = dot_exact(upto, df, 1, 1)
    be = dot_exact(before, db, 1, 1)
    end_f = cf[FRAMES - 1 :, :]
    end_b = dot_exact(jnp.ones((8, FRAMES), F32), db, 1, 1)[:1, :]
    return cf, be, end_f, end_b


def rows(df, db):
    row, col = places()
    upto = (row <= col).astype(F32)
    before = (row < col).astype(F32)
    return dot_exact(df, upto, 1, 0), dot_exact(db, before, 1, 0)


def spread(cols):
    lane = lax.broadcasted_iota(jnp.int32, (cols.shape[0], LANES), 1)
    pairs = [
        jnp.where(lane < HEAD_DIM, cols[:, 2 * g : 2 * g + 1], cols[:, 2 * g + 1 : 2 * g + 2])
        for g in range(HEADS // 2)
    ]
    return jnp.concatenate(pairs, axis=1)


def pair_decay(h, cf, be, cf_row, be_row, row, col):
    gap = jnp.where(
        row > col,
        cf[:, h : h + 1] - cf_row[h : h + 1, :],
        be_row[h : h + 1, :] - be[:, h : h + 1],
    )
    return jnp.where(row == col, 2.0, jnp.exp(jnp.minimum(gap, 0.0)))


def own_lanes(pair, hh):
    lane = lax.broadcasted_iota(jnp.int32, pair.shape, 1)
    mine = lane < HEAD_DIM if hh == 0 else lane >= HEAD_DIM
    return jnp.where(mine, pair, jnp.zeros_like(pair))


def put_slices(out_ref, forward, backward):
    n = out_ref.shape[0]
    size = WIDTH // n
    for i in range(n):
        at = slice(i * size, (i + 1) * size)
        out_ref[i, 0:size, :] = forward[at, :]
        out_ref[i, size : 2 * size, :] = backward[at, :]


def take_slices(ref):
    n = ref.shape[0]
    size = WIDTH // n
    forward = jnp.concatenate([ref[i, 0:size, :] for i in range(n)], axis=0)
    backward = jnp.concatenate([ref[i, size : 2 * size, :] for i in range(n)], axis=0)
    return forward, backward


def local_states(_, x_hbm, b_hbm, df_hbm, db_hbm, out_ref, x_ref, b_ref, df_ref, db_ref, sems):
    sources, targets = (x_hbm, b_hbm, df_hbm, db_hbm), (x_ref, b_ref, df_ref, db_ref)
    copies = [pltpu.make_async_copy(s, t, sems.at[i]) for i, (s, t) in enumerate(zip(sources, targets))]
    for copy in copies[::-1]:
        copy.start()
    copies[2].wait()
    copies[3].wait()
    cf, be, end_f, end_b = columns(df_ref[...], db_ref[...])
    copies[0].wait()
    copies[1].wait()
    x = x_ref[...].astype(F32)
    b = b_ref[...]
    state_f = dot_left(x * spread(jnp.exp(end_f - cf)), b, 0, 0)
    state_b = dot_left(x * spread(jnp.exp(be)), b, 0, 0)
    put_slices(out_ref, state_f, state_b)
    n = out_ref.shape[0]
    size = WIDTH // n
    total_f, total_b = jnp.exp(end_f), jnp.exp(end_b)
    half = lax.broadcasted_iota(jnp.int32, (8, LANES), 0) < 4
    for j in range(HEADS):
        both = jnp.where(half, total_f[:, j : j + 1], total_b[:, j : j + 1])
        for i in range(j * n // HEADS, (j + 1) * n // HEADS):
            out_ref[i, 2 * size :, :] = both


def totals_at(ref, i, start):
    return ref[i, start : start + 1, :], ref[i, start + 4 : start + 5, :]


def sliced(ref, i, size):
    return ref[i, 0:size, :], ref[i, size : 2 * size, :]


def group_sums(dec_ref, rec_ref, forward_up):
    n = rec_ref.shape[0]
    size = WIDTH // n
    decays = [totals_at(dec_ref, i, 2 * size) for i in range(n)]
    parts = [sliced(rec_ref, i, size) for i in range(n)]
    sums = []
    for branch, up in enumerate((forward_up, not forward_up)):
        order = list(range(n)) if up else list(range(n))[::-1]
        acc = parts[order[0]][branch]
        for i in order[1:]:
            acc = decays[i][branch] * acc + parts[i][branch]
        sums.append(acc)
    return sums, decays


def totals_up(place_ref, rec_ref, out_ref):
    size = WIDTH // rec_ref.shape[0]
    (sum_f, sum_b), decays = group_sums(rec_ref, rec_ref, True)
    all_f, all_b = decays[0]
    for dec_f, dec_b in decays[1:]:
        all_f, all_b = all_f * dec_f, all_b * dec_b
    half = lax.broadcasted_iota(jnp.int32, (8, LANES), 0) < 4
    for k in range(out_ref.shape[0]):
        out_ref[k, 0:size, :] = jnp.where(place_ref[0] < k, sum_f, sum_b)
        out_ref[k, size:, :] = jnp.where(half, all_f, all_b)


def entries_up(place_ref, zrec_ref, rec_ref, out_ref):
    n_g, n = zrec_ref.shape[0], rec_ref.shape[0]
    size = WIDTH // n
    place = place_ref[0]
    for branch, up in enumerate((True, False)):
        entry = jnp.zeros((size, LANES), F32)
        for k in list(range(n_g)) if up else list(range(n_g))[::-1]:
            passed = place > k if up else place < k
            after = totals_at(zrec_ref, k, size)[branch] * entry + zrec_ref[k, 0:size, :]
            entry = jnp.where(passed, after, entry)
        put_entries(out_ref, branch, up, entry, rec_ref, rec_ref)


def put_entries(out_ref, branch, up, entry, dec_ref, rec_ref):
    n = rec_ref.shape[0]
    size = WIDTH // n
    for i in list(range(n)) if up else list(range(n))[::-1]:
        out_ref[i, branch * size : (branch + 1) * size, :] = entry
        entry = totals_at(dec_ref, i, 2 * size)[branch] * entry + sliced(rec_ref, i, size)[branch]


def totals_down(place_ref, dec_ref, rec_ref, out_ref):
    n, n_g = rec_ref.shape[0], out_ref.shape[0]
    size = WIDTH // n
    (sum_f, sum_b), _ = group_sums(dec_ref, rec_ref, False)
    weight = rec_ref[0, 2 * size :, :]
    for i in range(1, n):
        weight = weight + rec_ref[i, 2 * size :, :]
    part = weight.shape[0] // n_g
    for k in range(n_g):
        out_ref[k, 0:size, :] = jnp.where(place_ref[0] > k, sum_f, sum_b)
        out_ref[k, size:, :] = weight[k * part : (k + 1) * part, :]


def entries_down(place_ref, zdec_ref, zrec_ref, dec_ref, rec_ref, out_ref, w_ref):
    n_g, n = zrec_ref.shape[0], rec_ref.shape[0]
    size = WIDTH // n
    place = place_ref[0]
    for branch, up in enumerate((False, True)):
        entry = jnp.zeros((size, LANES), F32)
        for k in list(range(n_g)) if up else list(range(n_g))[::-1]:
            passed = place > k if up else place < k
            after = totals_at(zdec_ref, k, size)[branch] * entry + zrec_ref[k, 0:size, :]
            entry = jnp.where(passed, after, entry)
        put_entries(out_ref, branch, up, entry, dec_ref, rec_ref)
    weight = zrec_ref[0, size:, :]
    for k in range(1, n_g):
        weight = weight + zrec_ref[k, size:, :]
    for k in range(n_g):
        w_ref[k, :, :] = weight


def weight_copy(rec_ref, out_ref):
    n_g, part = rec_ref.shape[0], rec_ref.shape[1]
    for k in range(n_g):
        rows = rec_ref[k, :, :]
        for i in range(out_ref.shape[0]):
            out_ref[i, k * part : (k + 1) * part, :] = rows


def weight_rows(rec_ref, gw_ref):
    n = rec_ref.shape[0]
    size = WIDTH // n
    for i in range(n):
        for block in range(gw_ref.shape[1] // LANES):
            gw_ref[i * size : (i + 1) * size, block * LANES : (block + 1) * LANES] = (
                rec_ref[i, block * size : (block + 1) * size, :] * WEIGHT_SCALE
            )


def across_rows(cols):
    lane = lax.broadcasted_iota(jnp.int32, (LANES, LANES), 1)
    grid = jnp.zeros((LANES, LANES), F32)
    for i, col in enumerate(cols):
        for part in range(FRAMES // LANES):
            at = i * (FRAMES // LANES) + part
            grid = jnp.where(lane == at, col[part * LANES : (part + 1) * LANES, :], grid)
    return jnp.transpose(grid)[0:8, :]


def near_outputs(
    skip_ref, x_ref, b_ref, c_ref, df_ref, db_ref, gain_ref, w_ref, do_ref, y_ref, m_ref
):
    df, db = df_ref[...], db_ref[...]
    cf, be, end_f, end_b = columns(df, db)
    cf_row, be_row = rows(df, db)
    row, col = places()
    scores = dot(c_ref[...], b_ref[...], 1, 1)
    lane = lax.broadcasted_iota(jnp.int32, (1, LANES), 1)
    for g in range(HEADS // 2):
        at = slice(g * LANES, (g + 1) * LANES)
        pair = x_ref[:, at]
        acc = jnp.where(lane < HEAD_DIM, skip_ref[2 * g], skip_ref[2 * g + 1]) * pair.astype(F32)
        for hh in range(2):
            weights = scores * pair_decay(2 * g + hh, cf, be, cf_row, be_row, row, col)
            acc = acc + dot_left(weights, own_lanes(pair, hh), 1, 0)
        y_ref[:, at] = acc
    m_ref[...] = dot(do_ref[...], w_ref[...], 1, 1) * gain_ref[...]


def outputs(near_ref, m_ref, z_ref, c_ref, df_ref, db_ref, ent_ref, y_ref, sums_ref):
    cf, be, end_f, end_b = columns(df_ref[...], db_ref[...])
    c = c_ref[...]
    entry_f, entry_b = take_slices(ent_ref)
    y = near_ref[...] + spread(jnp.exp(cf)) * dot_right(c, entry_f, 1, 1)
    y = y + spread(jnp.exp(end_b - be)) * dot_right(c, entry_b, 1, 1)
    y_ref[...] = y
    z, m = z_ref[...].astype(F32), m_ref[...]
    u = y * z * jax.nn.sigmoid(z)
    sums = across_rows([jnp.sum(u * u, axis=1, keepdims=True), jnp.sum(u * m, axis=1, keepdims=True)])
    for i in range(sums_ref.shape[0]):
        sums_ref[i, :, :] = sums


def gradients(
    sums_ref, y_ref, m_ref, z_ref, c_ref, df_ref, db_ref, gain_ref, do_ref,
    dy_ref, du_ref, out_ref, *, inner,
):
    total = sums_ref[0, :, :]
    for i in range(1, sums_ref.shape[0]):
        total = total + sums_ref[i, :, :]
    grid = jnp.transpose(jnp.concatenate([total, jnp.zeros((LANES - 8, LANES), F32)], axis=0))
    square = jnp.concatenate([grid[:, 0:1], grid[:, 1:2]], axis=0) / inner
    cross = jnp.concatenate([grid[:, 2:3], grid[:, 3:4]], axis=0) / inner
    q = lax.rsqrt(square + EPS_NORM)
    y, m, z = y_ref[...], m_ref[...], z_ref[...].astype(F32)
    sig = jax.nn.sigmoid(z)
    silu = z * sig
    u = y * z * sig
    normed = (u * q * gain_ref[...]).astype(BF16)
    du = q * m - u * (q * q * q * cross)
    dy = du * silu
    dy_ref[...] = dy
    du_ref[...] = du
    cf, be, end_f, end_b = columns(df_ref[...], db_ref[...])
    c = c_ref[...]
    back_f = dot_left(dy * spread(jnp.exp(cf)), c, 0, 0)
    back_b = dot_left(dy * spread(jnp.exp(end_b - be)), c, 0, 0)
    put_slices(out_ref, back_f, back_b)
    weight = dot(normed, do_ref[...], 0, 0)
    n = out_ref.shape[0]
    size = WIDTH // n
    for i in range(n):
        for block in range(weight.shape[1] // LANES):
            at = 2 * size + block * size
            out_ref[i, at : at + size, :] = weight[
                i * size : (i + 1) * size, block * LANES : (block + 1) * LANES
            ]


def near_gradients(
    skip_ref, x_ref, b_ref, c_ref, df_ref, db_ref, dy_ref, ent_ref, gx_ref, gb_ref, gc_ref
):
    df, db = df_ref[...], db_ref[...]
    cf, be, end_f, end_b = columns(df, db)
    cf_row, be_row = rows(df, db)
    row, col = places()
    b, c, dy = b_ref[...], c_ref[...], dy_ref[...]
    scores = dot(c, b, 1, 1)
    pair_sum = jnp.zeros((FRAMES, FRAMES), F32)
    lane = lax.broadcasted_iota(jnp.int32, (1, LANES), 1)
    for g in range(HEADS // 2):
        at = slice(g * LANES, (g + 1) * LANES)
        acc = jnp.where(lane < HEAD_DIM, skip_ref[2 * g], skip_ref[2 * g + 1]) * dy[:, at]
        for hh in range(2):
            decay = pair_decay(2 * g + hh, cf, be, cf_row, be_row, row, col)
            dy_own = own_lanes(dy[:, at], hh)
            pair_sum = pair_sum + decay * dot_left(dy_own, x_ref[:, at], 1, 1)
            acc = acc + dot_both(scores * decay, dy_own, 0, 0)
        gx_ref[:, at] = acc
    entry_f, entry_b = take_slices(ent_ref)
    rise_f, rise_b = spread(jnp.exp(cf)), spread(jnp.exp(end_b - be))
    grad_c = dot_left(pair_sum, b, 1, 0)
    gc_ref[...] = grad_c + dot_both(dy * rise_f, entry_f, 1, 0) + dot_both(dy * rise_b, entry_b, 1, 0)
    gb_ref[...] = dot_left(pair_sum, c, 0, 0)


def gate_gradient(du_ref, y_ref, z_ref, gz_ref):
    z = z_ref[...].astype(F32)
    sig = jax.nn.sigmoid(z)
    gz_ref[...] = (du_ref[...] * y_ref[...] * sig * (1.0 + z * (1.0 - sig))).astype(BF16)


def finish(x_ref, df_ref, db_ref, exit_ref, gb_near, gc_near, out_ref):
    cf, be, end_f, end_b = columns(df_ref[...], db_ref[...])
    x = x_ref[...].astype(F32)
    exit_f, exit_b = take_slices(exit_ref)
    grad_b = gb_near[...] + dot_both(x * spread(jnp.exp(end_f - cf)), exit_f, 1, 0)
    grad_b = grad_b + dot_both(x * spread(jnp.exp(be)), exit_b, 1, 0)
    out_ref[0, :, :] = grad_b
    out_ref[1, :, :] = gc_near[...]


def finish_x(b_ref, df_ref, db_ref, exit_ref, gx_near, gx_ref):
    cf, be, end_f, end_b = columns(df_ref[...], db_ref[...])
    b = b_ref[...]
    exit_f, exit_b = take_slices(exit_ref)
    gx = gx_near[...] + spread(jnp.exp(end_f - cf)) * dot_right(b, exit_f, 1, 1)
    gx_ref[...] = (gx + spread(jnp.exp(be)) * dot_right(b, exit_b, 1, 1)).astype(BF16)


def add_two(a_ref, b_ref, out_ref):
    out_ref[...] = a_ref[...] + b_ref[...]


def add_last(a_ref, b_ref, gb_ref, gc_ref):
    gb_ref[...] = a_ref[0, :, :] + b_ref[0, :, :]
    gc_ref[...] = a_ref[1, :, :] + b_ref[1, :, :]


VMEM = pl.BlockSpec(memory_space=pltpu.VMEM)
SMEM = pl.BlockSpec(memory_space=pltpu.SMEM)
HBM = pl.BlockSpec(memory_space=pltpu.MemorySpace.HBM)


def call(kernel, name, out, *args, scalars=0, own=()):
    shapes = [jax.ShapeDtypeStruct(shape, dtype) for shape, dtype in out]
    single = len(shapes) == 1
    return pl.pallas_call(
        kernel,
        name=name,
        out_shape=shapes[0] if single else tuple(shapes),
        in_specs=[SMEM] * scalars + [HBM if own else VMEM] * (len(args) - scalars),
        out_specs=VMEM if single else tuple(VMEM for _ in shapes),
        scratch_shapes=list(own),
        compiler_params=pltpu.CompilerParams(vmem_limit_bytes=48 * 1024 * 1024),
    )(*args)


def exchange(a, axis):
    return lax.all_to_all(a, axis, 0, 0, tiled=True)


def swapped(a, mask, n_h):
    return lax.ppermute(a, "head", [(i, i ^ mask) for i in range(n_h)])


def body(x_in, gate_in, b_in, c_in, decay_fwd, decay_bwd, skip_gain, norm_gain, w_out, d_out):
    n_hi, n_lo, n_x, n_h = (lax.axis_size(axis) for axis in ("z_hi", "z_lo", "x", "head"))
    group = ("z_lo", "x")
    n = n_lo * n_x
    model = d_out.shape[1]
    gain = norm_gain.reshape(1, WIDTH)
    size = WIDTH // n
    weights = size * model // LANES
    place = lax.axis_index("z_hi").astype(jnp.int32).reshape(1)
    decays = (decay_fwd, decay_bwd)
    square = (FRAMES, WIDTH)

    firsts = tuple(pltpu.with_memory_space_constraint(a, pltpu.MemorySpace.HBM) for a in (x_in, b_in, *decays))
    own = [pltpu.VMEM(a.shape, a.dtype) for a in firsts] + [pltpu.SemaphoreType.DMA((4,))]
    sent = call(
        local_states, "local_states", [((n, 2 * size + 8, LANES), F32)], place, *firsts, scalars=1, own=own
    )
    rec1 = exchange(sent, group)
    near, m = call(
        near_outputs, "near_outputs", [(square, F32)] * 2,
        skip_gain, x_in, b_in, c_in, *decays, gain, w_out, d_out, scalars=1,
    )
    sent = call(totals_up, "totals_up", [((n_hi, size + 8, LANES), F32)], place, rec1, scalars=1)
    recz1 = exchange(sent, "z_hi")
    recz1, near, m = lax.optimization_barrier((recz1, near, m))
    sent = call(entries_up, "entries_up", [((n, 2 * size, LANES), F32)], place, recz1, rec1, scalars=1)
    entries = exchange(sent, group)

    y, sums = call(
        outputs, "outputs", [(square, F32), ((n_h, 8, LANES), F32)],
        near, m, gate_in, c_in, *decays, entries,
    )
    sums = exchange(sums, "head")
    dy, du, sent = call(
        functools.partial(gradients, inner=WIDTH * n_h), "gradients",
        [(square, F32), (square, F32), ((n, 2 * size + weights, LANES), F32)],
        sums, y, m, gate_in, c_in, *decays, gain, d_out,
    )

    rec2 = exchange(sent, group)
    gx_near, gb_near, gc_near = call(
        near_gradients, "near_gradients", [(square, F32)] + [((FRAMES, STATE), F32)] * 2,
        skip_gain, x_in, b_in, c_in, *decays, dy, entries, scalars=1,
    )
    grad_z = call(gate_gradient, "gate_gradient", [(square, BF16)], du, y, gate_in)
    part = weights // n_hi
    sent = call(totals_down, "totals_down", [((n_hi, size + part, LANES), F32)], place, rec1, rec2, scalars=1)
    recz2 = exchange(sent, "z_hi")
    recz2, gx_near, gb_near, gc_near, grad_z = lax.optimization_barrier(
        (recz2, gx_near, gb_near, gc_near, grad_z)
    )
    sent, weight = call(
        entries_down, "entries_down", [((n, 2 * size, LANES), F32), ((n_hi, part, LANES), F32)],
        place, recz1, recz2, rec1, rec2, scalars=1,
    )
    exits = exchange(sent, group)

    exits, weight = lax.optimization_barrier((exits, weight))
    weight = exchange(weight, "z_hi")

    both = [((2, FRAMES, STATE), F32)]
    own = call(finish, "finish", both, x_in, *decays, exits, gb_near, gc_near)
    own = call(add_two, "add_core", both, own, swapped(own, 1, n_h))
    own = call(add_two, "add_y", both, own, swapped(own, 2, n_h))
    weight, own = lax.optimization_barrier((weight, own))

    weight = call(weight_copy, "weight_copy", [((n, weights, LANES), F32)], weight)
    weight = exchange(weight, group)
    grad_w = call(weight_rows, "weight_rows", [((WIDTH, model), F32)], weight)

    grad_x = call(finish_x, "finish_x", [(square, BF16)], b_in, *decays, exits, gx_near)
    grads = [((FRAMES, STATE), F32)] * 2
    grad_b, grad_c = call(add_last, "add_last", grads, own, swapped(own, 6, n_h))
    return grad_x, grad_z, grad_b, grad_c, grad_w


def solution(mesh):
    n_seq, n_head = mesh.devices.shape
    n_z = n_seq // HEADS
    n_lo = min(2, n_z // 2)
    split = Mesh(mesh.devices.reshape(n_z // n_lo, n_lo, HEADS, n_head), ("z_hi", "z_lo", "x", "head"))
    seq = ("z_hi", "z_lo", "x")
    in_specs = (
        P(seq, "head"),
        P(seq, "head"),
        P(seq, None),
        P(seq, None),
        P("head", seq),
        P("head", seq),
        P("head"),
        P("head"),
        P("head", None),
        P(seq, None),
    )
    out_specs = (
        P(seq, "head"),
        P(seq, "head"),
        P(seq, None),
        P(seq, None),
        P("head", None),
    )
    return jax.shard_map(body, mesh=split, in_specs=in_specs, out_specs=out_specs, check_vma=False)
```

```python
import functools

import jax
import jax.numpy as jnp
from jax import lax
from jax.experimental import pallas as pl
from jax.experimental.pallas import tpu as pltpu
from jax.sharding import Mesh, PartitionSpec as P

HEADS = 4
HEAD_DIM = 64
STATE = 128
FRAMES = 256
WIDTH = HEADS * HEAD_DIM
LANES = 128
EPS_NORM = 1e-05
WEIGHT_SCALE = 0.0078125
F32, BF16 = jnp.float32, jnp.bfloat16


def dot(a, b, ca, cb):
    return lax.dot_general(a, b, (((ca,), (cb,)), ((), ())), preferred_element_type=F32)


def halves(a):
    high = a.astype(BF16)
    return high, (a - high.astype(F32)).astype(BF16)


def dot_left(a, b, ca, cb):
    ah, al = halves(a)
    return dot(ah, b, ca, cb) + dot(al, b, ca, cb)


def dot_right(a, b, ca, cb):
    bh, bl = halves(b)
    return dot(a, bh, ca, cb) + dot(a, bl, ca, cb)


def dot_both(a, b, ca, cb):
    ah, al = halves(a)
    bh, bl = halves(b)
    return dot(ah, bh, ca, cb) + (dot(ah, bl, ca, cb) + dot(al, bh, ca, cb))


def dot_exact(a, b, ca, cb):
    return lax.dot_general(
        a, b, (((ca,), (cb,)), ((), ())), precision=lax.Precision.HIGHEST, preferred_element_type=F32
    )


def places():
    row = lax.broadcasted_iota(jnp.int32, (FRAMES, FRAMES), 0)
    col = lax.broadcasted_iota(jnp.int32, (FRAMES, FRAMES), 1)
    return row, col


def columns(df, db):
    row, col = places()
    upto = (col <= row).astype(F32)
    before = (col < row).astype(F32)
    cf = dot_exact(upto, df, 1, 1)
    be = dot_exact(before, db, 1, 1)
    end_f = cf[FRAMES - 1 :, :]
    end_b = dot_exact(jnp.ones((8, FRAMES), F32), db, 1, 1)[:1, :]
    return cf, be, end_f, end_b


def rows(df, db):
    row, col = places()
    upto = (row <= col).astype(F32)
    before = (row < col).astype(F32)
    return dot_exact(df, upto, 1, 0), dot_exact(db, before, 1, 0)


def spread(cols):
    lane = lax.broadcasted_iota(jnp.int32, (cols.shape[0], LANES), 1)
    pairs = [
        jnp.where(lane < HEAD_DIM, cols[:, 2 * g : 2 * g + 1], cols[:, 2 * g + 1 : 2 * g + 2])
        for g in range(HEADS // 2)
    ]
    return jnp.concatenate(pairs, axis=1)


def pair_decay(h, cf, be, cf_row, be_row, row, col):
    gap = jnp.where(
        row > col,
        cf[:, h : h + 1] - cf_row[h : h + 1, :],
        be_row[h : h + 1, :] - be[:, h : h + 1],
    )
    return jnp.where(row == col, 2.0, jnp.exp(jnp.minimum(gap, 0.0)))


def own_lanes(pair, hh):
    lane = lax.broadcasted_iota(jnp.int32, pair.shape, 1)
    mine = lane < HEAD_DIM if hh == 0 else lane >= HEAD_DIM
    return jnp.where(mine, pair, jnp.zeros_like(pair))


def put_slices(out_ref, forward, backward):
    n = out_ref.shape[0]
    size = WIDTH // n
    for i in range(n):
        at = slice(i * size, (i + 1) * size)
        out_ref[i, 0:size, :] = forward[at, :]
        out_ref[i, size : 2 * size, :] = backward[at, :]


def take_slices(ref):
    n = ref.shape[0]
    size = WIDTH // n
    forward = jnp.concatenate([ref[i, 0:size, :] for i in range(n)], axis=0)
    backward = jnp.concatenate([ref[i, size : 2 * size, :] for i in range(n)], axis=0)
    return forward, backward


def local_states(_, x_hbm, b_hbm, df_hbm, db_hbm, out_ref, x_ref, b_ref, df_ref, db_ref, sems):
    sources, targets = (x_hbm, b_hbm, df_hbm, db_hbm), (x_ref, b_ref, df_ref, db_ref)
    copies = [pltpu.make_async_copy(s, t, sems.at[i]) for i, (s, t) in enumerate(zip(sources, targets))]
    for copy in copies[::-1]:
        copy.start()
    copies[2].wait()
    copies[3].wait()
    cf, be, end_f, end_b = columns(df_ref[...], db_ref[...])
    copies[0].wait()
    copies[1].wait()
    x = x_ref[...].astype(F32)
    b = b_ref[...]
    state_f = dot_left(x * spread(jnp.exp(end_f - cf)), b, 0, 0)
    state_b = dot_left(x * spread(jnp.exp(be)), b, 0, 0)
    put_slices(out_ref, state_f, state_b)
    n = out_ref.shape[0]
    size = WIDTH // n
    total_f, total_b = jnp.exp(end_f), jnp.exp(end_b)
    half = lax.broadcasted_iota(jnp.int32, (8, LANES), 0) < 4
    for j in range(HEADS):
        both = jnp.where(half, total_f[:, j : j + 1], total_b[:, j : j + 1])
        for i in range(j * n // HEADS, (j + 1) * n // HEADS):
            out_ref[i, 2 * size :, :] = both


def totals_at(ref, i, start):
    return ref[i, start : start + 1, :], ref[i, start + 4 : start + 5, :]


def sliced(ref, i, size):
    return ref[i, 0:size, :], ref[i, size : 2 * size, :]


def group_sums(dec_ref, rec_ref, forward_up):
    n = rec_ref.shape[0]
    size = WIDTH // n
    decays = [totals_at(dec_ref, i, 2 * size) for i in range(n)]
    parts = [sliced(rec_ref, i, size) for i in range(n)]
    sums = []
    for branch, up in enumerate((forward_up, not forward_up)):
        order = list(range(n)) if up else list(range(n))[::-1]
        acc = parts[order[0]][branch]
        for i in order[1:]:
            acc = decays[i][branch] * acc + parts[i][branch]
        sums.append(acc)
    return sums, decays


def totals_up(place_ref, rec_ref, out_ref):
    size = WIDTH // rec_ref.shape[0]
    (sum_f, sum_b), decays = group_sums(rec_ref, rec_ref, True)
    all_f, all_b = decays[0]
    for dec_f, dec_b in decays[1:]:
        all_f, all_b = all_f * dec_f, all_b * dec_b
    half = lax.broadcasted_iota(jnp.int32, (8, LANES), 0) < 4
    for k in range(out_ref.shape[0]):
        out_ref[k, 0:size, :] = jnp.where(place_ref[0] < k, sum_f, sum_b)
        out_ref[k, size:, :] = jnp.where(half, all_f, all_b)


def entries_up(place_ref, zrec_ref, rec_ref, out_ref):
    n_g, n = zrec_ref.shape[0], rec_ref.shape[0]
    size = WIDTH // n
    place = place_ref[0]
    for branch, up in enumerate((True, False)):
        entry = jnp.zeros((size, LANES), F32)
        for k in list(range(n_g)) if up else list(range(n_g))[::-1]:
            passed = place > k if up else place < k
            after = totals_at(zrec_ref, k, size)[branch] * entry + zrec_ref[k, 0:size, :]
            entry = jnp.where(passed, after, entry)
        put_entries(out_ref, branch, up, entry, rec_ref, rec_ref)


def put_entries(out_ref, branch, up, entry, dec_ref, rec_ref):
    n = rec_ref.shape[0]
    size = WIDTH // n
    for i in list(range(n)) if up else list(range(n))[::-1]:
        out_ref[i, branch * size : (branch + 1) * size, :] = entry
        entry = totals_at(dec_ref, i, 2 * size)[branch] * entry + sliced(rec_ref, i, size)[branch]


def totals_down(place_ref, dec_ref, rec_ref, out_ref):
    n, n_g = rec_ref.shape[0], out_ref.shape[0]
    size = WIDTH // n
    (sum_f, sum_b), _ = group_sums(dec_ref, rec_ref, False)
    weight = rec_ref[0, 2 * size :, :]
    for i in range(1, n):
        weight = weight + rec_ref[i, 2 * size :, :]
    part = weight.shape[0] // n_g
    for k in range(n_g):
        out_ref[k, 0:size, :] = jnp.where(place_ref[0] > k, sum_f, sum_b)
        out_ref[k, size:, :] = weight[k * part : (k + 1) * part, :]


def entries_down(place_ref, zdec_ref, zrec_ref, dec_ref, rec_ref, out_ref, w_ref):
    n_g, n = zrec_ref.shape[0], rec_ref.shape[0]
    size = WIDTH // n
    place = place_ref[0]
    for branch, up in enumerate((False, True)):
        entry = jnp.zeros((size, LANES), F32)
        for k in list(range(n_g)) if up else list(range(n_g))[::-1]:
            passed = place > k if up else place < k
            after = totals_at(zdec_ref, k, size)[branch] * entry + zrec_ref[k, 0:size, :]
            entry = jnp.where(passed, after, entry)
        put_entries(out_ref, branch, up, entry, dec_ref, rec_ref)
    weight = zrec_ref[0, size:, :]
    for k in range(1, n_g):
        weight = weight + zrec_ref[k, size:, :]
    for k in range(n_g):
        w_ref[k, :, :] = weight


def weight_copy(rec_ref, out_ref):
    n_g, part = rec_ref.shape[0], rec_ref.shape[1]
    for k in range(n_g):
        rows = rec_ref[k, :, :]
        for i in range(out_ref.shape[0]):
            out_ref[i, k * part : (k + 1) * part, :] = rows


def weight_rows(rec_ref, gw_ref):
    n = rec_ref.shape[0]
    size = WIDTH // n
    for i in range(n):
        for block in range(gw_ref.shape[1] // LANES):
            gw_ref[i * size : (i + 1) * size, block * LANES : (block + 1) * LANES] = (
                rec_ref[i, block * size : (block + 1) * size, :] * WEIGHT_SCALE
            )


def across_rows(cols):
    lane = lax.broadcasted_iota(jnp.int32, (LANES, LANES), 1)
    grid = jnp.zeros((LANES, LANES), F32)
    for i, col in enumerate(cols):
        for part in range(FRAMES // LANES):
            at = i * (FRAMES // LANES) + part
            grid = jnp.where(lane == at, col[part * LANES : (part + 1) * LANES, :], grid)
    return jnp.transpose(grid)[0:8, :]


def near_outputs(
    skip_ref, x_ref, b_ref, c_ref, df_ref, db_ref, gain_ref, w_ref, do_ref, y_ref, m_ref
):
    df, db = df_ref[...], db_ref[...]
    cf, be, end_f, end_b = columns(df, db)
    cf_row, be_row = rows(df, db)
    row, col = places()
    scores = dot(c_ref[...], b_ref[...], 1, 1)
    lane = lax.broadcasted_iota(jnp.int32, (1, LANES), 1)
    for g in range(HEADS // 2):
        at = slice(g * LANES, (g + 1) * LANES)
        pair = x_ref[:, at]
        acc = jnp.where(lane < HEAD_DIM, skip_ref[2 * g], skip_ref[2 * g + 1]) * pair.astype(F32)
        for hh in range(2):
            weights = scores * pair_decay(2 * g + hh, cf, be, cf_row, be_row, row, col)
            acc = acc + dot_left(weights, own_lanes(pair, hh), 1, 0)
        y_ref[:, at] = acc
    m_ref[...] = dot(do_ref[...], w_ref[...], 1, 1) * gain_ref[...]


def outputs(near_ref, m_ref, z_ref, c_ref, df_ref, db_ref, ent_ref, y_ref, sums_ref):
    cf, be, end_f, end_b = columns(df_ref[...], db_ref[...])
    c = c_ref[...]
    entry_f, entry_b = take_slices(ent_ref)
    y = near_ref[...] + spread(jnp.exp(cf)) * dot_right(c, entry_f, 1, 1)
    y = y + spread(jnp.exp(end_b - be)) * dot_right(c, entry_b, 1, 1)
    y_ref[...] = y
    z, m = z_ref[...].astype(F32), m_ref[...]
    u = y * z * jax.nn.sigmoid(z)
    sums = across_rows([jnp.sum(u * u, axis=1, keepdims=True), jnp.sum(u * m, axis=1, keepdims=True)])
    for i in range(sums_ref.shape[0]):
        sums_ref[i, :, :] = sums


def gradients(
    sums_ref, y_ref, m_ref, z_ref, c_ref, df_ref, db_ref, gain_ref, do_ref,
    dy_ref, du_ref, out_ref, *, inner,
):
    total = sums_ref[0, :, :]
    for i in range(1, sums_ref.shape[0]):
        total = total + sums_ref[i, :, :]
    grid = jnp.transpose(jnp.concatenate([total, jnp.zeros((LANES - 8, LANES), F32)], axis=0))
    square = jnp.concatenate([grid[:, 0:1], grid[:, 1:2]], axis=0) / inner
    cross = jnp.concatenate([grid[:, 2:3], grid[:, 3:4]], axis=0) / inner
    q = lax.rsqrt(square + EPS_NORM)
    y, m, z = y_ref[...], m_ref[...], z_ref[...].astype(F32)
    sig = jax.nn.sigmoid(z)
    silu = z * sig
    u = y * z * sig
    normed = (u * q * gain_ref[...]).astype(BF16)
    du = q * m - u * (q * q * q * cross)
    dy = du * silu
    dy_ref[...] = dy
    du_ref[...] = du
    cf, be, end_f, end_b = columns(df_ref[...], db_ref[...])
    c = c_ref[...]
    back_f = dot_left(dy * spread(jnp.exp(cf)), c, 0, 0)
    back_b = dot_left(dy * spread(jnp.exp(end_b - be)), c, 0, 0)
    put_slices(out_ref, back_f, back_b)
    weight = dot(normed, do_ref[...], 0, 0)
    n = out_ref.shape[0]
    size = WIDTH // n
    for i in range(n):
        for block in range(weight.shape[1] // LANES):
            at = 2 * size + block * size
            out_ref[i, at : at + size, :] = weight[
                i * size : (i + 1) * size, block * LANES : (block + 1) * LANES
            ]


def near_gradients(
    skip_ref, x_ref, b_ref, c_ref, df_ref, db_ref, dy_ref, ent_ref, gx_ref, gb_ref, gc_ref
):
    df, db = df_ref[...], db_ref[...]
    cf, be, end_f, end_b = columns(df, db)
    cf_row, be_row = rows(df, db)
    row, col = places()
    b, c, dy = b_ref[...], c_ref[...], dy_ref[...]
    scores = dot(c, b, 1, 1)
    pair_sum = jnp.zeros((FRAMES, FRAMES), F32)
    lane = lax.broadcasted_iota(jnp.int32, (1, LANES), 1)
    for g in range(HEADS // 2):
        at = slice(g * LANES, (g + 1) * LANES)
        acc = jnp.where(lane < HEAD_DIM, skip_ref[2 * g], skip_ref[2 * g + 1]) * dy[:, at]
        for hh in range(2):
            decay = pair_decay(2 * g + hh, cf, be, cf_row, be_row, row, col)
            dy_own = own_lanes(dy[:, at], hh)
            pair_sum = pair_sum + decay * dot_left(dy_own, x_ref[:, at], 1, 1)
            acc = acc + dot_both(scores * decay, dy_own, 0, 0)
        gx_ref[:, at] = acc
    entry_f, entry_b = take_slices(ent_ref)
    rise_f, rise_b = spread(jnp.exp(cf)), spread(jnp.exp(end_b - be))
    grad_c = dot_left(pair_sum, b, 1, 0)
    gc_ref[...] = grad_c + dot_both(dy * rise_f, entry_f, 1, 0) + dot_both(dy * rise_b, entry_b, 1, 0)
    gb_ref[...] = dot_left(pair_sum, c, 0, 0)


def gate_gradient(du_ref, y_ref, z_ref, gz_ref):
    z = z_ref[...].astype(F32)
    sig = jax.nn.sigmoid(z)
    gz_ref[...] = (du_ref[...] * y_ref[...] * sig * (1.0 + z * (1.0 - sig))).astype(BF16)


def finish(core_ref, x_ref, df_ref, db_ref, exit_ref, gb_near, gc_near, keep_ref, give_ref):
    cf, be, end_f, end_b = columns(df_ref[...], db_ref[...])
    x = x_ref[...].astype(F32)
    exit_f, exit_b = take_slices(exit_ref)
    grad_b = gb_near[...] + dot_both(x * spread(jnp.exp(end_f - cf)), exit_f, 1, 0)
    grad_b = grad_b + dot_both(x * spread(jnp.exp(be)), exit_b, 1, 0)
    half = FRAMES // 2
    first = core_ref[0] == 0
    for i, grad in enumerate((grad_b, gc_near[...])):
        at = slice(i * half, (i + 1) * half)
        keep_ref[at, :] = jnp.where(first, grad[:half, :], grad[half:, :])
        give_ref[at, :] = jnp.where(first, grad[half:, :], grad[:half, :])


def finish_x(b_ref, df_ref, db_ref, exit_ref, gx_near, gx_ref):
    cf, be, end_f, end_b = columns(df_ref[...], db_ref[...])
    b = b_ref[...]
    exit_f, exit_b = take_slices(exit_ref)
    gx = gx_near[...] + spread(jnp.exp(end_f - cf)) * dot_right(b, exit_f, 1, 1)
    gx_ref[...] = (gx + spread(jnp.exp(be)) * dot_right(b, exit_b, 1, 1)).astype(BF16)


def add_two(a_ref, b_ref, out_ref):
    out_ref[...] = a_ref[...] + b_ref[...]


def deal_out(core_ref, own_ref, other_ref, gb_ref, gc_ref):
    half = FRAMES // 2
    first = core_ref[0] == 0
    for i, ref in enumerate((gb_ref, gc_ref)):
        at = slice(i * half, (i + 1) * half)
        ref[0:half, :] = jnp.where(first, own_ref[at, :], other_ref[at, :])
        ref[half:, :] = jnp.where(first, other_ref[at, :], own_ref[at, :])


VMEM = pl.BlockSpec(memory_space=pltpu.VMEM)
SMEM = pl.BlockSpec(memory_space=pltpu.SMEM)
HBM = pl.BlockSpec(memory_space=pltpu.MemorySpace.HBM)


def call(kernel, name, out, *args, scalars=0, own=()):
    shapes = [jax.ShapeDtypeStruct(shape, dtype) for shape, dtype in out]
    single = len(shapes) == 1
    return pl.pallas_call(
        kernel,
        name=name,
        out_shape=shapes[0] if single else tuple(shapes),
        in_specs=[SMEM] * scalars + [HBM if own else VMEM] * (len(args) - scalars),
        out_specs=VMEM if single else tuple(VMEM for _ in shapes),
        scratch_shapes=list(own),
        compiler_params=pltpu.CompilerParams(vmem_limit_bytes=48 * 1024 * 1024),
    )(*args)


def exchange(a, axis):
    return lax.all_to_all(a, axis, 0, 0, tiled=True)


def swapped(a, mask, n_h):
    return lax.ppermute(a, "head", [(i, i ^ mask) for i in range(n_h)])


def body(x_in, gate_in, b_in, c_in, decay_fwd, decay_bwd, skip_gain, norm_gain, w_out, d_out):
    n_hi, n_lo, n_x, n_h = (lax.axis_size(axis) for axis in ("z_hi", "z_lo", "x", "head"))
    group = ("z_lo", "x")
    n = n_lo * n_x
    model = d_out.shape[1]
    gain = norm_gain.reshape(1, WIDTH)
    size = WIDTH // n
    weights = size * model // LANES
    place = lax.axis_index("z_hi").astype(jnp.int32).reshape(1)
    decays = (decay_fwd, decay_bwd)
    square = (FRAMES, WIDTH)

    firsts = tuple(pltpu.with_memory_space_constraint(a, pltpu.MemorySpace.HBM) for a in (x_in, b_in, *decays))
    own = [pltpu.VMEM(a.shape, a.dtype) for a in firsts] + [pltpu.SemaphoreType.DMA((4,))]
    sent = call(
        local_states, "local_states", [((n, 2 * size + 8, LANES), F32)], place, *firsts, scalars=1, own=own
    )
    rec1 = exchange(sent, group)
    near, m = call(
        near_outputs, "near_outputs", [(square, F32)] * 2,
        skip_gain, x_in, b_in, c_in, *decays, gain, w_out, d_out, scalars=1,
    )
    sent = call(totals_up, "totals_up", [((n_hi, size + 8, LANES), F32)], place, rec1, scalars=1)
    recz1 = exchange(sent, "z_hi")
    recz1, near, m = lax.optimization_barrier((recz1, near, m))
    sent = call(entries_up, "entries_up", [((n, 2 * size, LANES), F32)], place, recz1, rec1, scalars=1)
    entries = exchange(sent, group)

    y, sums = call(
        outputs, "outputs", [(square, F32), ((n_h, 8, LANES), F32)],
        near, m, gate_in, c_in, *decays, entries,
    )
    sums = exchange(sums, "head")
    dy, du, sent = call(
        functools.partial(gradients, inner=WIDTH * n_h), "gradients",
        [(square, F32), (square, F32), ((n, 2 * size + weights, LANES), F32)],
        sums, y, m, gate_in, c_in, *decays, gain, d_out,
    )

    rec2 = exchange(sent, group)
    gx_near, gb_near, gc_near = call(
        near_gradients, "near_gradients", [(square, F32)] + [((FRAMES, STATE), F32)] * 2,
        skip_gain, x_in, b_in, c_in, *decays, dy, entries, scalars=1,
    )
    grad_z = call(gate_gradient, "gate_gradient", [(square, BF16)], du, y, gate_in)
    part = weights // n_hi
    sent = call(totals_down, "totals_down", [((n_hi, size + part, LANES), F32)], place, rec1, rec2, scalars=1)
    recz2 = exchange(sent, "z_hi")
    recz2, gx_near, gb_near, gc_near, grad_z = lax.optimization_barrier(
        (recz2, gx_near, gb_near, gc_near, grad_z)
    )
    sent, weight = call(
        entries_down, "entries_down", [((n, 2 * size, LANES), F32), ((n_hi, part, LANES), F32)],
        place, recz1, recz2, rec1, rec2, scalars=1,
    )
    exits = exchange(sent, group)

    exits, weight = lax.optimization_barrier((exits, weight))
    weight = exchange(weight, "z_hi")

    core = (lax.axis_index("head") % 2).astype(jnp.int32).reshape(1)
    half = [((FRAMES, STATE), F32)]
    own, give = call(finish, "finish", half * 2, core, x_in, *decays, exits, gb_near, gc_near, scalars=1)
    own = call(add_two, "add_core", half, own, swapped(give, 1, n_h))
    own = call(add_two, "add_y", half, own, swapped(own, 2, n_h))
    grad_x = call(finish_x, "finish_x", [(square, BF16)], b_in, *decays, exits, gx_near)
    weight, own, grad_x = lax.optimization_barrier((weight, own, grad_x))

    weight = call(weight_copy, "weight_copy", [((n, weights, LANES), F32)], weight)
    weight = exchange(weight, group)
    grad_w = call(weight_rows, "weight_rows", [((WIDTH, model), F32)], weight)

    own = call(add_two, "add_y", half, own, swapped(own, 6, n_h))
    other = swapped(own, 1, n_h)
    grad_b, grad_c = call(deal_out, "deal_out", half * 2, core, own, other, scalars=1)
    return grad_x, grad_z, grad_b, grad_c, grad_w


def solution(mesh):
    n_seq, n_head = mesh.devices.shape
    n_z = n_seq // HEADS
    n_lo = min(2, n_z // 2)
    split = Mesh(mesh.devices.reshape(n_z // n_lo, n_lo, HEADS, n_head), ("z_hi", "z_lo", "x", "head"))
    seq = ("z_hi", "z_lo", "x")
    in_specs = (
        P(seq, "head"),
        P(seq, "head"),
        P(seq, None),
        P(seq, None),
        P("head", seq),
        P("head", seq),
        P("head"),
        P("head"),
        P("head", None),
        P(seq, None),
    )
    out_specs = (
        P(seq, "head"),
        P(seq, "head"),
        P(seq, None),
        P(seq, None),
        P("head", None),
    )
    return jax.shard_map(body, mesh=split, in_specs=in_specs, out_specs=out_specs, check_vma=False)
```

```python
import functools

import jax
import jax.numpy as jnp
from jax import lax
from jax.experimental import pallas as pl
from jax.experimental.pallas import tpu as pltpu
from jax.sharding import Mesh, PartitionSpec as P

HEADS = 4
HEAD_DIM = 64
STATE = 128
FRAMES = 256
WIDTH = HEADS * HEAD_DIM
LANES = 128
EPS_NORM = 1e-05
WEIGHT_SCALE = 0.0078125
F32, BF16 = jnp.float32, jnp.bfloat16


def dot(a, b, ca, cb):
    return lax.dot_general(a, b, (((ca,), (cb,)), ((), ())), preferred_element_type=F32)


def halves(a):
    high = a.astype(BF16)
    return high, (a - high.astype(F32)).astype(BF16)


def dot_left(a, b, ca, cb):
    ah, al = halves(a)
    return dot(ah, b, ca, cb) + dot(al, b, ca, cb)


def dot_right(a, b, ca, cb):
    bh, bl = halves(b)
    return dot(a, bh, ca, cb) + dot(a, bl, ca, cb)


def dot_both(a, b, ca, cb):
    ah, al = halves(a)
    bh, bl = halves(b)
    return dot(ah, bh, ca, cb) + (dot(ah, bl, ca, cb) + dot(al, bh, ca, cb))


def dot_exact(a, b, ca, cb):
    return lax.dot_general(
        a, b, (((ca,), (cb,)), ((), ())), precision=lax.Precision.HIGHEST, preferred_element_type=F32
    )


def places():
    row = lax.broadcasted_iota(jnp.int32, (FRAMES, FRAMES), 0)
    col = lax.broadcasted_iota(jnp.int32, (FRAMES, FRAMES), 1)
    return row, col


def columns(df, db):
    row, col = places()
    upto = (col <= row).astype(F32)
    before = (col < row).astype(F32)
    cf = dot_exact(upto, df, 1, 1)
    be = dot_exact(before, db, 1, 1)
    end_f = cf[FRAMES - 1 :, :]
    end_b = dot_exact(jnp.ones((8, FRAMES), F32), db, 1, 1)[:1, :]
    return cf, be, end_f, end_b


def rows(df, db):
    row, col = places()
    upto = (row <= col).astype(F32)
    before = (row < col).astype(F32)
    return dot_exact(df, upto, 1, 0), dot_exact(db, before, 1, 0)


def spread(cols):
    lane = lax.broadcasted_iota(jnp.int32, (cols.shape[0], LANES), 1)
    pairs = [
        jnp.where(lane < HEAD_DIM, cols[:, 2 * g : 2 * g + 1], cols[:, 2 * g + 1 : 2 * g + 2])
        for g in range(HEADS // 2)
    ]
    return jnp.concatenate(pairs, axis=1)


def pair_decay(h, cf, be, cf_row, be_row, row, col):
    gap = jnp.where(
        row > col,
        cf[:, h : h + 1] - cf_row[h : h + 1, :],
        be_row[h : h + 1, :] - be[:, h : h + 1],
    )
    return jnp.where(row == col, 2.0, jnp.exp(jnp.minimum(gap, 0.0)))


def own_lanes(pair, hh):
    lane = lax.broadcasted_iota(jnp.int32, pair.shape, 1)
    mine = lane < HEAD_DIM if hh == 0 else lane >= HEAD_DIM
    return jnp.where(mine, pair, jnp.zeros_like(pair))


def put_slices(out_ref, forward, backward):
    n = out_ref.shape[0]
    size = WIDTH // n
    for i in range(n):
        at = slice(i * size, (i + 1) * size)
        out_ref[i, 0:size, :] = forward[at, :]
        out_ref[i, size : 2 * size, :] = backward[at, :]


def take_slices(ref):
    n = ref.shape[0]
    size = WIDTH // n
    forward = jnp.concatenate([ref[i, 0:size, :] for i in range(n)], axis=0)
    backward = jnp.concatenate([ref[i, size : 2 * size, :] for i in range(n)], axis=0)
    return forward, backward


def local_states(_, x_hbm, b_hbm, df_hbm, db_hbm, out_ref, x_ref, b_ref, df_ref, db_ref, sems):
    sources, targets = (x_hbm, b_hbm, df_hbm, db_hbm), (x_ref, b_ref, df_ref, db_ref)
    copies = [pltpu.make_async_copy(s, t, sems.at[i]) for i, (s, t) in enumerate(zip(sources, targets))]
    for copy in copies[::-1]:
        copy.start()
    copies[2].wait()
    copies[3].wait()
    cf, be, end_f, end_b = columns(df_ref[...], db_ref[...])
    copies[0].wait()
    copies[1].wait()
    x = x_ref[...].astype(F32)
    b = b_ref[...]
    state_f = dot_left(x * spread(jnp.exp(end_f - cf)), b, 0, 0)
    state_b = dot_left(x * spread(jnp.exp(be)), b, 0, 0)
    put_slices(out_ref, state_f, state_b)
    n = out_ref.shape[0]
    size = WIDTH // n
    total_f, total_b = jnp.exp(end_f), jnp.exp(end_b)
    half = lax.broadcasted_iota(jnp.int32, (8, LANES), 0) < 4
    for j in range(HEADS):
        both = jnp.where(half, total_f[:, j : j + 1], total_b[:, j : j + 1])
        for i in range(j * n // HEADS, (j + 1) * n // HEADS):
            out_ref[i, 2 * size :, :] = both


def totals_at(ref, i, start):
    return ref[i, start : start + 1, :], ref[i, start + 4 : start + 5, :]


def sliced(ref, i, size):
    return ref[i, 0:size, :], ref[i, size : 2 * size, :]


def group_sums(dec_ref, rec_ref, forward_up):
    n = rec_ref.shape[0]
    size = WIDTH // n
    decays = [totals_at(dec_ref, i, 2 * size) for i in range(n)]
    parts = [sliced(rec_ref, i, size) for i in range(n)]
    sums = []
    for branch, up in enumerate((forward_up, not forward_up)):
        order = list(range(n)) if up else list(range(n))[::-1]
        acc = parts[order[0]][branch]
        for i in order[1:]:
            acc = decays[i][branch] * acc + parts[i][branch]
        sums.append(acc)
    return sums, decays


def totals_up(place_ref, rec_ref, out_ref):
    size = WIDTH // rec_ref.shape[0]
    (sum_f, sum_b), decays = group_sums(rec_ref, rec_ref, True)
    all_f, all_b = decays[0]
    for dec_f, dec_b in decays[1:]:
        all_f, all_b = all_f * dec_f, all_b * dec_b
    half = lax.broadcasted_iota(jnp.int32, (8, LANES), 0) < 4
    for k in range(out_ref.shape[0]):
        out_ref[k, 0:size, :] = jnp.where(place_ref[0] < k, sum_f, sum_b)
        out_ref[k, size:, :] = jnp.where(half, all_f, all_b)


def entries_up(place_ref, zrec_ref, rec_ref, out_ref):
    n_g, n = zrec_ref.shape[0], rec_ref.shape[0]
    size = WIDTH // n
    place = place_ref[0]
    for branch, up in enumerate((True, False)):
        entry = jnp.zeros((size, LANES), F32)
        for k in list(range(n_g)) if up else list(range(n_g))[::-1]:
            passed = place > k if up else place < k
            after = totals_at(zrec_ref, k, size)[branch] * entry + zrec_ref[k, 0:size, :]
            entry = jnp.where(passed, after, entry)
        put_entries(out_ref, branch, up, entry, rec_ref, rec_ref)


def put_entries(out_ref, branch, up, entry, dec_ref, rec_ref):
    n = rec_ref.shape[0]
    size = WIDTH // n
    for i in list(range(n)) if up else list(range(n))[::-1]:
        out_ref[i, branch * size : (branch + 1) * size, :] = entry
        entry = totals_at(dec_ref, i, 2 * size)[branch] * entry + sliced(rec_ref, i, size)[branch]


def totals_down(place_ref, dec_ref, rec_ref, out_ref):
    n, n_g = rec_ref.shape[0], out_ref.shape[0]
    size = WIDTH // n
    (sum_f, sum_b), _ = group_sums(dec_ref, rec_ref, False)
    weight = rec_ref[0, 2 * size :, :]
    for i in range(1, n):
        weight = weight + rec_ref[i, 2 * size :, :]
    part = weight.shape[0] // n_g
    for k in range(n_g):
        out_ref[k, 0:size, :] = jnp.where(place_ref[0] > k, sum_f, sum_b)
        out_ref[k, size:, :] = weight[k * part : (k + 1) * part, :]


def entries_down(place_ref, zdec_ref, zrec_ref, dec_ref, rec_ref, out_ref, w_ref):
    n_g, n = zrec_ref.shape[0], rec_ref.shape[0]
    size = WIDTH // n
    place = place_ref[0]
    for branch, up in enumerate((False, True)):
        entry = jnp.zeros((size, LANES), F32)
        for k in list(range(n_g)) if up else list(range(n_g))[::-1]:
            passed = place > k if up else place < k
            after = totals_at(zdec_ref, k, size)[branch] * entry + zrec_ref[k, 0:size, :]
            entry = jnp.where(passed, after, entry)
        put_entries(out_ref, branch, up, entry, dec_ref, rec_ref)
    weight = zrec_ref[0, size:, :]
    for k in range(1, n_g):
        weight = weight + zrec_ref[k, size:, :]
    for k in range(n_g):
        w_ref[k, :, :] = weight


def weight_copy(rec_ref, out_ref):
    n_g, size = rec_ref.shape[0], rec_ref.shape[1]
    for k in range(n_g):
        rows = rec_ref[k, :, :] * WEIGHT_SCALE
        for i in range(out_ref.shape[0] // size):
            out_ref[i * size : (i + 1) * size, k * LANES : (k + 1) * LANES] = rows


def across_rows(cols):
    lane = lax.broadcasted_iota(jnp.int32, (LANES, LANES), 1)
    grid = jnp.zeros((LANES, LANES), F32)
    for i, col in enumerate(cols):
        for part in range(FRAMES // LANES):
            at = i * (FRAMES // LANES) + part
            grid = jnp.where(lane == at, col[part * LANES : (part + 1) * LANES, :], grid)
    return jnp.transpose(grid)[0:8, :]


def near_outputs(
    skip_ref, x_ref, b_ref, c_ref, df_ref, db_ref, gain_ref, w_ref, do_ref, y_ref, m_ref
):
    df, db = df_ref[...], db_ref[...]
    cf, be, end_f, end_b = columns(df, db)
    cf_row, be_row = rows(df, db)
    row, col = places()
    scores = dot(c_ref[...], b_ref[...], 1, 1)
    lane = lax.broadcasted_iota(jnp.int32, (1, LANES), 1)
    for g in range(HEADS // 2):
        at = slice(g * LANES, (g + 1) * LANES)
        pair = x_ref[:, at]
        acc = jnp.where(lane < HEAD_DIM, skip_ref[2 * g], skip_ref[2 * g + 1]) * pair.astype(F32)
        for hh in range(2):
            weights = scores * pair_decay(2 * g + hh, cf, be, cf_row, be_row, row, col)
            acc = acc + dot_left(weights, own_lanes(pair, hh), 1, 0)
        y_ref[:, at] = acc
    m_ref[...] = dot(do_ref[...], w_ref[...], 1, 1) * gain_ref[...]


def outputs(near_ref, m_ref, z_ref, c_ref, df_ref, db_ref, ent_ref, y_ref, sums_ref):
    cf, be, end_f, end_b = columns(df_ref[...], db_ref[...])
    c = c_ref[...]
    entry_f, entry_b = take_slices(ent_ref)
    y = near_ref[...] + spread(jnp.exp(cf)) * dot_right(c, entry_f, 1, 1)
    y = y + spread(jnp.exp(end_b - be)) * dot_right(c, entry_b, 1, 1)
    y_ref[...] = y
    z, m = z_ref[...].astype(F32), m_ref[...]
    u = y * z * jax.nn.sigmoid(z)
    sums = across_rows([jnp.sum(u * u, axis=1, keepdims=True), jnp.sum(u * m, axis=1, keepdims=True)])
    for i in range(sums_ref.shape[0]):
        sums_ref[i, :, :] = sums


def gradients(
    sums_ref, y_ref, m_ref, z_ref, c_ref, df_ref, db_ref, gain_ref, do_ref,
    dy_ref, du_ref, out_ref, *, inner,
):
    total = sums_ref[0, :, :]
    for i in range(1, sums_ref.shape[0]):
        total = total + sums_ref[i, :, :]
    grid = jnp.transpose(jnp.concatenate([total, jnp.zeros((LANES - 8, LANES), F32)], axis=0))
    square = jnp.concatenate([grid[:, 0:1], grid[:, 1:2]], axis=0) / inner
    cross = jnp.concatenate([grid[:, 2:3], grid[:, 3:4]], axis=0) / inner
    q = lax.rsqrt(square + EPS_NORM)
    y, m, z = y_ref[...], m_ref[...], z_ref[...].astype(F32)
    sig = jax.nn.sigmoid(z)
    silu = z * sig
    u = y * z * sig
    normed = (u * q * gain_ref[...]).astype(BF16)
    du = q * m - u * (q * q * q * cross)
    dy = du * silu
    dy_ref[...] = dy
    du_ref[...] = du
    cf, be, end_f, end_b = columns(df_ref[...], db_ref[...])
    c = c_ref[...]
    back_f = dot_left(dy * spread(jnp.exp(cf)), c, 0, 0)
    back_b = dot_left(dy * spread(jnp.exp(end_b - be)), c, 0, 0)
    put_slices(out_ref, back_f, back_b)
    weight = dot(normed, do_ref[...], 0, 0)
    n = out_ref.shape[0]
    size = WIDTH // n
    for i in range(n):
        for block in range(weight.shape[1] // LANES):
            at = 2 * size + block * size
            out_ref[i, at : at + size, :] = weight[
                i * size : (i + 1) * size, block * LANES : (block + 1) * LANES
            ]


def near_gradients(
    skip_ref, x_ref, b_ref, c_ref, df_ref, db_ref, dy_ref, ent_ref, gx_ref, gb_ref, gc_ref
):
    df, db = df_ref[...], db_ref[...]
    cf, be, end_f, end_b = columns(df, db)
    cf_row, be_row = rows(df, db)
    row, col = places()
    b, c, dy = b_ref[...], c_ref[...], dy_ref[...]
    scores = dot(c, b, 1, 1)
    pair_sum = jnp.zeros((FRAMES, FRAMES), F32)
    lane = lax.broadcasted_iota(jnp.int32, (1, LANES), 1)
    for g in range(HEADS // 2):
        at = slice(g * LANES, (g + 1) * LANES)
        acc = jnp.where(lane < HEAD_DIM, skip_ref[2 * g], skip_ref[2 * g + 1]) * dy[:, at]
        for hh in range(2):
            decay = pair_decay(2 * g + hh, cf, be, cf_row, be_row, row, col)
            dy_own = own_lanes(dy[:, at], hh)
            pair_sum = pair_sum + decay * dot_left(dy_own, x_ref[:, at], 1, 1)
            acc = acc + dot_both(scores * decay, dy_own, 0, 0)
        gx_ref[:, at] = acc
    entry_f, entry_b = take_slices(ent_ref)
    rise_f, rise_b = spread(jnp.exp(cf)), spread(jnp.exp(end_b - be))
    grad_c = dot_left(pair_sum, b, 1, 0)
    gc_ref[...] = grad_c + dot_both(dy * rise_f, entry_f, 1, 0) + dot_both(dy * rise_b, entry_b, 1, 0)
    gb_ref[...] = dot_left(pair_sum, c, 0, 0)


def gate_gradient(du_ref, y_ref, z_ref, gz_ref):
    z = z_ref[...].astype(F32)
    sig = jax.nn.sigmoid(z)
    gz_ref[...] = (du_ref[...] * y_ref[...] * sig * (1.0 + z * (1.0 - sig))).astype(BF16)


def finish(core_ref, x_ref, df_ref, db_ref, exit_ref, gb_near, gc_near, keep_ref, give_ref):
    cf, be, end_f, end_b = columns(df_ref[...], db_ref[...])
    x = x_ref[...].astype(F32)
    exit_f, exit_b = take_slices(exit_ref)
    grad_b = gb_near[...] + dot_both(x * spread(jnp.exp(end_f - cf)), exit_f, 1, 0)
    grad_b = grad_b + dot_both(x * spread(jnp.exp(be)), exit_b, 1, 0)
    half = FRAMES // 2
    first = core_ref[0] == 0
    for i, grad in enumerate((grad_b, gc_near[...])):
        at = slice(i * half, (i + 1) * half)
        keep_ref[at, :] = jnp.where(first, grad[:half, :], grad[half:, :])
        give_ref[at, :] = jnp.where(first, grad[half:, :], grad[:half, :])


def finish_x(b_ref, df_ref, db_ref, exit_ref, gx_near, gx_ref):
    cf, be, end_f, end_b = columns(df_ref[...], db_ref[...])
    b = b_ref[...]
    exit_f, exit_b = take_slices(exit_ref)
    gx = gx_near[...] + spread(jnp.exp(end_f - cf)) * dot_right(b, exit_f, 1, 1)
    gx_ref[...] = (gx + spread(jnp.exp(be)) * dot_right(b, exit_b, 1, 1)).astype(BF16)


def add_two(a_ref, b_ref, out_ref):
    out_ref[...] = a_ref[...] + b_ref[...]


def deal_out(core_ref, own_ref, other_ref, gb_ref, gc_ref):
    half = FRAMES // 2
    first = core_ref[0] == 0
    for i, ref in enumerate((gb_ref, gc_ref)):
        at = slice(i * half, (i + 1) * half)
        ref[0:half, :] = jnp.where(first, own_ref[at, :], other_ref[at, :])
        ref[half:, :] = jnp.where(first, other_ref[at, :], own_ref[at, :])


VMEM = pl.BlockSpec(memory_space=pltpu.VMEM)
SMEM = pl.BlockSpec(memory_space=pltpu.SMEM)
HBM = pl.BlockSpec(memory_space=pltpu.MemorySpace.HBM)


def call(kernel, name, out, *args, scalars=0, own=()):
    shapes = [jax.ShapeDtypeStruct(shape, dtype) for shape, dtype in out]
    single = len(shapes) == 1
    return pl.pallas_call(
        kernel,
        name=name,
        out_shape=shapes[0] if single else tuple(shapes),
        in_specs=[SMEM] * scalars + [HBM if own else VMEM] * (len(args) - scalars),
        out_specs=VMEM if single else tuple(VMEM for _ in shapes),
        scratch_shapes=list(own),
        compiler_params=pltpu.CompilerParams(vmem_limit_bytes=48 * 1024 * 1024),
    )(*args)


def exchange(a, axis):
    return lax.all_to_all(a, axis, 0, 0, tiled=True)


def swapped(a, mask, n_h):
    return lax.ppermute(a, "head", [(i, i ^ mask) for i in range(n_h)])


def body(x_in, gate_in, b_in, c_in, decay_fwd, decay_bwd, skip_gain, norm_gain, w_out, d_out):
    n_hi, n_lo, n_x, n_h = (lax.axis_size(axis) for axis in ("z_hi", "z_lo", "x", "head"))
    group = ("z_lo", "x")
    n = n_lo * n_x
    model = d_out.shape[1]
    gain = norm_gain.reshape(1, WIDTH)
    size = WIDTH // n
    weights = size * model // LANES
    place = lax.axis_index("z_hi").astype(jnp.int32).reshape(1)
    decays = (decay_fwd, decay_bwd)
    square = (FRAMES, WIDTH)

    firsts = tuple(pltpu.with_memory_space_constraint(a, pltpu.MemorySpace.HBM) for a in (x_in, b_in, *decays))
    own = [pltpu.VMEM(a.shape, a.dtype) for a in firsts] + [pltpu.SemaphoreType.DMA((4,))]
    sent = call(
        local_states, "local_states", [((n, 2 * size + 8, LANES), F32)], place, *firsts, scalars=1, own=own
    )
    rec1 = exchange(sent, group)
    near, m = call(
        near_outputs, "near_outputs", [(square, F32)] * 2,
        skip_gain, x_in, b_in, c_in, *decays, gain, w_out, d_out, scalars=1,
    )
    sent = call(totals_up, "totals_up", [((n_hi, size + 8, LANES), F32)], place, rec1, scalars=1)
    recz1 = exchange(sent, "z_hi")
    recz1, near, m = lax.optimization_barrier((recz1, near, m))
    sent = call(entries_up, "entries_up", [((n, 2 * size, LANES), F32)], place, recz1, rec1, scalars=1)
    entries = exchange(sent, group)

    y, sums = call(
        outputs, "outputs", [(square, F32), ((n_h, 8, LANES), F32)],
        near, m, gate_in, c_in, *decays, entries,
    )
    sums = exchange(sums, "head")
    dy, du, sent = call(
        functools.partial(gradients, inner=WIDTH * n_h), "gradients",
        [(square, F32), (square, F32), ((n, 2 * size + weights, LANES), F32)],
        sums, y, m, gate_in, c_in, *decays, gain, d_out,
    )

    rec2 = exchange(sent, group)
    gx_near, gb_near, gc_near = call(
        near_gradients, "near_gradients", [(square, F32)] + [((FRAMES, STATE), F32)] * 2,
        skip_gain, x_in, b_in, c_in, *decays, dy, entries, scalars=1,
    )
    grad_z = call(gate_gradient, "gate_gradient", [(square, BF16)], du, y, gate_in)
    part = weights // n_hi
    sent = call(totals_down, "totals_down", [((n_hi, size + part, LANES), F32)], place, rec1, rec2, scalars=1)
    recz2 = exchange(sent, "z_hi")
    recz2, gx_near, gb_near, gc_near, grad_z = lax.optimization_barrier(
        (recz2, gx_near, gb_near, gc_near, grad_z)
    )
    sent, weight = call(
        entries_down, "entries_down", [((n, 2 * size, LANES), F32), ((n_hi, part, LANES), F32)],
        place, recz1, recz2, rec1, rec2, scalars=1,
    )
    exits = exchange(sent, group)

    exits, weight = lax.optimization_barrier((exits, weight))
    weight = exchange(weight, "z_hi")

    core = (lax.axis_index("head") % 2).astype(jnp.int32).reshape(1)
    half = [((FRAMES, STATE), F32)]
    own, give = call(finish, "finish", half * 2, core, x_in, *decays, exits, gb_near, gc_near, scalars=1)
    own = call(add_two, "add_core", half, own, swapped(give, 1, n_h))
    own = call(add_two, "add_y", half, own, swapped(own, 2, n_h))
    grad_x = call(finish_x, "finish_x", [(square, BF16)], b_in, *decays, exits, gx_near)
    weight, own, grad_x = lax.optimization_barrier((weight, own, grad_x))

    weight = weight.reshape(model // LANES, size, LANES)
    grad_w = exchange(call(weight_copy, "weight_copy", [((WIDTH, model), F32)], weight), group)

    own = call(add_two, "add_y", half, own, swapped(own, 6, n_h))
    other = swapped(own, 1, n_h)
    grad_b, grad_c = call(deal_out, "deal_out", half * 2, core, own, other, scalars=1)
    return grad_x, grad_z, grad_b, grad_c, grad_w


def solution(mesh):
    n_seq, n_head = mesh.devices.shape
    n_z = n_seq // HEADS
    n_lo = min(2, n_z // 2)
    split = Mesh(mesh.devices.reshape(n_z // n_lo, n_lo, HEADS, n_head), ("z_hi", "z_lo", "x", "head"))
    seq = ("z_hi", "z_lo", "x")
    in_specs = (
        P(seq, "head"),
        P(seq, "head"),
        P(seq, None),
        P(seq, None),
        P("head", seq),
        P("head", seq),
        P("head"),
        P("head"),
        P("head", None),
        P(seq, None),
    )
    out_specs = (
        P(seq, "head"),
        P(seq, "head"),
        P(seq, None),
        P(seq, None),
        P("head", None),
    )
    return jax.shard_map(body, mesh=split, in_specs=in_specs, out_specs=out_specs, check_vma=False)
```
